32 devices in a mesh: dp: 8 (over y, x, core), tensor: 4 (over z).
Axes of the slice: x: 2, y: 2, z: 4, core: 2. Of those that a mesh axis runs over, the one named last changes fastest.
Arguments:
- hidden: bfloat16 [64, 512, 768], P(('dp', 'tensor')), may hold values from -6 to 6
- cotangent: bfloat16 [64, 256, 768], P(('dp', 'tensor')), may hold values from -6 to 6
- segments: int32 [64, 512], P('dp'), may hold values from 0 to 7, as said below
- pooled_segments: int32 [64, 256], P('dp'), may hold values from 0 to 7, as said below
- positions: int32 [64, 512], P('dp'), may hold values from 0 to 511, as said below
- query_projection_weight: bfloat16 [768, 768], P(None, 'tensor'), may hold values from -0.21875 to 0.21875
- query_bias: bfloat16 [768], P('tensor'), may hold values from -3 to 3
- key_weight: bfloat16 [768, 768], P(None, 'tensor'), may hold values from -0.21875 to 0.21875
- value_weight: bfloat16 [768, 768], P(None, 'tensor'), may hold values from -0.21875 to 0.21875
- value_bias: bfloat16 [768], P('tensor'), may hold values from -3 to 3
- output_projection_weight: bfloat16 [768, 768], P('tensor'), may hold values from -1.75 to 1.75
- out_bias: bfloat16 [768], replicated, may hold values from -3 to 3
- relative_bias: float32 [12, 1024], P('tensor'), may hold values from -6 to 6
- first_gain: bfloat16 [768], replicated, may hold values from 0.5 to 1.5
- first_shift: bfloat16 [768], replicated, may hold values from -1.75 to 1.75
- up_projection_weight: bfloat16 [768, 3072], P(None, 'tensor'), may hold values from -0.21875 to 0.21875
- up_projection_bias: bfloat16 [3072], P('tensor'), may hold values from -3 to 3
- down_projection_weight: bfloat16 [3072, 768], P('tensor'), may hold values from -0.109375 to 0.109375
- down_bias: bfloat16 [768], replicated, may hold values from -3 to 3
- second_gain: bfloat16 [768], replicated, may hold values from 0.5 to 1.5
- second_shift: bfloat16 [768], replicated, may hold values from -1.75 to 1.75
Outputs:
- output: bfloat16 [64, 256, 768], P(('dp', 'tensor'))
- hidden_gradient: bfloat16 [64, 512, 768], P(('dp', 'tensor'))
- query_weight_gradient: float32 [768, 768], P(None, 'tensor')
- query_bias_gradient: float32 [768], P('tensor')
- key_weight_gradient: float32 [768, 768], P(None, 'tensor')
- value_weight_gradient: float32 [768, 768], P(None, 'tensor')
- value_bias_gradient: float32 [768], P('tensor')
- out_weight_gradient: float32 [768, 768], P('tensor')
- out_bias_gradient: float32 [768], replicated
- relative_bias_gradient: float32 [12, 1024], P('tensor')
- first_gain_gradient: float32 [768], replicated
- first_shift_gradient: float32 [768], replicated
- up_projection_weight_gradient: float32 [768, 3072], P(None, 'tensor')
- up_bias_gradient: float32 [3072], P('tensor')
- down_weight_gradient: float32 [3072, 768], P('tensor')
- down_bias_gradient: float32 [768], replicated
- second_gain_gradient: float32 [768], replicated
- second_shift_gradient: float32 [768], replicated
The draws below stay inside these ranges and needn't reach their ends.
Inputs may be any that keep to these rules, and one draw needn't show every extreme that they name: segments do not fall along a row and start at 0 in each row; equal ids mark one document; a row holds at most 8 documents. pooled_segments[b, q] = segments[b, 2q]. `positions`: 0 at the first token of each document, rising by one within it.
All inputs are finite; a program needn't handle non-finite values.
Results may differ from the reference program's by a relative error of at most 0.024.
Values may be sent and summed in bfloat16 or wider, within the bound.
No kernel may reach another device: no remote copies, remote signals or barrier semaphores. Data moves between devices by JAX's collectives and lax.ppermute only.
A program may use at most 192 MiB of HBM per device.

```python
import jax
import jax.numpy as jnp
from jax import lax

D = 768
H = 12
HEAD = 64
FF = 3072
SEQ = 512
BATCH = 64
POOLED = 256
NREL = 1024


def document_layout(key):
    boundary_key = jax.random.fold_in(key, 11)
    boundary = jax.random.randint(boundary_key, (BATCH, SEQ), 0, max(SEQ // 8, 2)) == 0
    index = jnp.arange(SEQ, dtype=jnp.int32)
    row = jnp.arange(BATCH, dtype=jnp.int32)[:, None]
    even_split = (index % (SEQ // 8) == 0)[None, :]
    boundary = jnp.where(row == 0, even_split, boundary)
    boundary = jnp.where(row == 1, False, boundary)
    boundary = boundary | (index == 0)[None, :]
    counted = jnp.cumsum(boundary.astype(jnp.int32), axis=1)
    boundary = boundary & (counted <= 8)
    segment_ids = jnp.cumsum(boundary.astype(jnp.int32), axis=1) - 1
    starts = lax.cummax(jnp.where(boundary, index[None, :], 0), axis=1)
    return (segment_ids.astype(jnp.int32), (index[None, :] - starts).astype(jnp.int32))


def draw_segments(key, part):
    return document_layout(key)[0]


def draw_pooled_segments(key, part):
    return document_layout(key)[0][:, 0::2]


def draw_positions(key, part):
    return document_layout(key)[1]


def steps_of(rng, shape, cuts, least, largest):
    factor_of = 1.0
    for axis_at, parts in cuts:
        heights = jax.random.uniform(jax.random.fold_in(jax.random.fold_in(rng, 6), axis_at), (parts,), jnp.float32, least / len(cuts), largest / len(cuts))
        factor_of = factor_of * jnp.repeat(jnp.exp(heights), shape[axis_at] // parts).reshape((-1,) + (1,) * (len(shape) - 1 - axis_at))
    return factor_of


def scatter_about(stream_key, extent, spread, most, pieces=(), kind=jnp.bfloat16):
    values = spread * jax.random.normal(stream_key, extent, jnp.float32)
    if pieces:
        values = values * steps_of(stream_key, extent, pieces, -0.22, 0.18)
    return jnp.clip(values, -most, most).astype(kind)


def setup_inputs(seed: int = 0) -> dict:
    key_of = jax.random.split(jax.random.key(seed), 22)
    return {
        "hidden": scatter_about(key_of[0], (BATCH, SEQ, D), 1.0, 6.0, ((0, 32),)),
        "cotangent": scatter_about(key_of[1], (BATCH, POOLED, D), 1.0, 6.0, ((0, 32),)),
        "segments": draw_segments(jax.random.fold_in(key_of[21], 71), 0),
        "pooled_segments": draw_pooled_segments(jax.random.fold_in(key_of[21], 71), 0),
        "positions": draw_positions(jax.random.fold_in(key_of[21], 71), 0),
        "query_projection_weight": scatter_about(key_of[5], (D, D), D ** -0.5, 0.21875, ((1, 4),)),
        "query_bias": scatter_about(key_of[6], (D,), 0.5, 3.0, ((0, 4),)),
        "key_weight": scatter_about(key_of[7], (D, D), D ** -0.5, 0.21875, ((1, 4),)),
        "value_weight": scatter_about(key_of[8], (D, D), D ** -0.5, 0.21875, ((1, 4),)),
        "value_bias": scatter_about(key_of[9], (D,), 0.5, 3.0, ((0, 4),)),
        "output_projection_weight": scatter_about(key_of[10], (D, D), (max(D // 64, 1)) ** -0.5, 1.75, ((0, 4),)),
        "out_bias": scatter_about(key_of[11], (D,), 0.5, 3.0),
        "relative_bias": scatter_about(key_of[12], (H, NREL), 1.0, 6.0, ((0, 4),), jnp.float32),
        "first_gain": jnp.clip(1.0 + 0.1 * jax.random.normal(key_of[13], (D,), jnp.float32), 0.5, 1.5).astype(jnp.bfloat16),
        "first_shift": scatter_about(key_of[14], (D,), 0.3, 1.75),
        "up_projection_weight": scatter_about(key_of[15], (D, FF), D ** -0.5, 0.21875, ((1, 4),)),
        "up_projection_bias": scatter_about(key_of[16], (FF,), 0.5, 3.0, ((0, 4),)),
        "down_projection_weight": scatter_about(key_of[17], (FF, D), FF ** -0.5, 0.109375, ((0, 4),)),
        "down_bias": scatter_about(key_of[18], (D,), 0.5, 3.0),
        "second_gain": jnp.clip(1.0 + 0.1 * jax.random.normal(key_of[19], (D,), jnp.float32), 0.5, 1.5).astype(jnp.bfloat16),
        "second_shift": scatter_about(key_of[20], (D,), 0.3, 1.75),
    }


@jax.custom_vjp
def low(v):
    return lax.optimization_barrier(v.astype(jnp.bfloat16)).astype(jnp.float32)

@jax.custom_vjp
def low_back(v):
    return v

def low_keep(v):
    return (low(v), None)

def low_pass(kept, grad):
    return (grad,)

def back_keep(v):
    return (v, None)

def back_low(kept, grad):
    return (low(grad),)
low.defvjp(low_keep, low_pass)
low_back.defvjp(back_keep, back_low)
PRECISE = lax.Precision.HIGHEST
EPSILON = 1e-05

def layer_norm(residual, gain, shift):
    center = residual - lax.optimization_barrier(jnp.mean(residual, axis=-1, keepdims=True))
    variance = lax.optimization_barrier(jnp.mean(center * center, axis=-1, keepdims=True))
    return center * lax.rsqrt(variance + EPSILON) * gain + shift

def project(activ, weight):
    return jnp.einsum('rsd,de->rse', activ, weight, precision=PRECISE)

def forward(hidden_rows, params, segments, pooled_segments, positions):
    query_projection_weight, query_bias, key_weight, value_weight, value_bias, output_projection_weight, out_bias, relative_bias, first_gain, first_shift, up_projection_weight, up_projection_bias, down_projection_weight, down_bias, second_gain, second_shift = params
    group_rows = hidden_rows.shape[0]
    pooled = 0.5 * (hidden_rows[:, 0::2] + hidden_rows[:, 1::2])
    pooled_low = low(pooled)
    queries = low_back(low(project(pooled_low, query_projection_weight) + query_bias)).reshape(group_rows, SEQ // 2, H, HEAD)
    key_heads = low_back(low(project(hidden_rows, key_weight))).reshape(group_rows, SEQ, H, HEAD)
    value_heads = low_back(low(project(hidden_rows, value_weight) + value_bias)).reshape(group_rows, SEQ, H, HEAD)
    relative = (positions[:, None, :] - positions[:, 0::2][:, :, None] + SEQ).astype(jnp.int32)
    looked = jnp.moveaxis(jnp.take(relative_bias, relative, axis=1), 0, 1)
    allowed = (pooled_segments[:, :, None] == segments[:, None, :])[:, None]
    raw_scores = jnp.einsum('rqhe,rkhe->rhqk', queries, key_heads, precision=PRECISE) * HEAD ** (-0.5) + looked
    scores = low_back(jnp.where(allowed, raw_scores, -1000000000.0))
    probability = low(jax.nn.softmax(scores, axis=-1))
    context_rows = low_back(low(jnp.einsum('rhqk,rkhe->rqhe', probability, value_heads, precision=PRECISE)))
    context_rows = context_rows.reshape(group_rows, SEQ // 2, D)
    attended_rows = low_back(project(context_rows, output_projection_weight)) + out_bias
    first_out = layer_norm(pooled + attended_rows, first_gain, first_shift)
    preactivation = low_back(project(low(first_out), up_projection_weight) + up_projection_bias)
    hidden_activation = low(jax.nn.gelu(preactivation, approximate=False))
    ffn_out = low_back(project(hidden_activation, down_projection_weight)) + down_bias
    return layer_norm(first_out + ffn_out, second_gain, second_shift)

def reference(hidden, cotangent, segments, pooled_segments, positions, query_projection_weight, query_bias, key_weight, value_weight, value_bias, output_projection_weight, out_bias, relative_bias, first_gain, first_shift, up_projection_weight, up_projection_bias, down_projection_weight, down_bias, second_gain, second_shift):
    params = tuple((p.astype(jnp.float32) for p in (query_projection_weight, query_bias, key_weight, value_weight, value_bias, output_projection_weight, out_bias, relative_bias, first_gain, first_shift, up_projection_weight, up_projection_bias, down_projection_weight, down_bias, second_gain, second_shift)))
    group_size = 8
    groups = BATCH // group_size

    def split(whole_array):
        return whole_array.reshape((groups, group_size) + whole_array.shape[1:])

    def one_group(carry, item):
        rows_in, rows_cot, seg_rows, pooled_rows, position_rows = item

        def run_group(hidden_rows, *weights):
            return forward(hidden_rows, weights, seg_rows, pooled_rows, position_rows)
        result, pullback = jax.vjp(run_group, rows_in.astype(jnp.float32), *params)
        grads = pullback(rows_cot.astype(jnp.float32))
        carry = tuple((a + g for a, g in zip(carry, grads[1:])))
        return (carry, (result.astype(jnp.bfloat16), grads[0].astype(jnp.bfloat16)))
    start = tuple((jnp.zeros_like(p) for p in params))
    totals, (results, input_grads) = lax.scan(one_group, start, (split(hidden), split(cotangent), split(segments), split(pooled_segments), split(positions)))
    return (results.reshape(BATCH, SEQ // 2, D), input_grads.reshape(BATCH, SEQ, D), totals[0], totals[1], totals[2], totals[3], totals[4], totals[5], totals[6], totals[7], totals[8], totals[9], totals[10], totals[11], totals[12], totals[13], totals[14], totals[15])
```

```python
from functools import partial

import jax
import jax.numpy as jnp
from jax import lax
from jax.experimental import pallas as pl
from jax.experimental.pallas import tpu as pltpu
from jax.sharding import PartitionSpec as P

EPSILON = 1e-05
MASKED_SCORE = -1000000000.0
GROUP = 8
F32 = jnp.float32
B16 = jnp.bfloat16
VMEM_LIMIT = 60 * 1024 * 1024


def nn(a, b):
    return lax.dot_general(a, b, (((1,), (0,)), ((), ())), preferred_element_type=F32)


def nt(a, b):
    return lax.dot_general(a, b, (((1,), (1,)), ((), ())), preferred_element_type=F32)


def tn(a, b):
    return lax.dot_general(a, b, (((0,), (0,)), ((), ())), preferred_element_type=F32)


def vmem(shape, dtype):
    return pltpu.VMEM(shape, dtype)


ANY = pl.BlockSpec(memory_space=pl.ANY)
SMEM = pl.BlockSpec(memory_space=pltpu.SMEM)


def whole(shape):
    zeros = (0,) * len(shape)
    return pl.BlockSpec(shape, lambda *_: zeros)


def call(body, grid, in_specs, out_specs, out_shape, scratch, args, flops, nbytes, aliases=None):
    return pl.pallas_call(
        body,
        grid=grid,
        in_specs=in_specs,
        out_specs=out_specs,
        out_shape=out_shape,
        scratch_shapes=scratch,
        input_output_aliases=aliases or {},
        compiler_params=pltpu.CompilerParams(
            vmem_limit_bytes=VMEM_LIMIT, dimension_semantics=("arbitrary",) * len(grid)
        ),
        cost_estimate=pl.CostEstimate(flops=flops, bytes_accessed=nbytes, transcendentals=0),
    )(*args)


class Gathered:
    def __init__(self, own, arrays, where):
        self.own, self.arrays, self.where = own, arrays, where
        self.rows = own.shape[0] // GROUP

    def count(self):
        return 1 + len(self.arrays)

    def copies(self, refs, block, slot, held, sems, me):
        out = []
        for j, (which, lead) in enumerate(self.where):
            src = refs[1 + which]
            src = src.at[block] if lead is None else src.at[lead, block]
            start = pl.multiple_of((me ^ j) * self.rows, self.rows)
            out.append(
                pltpu.make_async_copy(
                    src, held.at[slot, pl.ds(start, self.rows)], sems.at[slot, j]
                )
            )
        return out


def start_all(weight, refs, held, sems, me, own):
    blocks = held.shape[0] - (1 if own else 0)
    if own:
        pltpu.make_async_copy(refs[0], held.at[0], sems.at[0, 0]).start()
    for b in range(blocks):
        for c in weight.copies(refs, b, b + (1 if own else 0), held, sems, me):
            c.start()


def wait_one(weight, refs, held, sems, me, own, step):
    if own:

        @pl.when(step == 0)
        def _():
            pltpu.make_async_copy(refs[0], held.at[0], sems.at[0, 0]).wait()

        @pl.when(step > 0)
        def _():
            for c in weight.copies(refs, step - 1, step, held, sems, me):
                c.wait()
    else:
        for c in weight.copies(refs, step, step, held, sems, me):
            c.wait()


def put_pieces(me, grad, keep, send, rows):
    for j in range(GROUP):
        start = pl.multiple_of((me ^ j) * rows, rows)
        piece = grad[pl.ds(start, rows), :].astype(B16)
        (send if j % 2 else keep)[j // 2, 0] = piece


def norm(residual):
    center = residual - jnp.mean(residual, axis=-1, keepdims=True)
    variance = jnp.mean(center * center, axis=-1, keepdims=True)
    inverse = lax.rsqrt(variance + EPSILON)
    return center * inverse, inverse


def norm_back(upstream, normed, inverse, gain):
    scaled = upstream * gain
    return (
        scaled
        - jnp.mean(scaled, axis=-1, keepdims=True)
        - normed * jnp.mean(scaled * normed, axis=-1, keepdims=True)
    ) * inverse


def column_sum(x):
    return jnp.sum(x, axis=0, keepdims=True)


def bias_tiles(table, tiles, seq):
    heads, pooled = tiles.shape[0], tiles.shape[1]
    for h in range(heads):
        row = jnp.broadcast_to(table[h : h + 1, :], (pooled, table.shape[1]))
        rolled = pltpu.roll(row, table.shape[1] - seq, 1, stride=2, stride_axis=0)
        tiles[h] = rolled[:, :seq]


def attend(weight, hid, pool, bias, table, segq, segk, q_out, kv_out, ctx_out, lse_out, tiles, dims):
    rows, seq, pooled, heads, width = dims
    local = heads * width
    scale = width ** (-0.5)
    kv_bias = jnp.concatenate([jnp.zeros((1, local), F32), bias[:, local : 2 * local]], axis=1)
    q_bias = bias[:, :local]
    bias_tiles(table, tiles, seq)

    def project(r, carry):
        at = pl.ds(pl.multiple_of(r * seq, seq), seq)
        kv_out[0, at, :] = (nn(hid[at, :], weight[:, : 2 * local]) + kv_bias).astype(B16)
        at = pl.ds(pl.multiple_of(r * pooled, pooled), pooled)
        q_out[0, at, :] = (nn(pool[at, :], weight[:, 2 * local : 3 * local]) + q_bias).astype(B16)
        return carry

    lax.fori_loop(0, rows, project, 0)

    def one_row(r, carry):
        at = pl.ds(pl.multiple_of(r * seq, seq), seq)
        qat = pl.ds(pl.multiple_of(r * pooled, pooled), pooled)
        allowed = segq[r] == segk[r]
        for h in range(heads):
            lanes = slice(h * width, (h + 1) * width)
            query = (q_out[0, qat, lanes].astype(F32) * scale).astype(B16)
            scores = nt(query, kv_out[0, at, lanes]) + tiles[h]
            scores = jnp.where(allowed, scores, MASKED_SCORE)
            top = jnp.max(scores, axis=-1, keepdims=True)
            exponent = jnp.exp(scores - top)
            total = jnp.sum(exponent, axis=-1, keepdims=True)
            low = (exponent * (1.0 / total)).astype(B16)
            value = kv_out[0, at, local + h * width : local + (h + 1) * width]
            ctx_out[0, qat, lanes] = nn(low, value).astype(B16)
            lse_out[0, qat, h : h + 1] = top + jnp.log(total)
        return carry

    lax.fori_loop(0, rows, one_row, 0)


def own_body(dims, hidden, weight, bias, table, segq, segk,
             pooled_out, pool_low, q_out, kv_out, ctx_out, lse_out, partial_out, wide, tiles):
    rows, seq, pooled, heads, width = dims
    local = heads * width
    n = rows * pooled
    for c in range(0, hidden.shape[1], 128):
        wide[...] = hidden[:, c : c + 128].astype(F32)
        mean = 0.5 * (wide[pl.ds(0, n, stride=2), :] + wide[pl.ds(1, n, stride=2), :])
        pooled_out[:, c : c + 128] = mean
        pool_low[:, c : c + 128] = mean.astype(B16)
    attend(weight, hidden, pool_low, bias[0], table.at[0], segq, segk,
           q_out, kv_out, ctx_out, lse_out, tiles, dims)
    partial_out[...] = nt(ctx_out[0], weight[:, 3 * local :])


def rest_body(dims, gathered, me_ref, hidden, pool_low, bias, table, segq, segk, partial_in,
              pooled, out_bias, q_in, kv_in, ctx_in, lse_in, *refs):
    rows, seq, pooled_len, heads, width = dims
    local = heads * width
    sources = refs[: gathered.count()]
    q_out, kv_out, ctx_out, lse_out, normed, inverse, held, tiles, total, sems = refs[gathered.count() :]
    step = pl.program_id(0)
    me = me_ref[0]

    @pl.when(step == 0)
    def _():
        start_all(gathered, sources, held, sems, me, False)
        total[...] = partial_in[...]

    wait_one(gathered, sources, held, sems, me, False, step)
    weight = held.at[step]
    attend(weight, hidden, pool_low, bias[0], table.at[0], segq, segk,
           q_out, kv_out, ctx_out, lse_out, tiles, dims)
    total[...] += nt(ctx_out[0], weight[:, 3 * local :])

    @pl.when(step == pl.num_programs(0) - 1)
    def _():
        n, s = norm(pooled[...] + (total[...] + out_bias[...]))
        normed[...] = n
        inverse[...] = s


def up_body(gathered, me_ref, normed, gain, shift, bias, *refs):
    sources = refs[: gathered.count()]
    act, slope, held, low, sems = refs[gathered.count() :]
    step = pl.program_id(0)
    me = me_ref[0]

    @pl.when(step == 0)
    def _():
        start_all(gathered, sources, held, sems, me, True)
        low[...] = (normed[...] * gain[...] + shift[...]).astype(B16)

    wait_one(gathered, sources, held, sems, me, True, step)
    n = held.shape[2]
    chunk = 256
    for c in range(0, n, chunk):
        pre = nn(low[...], held[step, :, c : c + chunk]) + bias[0][:, c : c + chunk]
        phi = 0.5 * (1.0 + lax.erf(pre * (0.5**0.5)))
        density = jnp.exp(-0.5 * pre * pre) * 0.3989422804014327
        act[0, :, c : c + chunk] = (pre * phi).astype(B16)
        slope[0, :, c : c + chunk] = (phi + pre * density).astype(B16)


def down_body(gathered, me_ref, act, slope, normed, gain1, shift1, bias, gain2, shift2, cot, *refs):
    sources = refs[: gathered.count()]
    (output, grad_out, sums, gpre, bias_grad, keep, send,
     held, total, low, grad, sems) = refs[gathered.count() :]
    phase, step = pl.program_id(0), pl.program_id(1)
    me = me_ref[0]

    @pl.when(phase == 0)
    def _():
        @pl.when(step == 0)
        def _():
            start_all(gathered, sources, held, sems, me, True)
            total[...] = normed[...] * gain1[...] + shift1[...] + bias[...]

        wait_one(gathered, sources, held, sems, me, True, step)
        total[...] += nn(act[0], held[step])

        @pl.when(step == pl.num_programs(1) - 1)
        def _():
            n, s = norm(total[...])
            output[...] = (n * gain2[...] + shift2[...]).astype(B16)
            upstream = cot[...].astype(F32)
            back = norm_back(upstream, n, s, gain2[...])
            grad_out[...] = back
            low[...] = back.astype(B16)
            sums[...] = jnp.zeros_like(sums)
            sums[0:1, :] = column_sum(upstream * n)
            sums[1:2, :] = column_sum(upstream)
            sums[2:3, :] = column_sum(back)

    @pl.when(phase == 1)
    def _():
        grad[...] = tn(act[0], low[...])
        put_pieces(me, grad, keep, send, gathered.rows)
        low_pre = (nt(low[...], held[step]) * slope[0].astype(F32)).astype(B16)
        gpre[0] = low_pre
        bias_grad[0] = column_sum(low_pre.astype(F32))


def up_back_body(gathered, me_ref, gpre, normed, inverse, gain, shift, grad_in, *refs):
    sources = refs[: gathered.count()]
    (grad_first, grad_low, sums, keep, send, held, total, low, grad, sems) = refs[gathered.count() :]
    step = pl.program_id(0)
    me = me_ref[0]

    @pl.when(step == 0)
    def _():
        start_all(gathered, sources, held, sems, me, True)
        low[...] = (normed[...] * gain[...] + shift[...]).astype(B16)
        total[...] = grad_in[...]

    grad[...] = tn(low[...], gpre[0])
    put_pieces(me, grad, keep, send, gathered.rows)
    wait_one(gathered, sources, held, sems, me, True, step)
    total[...] += nt(gpre[0], held[step])

    @pl.when(step == pl.num_programs(0) - 1)
    def _():
        upstream = total[...]
        n = normed[...]
        back = norm_back(upstream, n, inverse[...], gain[...])
        grad_first[...] = back
        grad_low[...] = back.astype(B16)
        sums[...] = jnp.zeros_like(sums)
        sums[0:1, :] = column_sum(upstream * n)
        sums[1:2, :] = column_sum(upstream)
        sums[2:3, :] = column_sum(back)


def diagonal_sums(tile, seq, table_len):
    rows = tile.shape[0]
    x = jnp.concatenate([jnp.zeros((rows, table_len - seq), F32), tile], axis=1)
    while rows > 8:
        half = rows // 2
        x = x[:half] + pltpu.roll(x[half:], table_len - 2 * half, 1)
        rows = half
    out = x[0:1]
    for i in range(1, rows):
        out = out + pltpu.roll(x, table_len - 2 * i, 1)[i : i + 1]
    return out


def attend_back_body(dims, gathered, me_ref, hidden, pool_low, table, segq, segk, q_in, kv_in, ctx_in,
                     lse_in, grad_first, grad_low, *refs):
    rows, seq, pooled, heads, width = dims
    local = heads * width
    scale = width ** (-0.5)
    sources = refs[: gathered.count()]
    (hidden_grad, small, keep, send, held, tiles, tile_grad, gctx, dq, dkv, grad, htotal, ptotal,
     wide, sems) = refs[gathered.count() :]
    step = pl.program_id(0)
    me = me_ref[0]

    @pl.when(step == 0)
    def _():
        start_all(gathered, sources, held, sems, me, True)
        htotal[...] = jnp.zeros_like(htotal)
        ptotal[...] = grad_first[...]

    bias_tiles(table.at[0], tiles, seq)
    tile_grad[...] = jnp.zeros_like(tile_grad)
    wait_one(gathered, sources, held, sems, me, True, step)
    weight = held.at[step]
    gctx[...] = nn(grad_low[...], weight[:, 3 * local :]).astype(B16)

    def one_row(r, carry):
        at = pl.ds(pl.multiple_of(r * seq, seq), seq)
        qat = pl.ds(pl.multiple_of(r * pooled, pooled), pooled)
        allowed = segq[r] == segk[r]
        for h in range(heads):
            lanes = slice(h * width, (h + 1) * width)
            vlanes = slice(local + h * width, local + (h + 1) * width)
            query = (q_in[0, qat, lanes].astype(F32) * scale).astype(B16)
            key = kv_in[0, at, lanes]
            scores = nt(query, key) + tiles[h]
            scores = jnp.where(allowed, scores, MASKED_SCORE)
            prob = jnp.exp(scores - lse_in[0, qat, h : h + 1])
            upstream = gctx[qat, lanes]
            gprob = nt(upstream, kv_in[0, at, vlanes])
            inner = jnp.sum(prob * gprob, axis=-1, keepdims=True)
            gscore = (prob * (gprob - inner)).astype(B16)
            tile_grad[h] += gscore.astype(F32)
            dkv[at, vlanes] = tn(prob.astype(B16), upstream).astype(B16)
            dkv[at, lanes] = tn(gscore, query).astype(B16)
            dq[qat, lanes] = (nn(gscore, key) * scale).astype(B16)
        return carry

    lax.fori_loop(0, rows, one_row, 0)
    small[...] = jnp.zeros_like(small)
    for h in range(heads):
        small[0, h : h + 1, :] = diagonal_sums(tile_grad[h], seq, small.shape[2])
    small[0, heads : heads + 1, :local] = column_sum(dq[...].astype(F32))
    small[0, heads + 1 : heads + 2, :local] = column_sum(dkv[:, local:].astype(F32))
    grad[:, : 2 * local] = tn(hidden[...], dkv[...])
    grad[:, 2 * local : 3 * local] = tn(pool_low[...], dq[...])
    grad[:, 3 * local :] = tn(grad_low[...], ctx_in[0])
    put_pieces(me, grad, keep, send, gathered.rows)
    htotal[...] += nt(dkv[...], weight[:, : 2 * local])
    ptotal[...] += nt(dq[...], weight[:, 2 * local : 3 * local])

    @pl.when(step == pl.num_programs(0) - 1)
    def _():
        n = ptotal.shape[0]
        for c in range(0, ptotal.shape[1], 128):
            half = 0.5 * ptotal[:, c : c + 128]
            wide[pl.ds(0, n, stride=2), :] = half
            wide[pl.ds(1, n, stride=2), :] = half
            hidden_grad[:, c : c + 128] = (htotal[:, c : c + 128] + wide[...]).astype(B16)


def unpack_body(where, me_ref, *refs):
    n = max(w for w, _ in where) + 1
    out = refs[n]
    rows = out.shape[0] // GROUP
    for j, (which, lead) in enumerate(where):
        src = refs[which][...] if lead is None else refs[which][lead]
        out[pl.ds(pl.multiple_of((me_ref[0] ^ j) * rows, rows), rows), :] = src.astype(F32)


def unpack_attention_body(where, me_ref, *refs):
    n = max(w for w, _ in where) + 1
    key, value, query, out, turned = refs[n:]
    rows = key.shape[0] // GROUP
    local = key.shape[1]
    for j, (which, lead) in enumerate(where):
        src = (refs[which][...] if lead is None else refs[which][lead]).astype(F32)
        at = pl.ds(pl.multiple_of((me_ref[0] ^ j) * rows, rows), rows)
        key[at, :] = src[:, :local]
        value[at, :] = src[:, local : 2 * local]
        query[at, :] = src[:, 2 * local : 3 * local]
        turned[at, :] = src[:, 3 * local :]
    out[...] = turned[...].T


def per_device(n_dp, n_t, hidden, cotangent, segments, pooled_segments, positions,
               query_projection_weight, query_bias, key_weight, value_weight, value_bias,
               output_projection_weight, out_bias, relative_bias, first_gain, first_shift,
               up_projection_weight, up_projection_bias, down_projection_weight, down_bias,
               second_gain, second_shift):
    rows, seq, model = hidden.shape
    pooled_len = seq // 2
    heads, table_len = relative_bias.shape
    width = query_projection_weight.shape[1] // heads
    local = heads * width
    ff = up_projection_weight.shape[1]
    dims = (rows, seq, pooled_len, heads, width)
    tokens, ptokens = rows * seq, rows * pooled_len
    blocks = n_t
    dp_index = lax.axis_index("dp")
    t_index = lax.axis_index("tensor")
    me = dp_index % GROUP
    me_arr = me.astype(jnp.int32).reshape(1)

    def across(x, mask):
        return lax.ppermute(x, "dp", [(i, i ^ mask) for i in range(n_dp)])

    def along(x, mask):
        return lax.ppermute(x, "tensor", [(i, i ^ mask) for i in range(n_t)])

    def gather(own, order):
        size = own.shape[0] // GROUP
        piece = lax.dynamic_slice(own, (me * size, 0), (size, own.shape[1]))
        base = jnp.stack([along(piece, k) for k in range(1, blocks)])
        if order is None:
            a, b, c = across(base, 2), across(base, 4), across(base, 6)
            even = [base, a, b, c]
            arrays = even + [across(e, 1) for e in even]
            where = [(0, None), (4, None), (1, None), (5, None), (2, None), (6, None), (3, None), (7, None)]
        else:
            first, second = order
            a = across(base, first)
            b = across(jnp.stack([base, a]), second)
            even = [base, a, b]
            arrays = even + [across(e, 1) for e in even]
            place = {0: (0, None), first: (1, None), second: (2, 0), first | second: (2, 1)}
            where = []
            for j in range(GROUP):
                which, lead = place[j & 6]
                where.append((which + (3 if j & 1 else 0), lead))
        return Gathered(own, arrays, where)

    def reduce(keep, send, x_first):
        got = across(send, 1)
        sum0 = keep.astype(F32) + got.astype(F32)
        sum0 = sum0.reshape((2, 2) + sum0.shape[1:])
        if x_first:
            out1, in1, m1, m2 = sum0[:, 1], sum0[:, 0], 2, 4
        else:
            out1, in1, m1, m2 = sum0[1], sum0[0], 4, 2
        sum1 = in1 + across(out1.astype(B16), m1).astype(F32)
        sum2 = sum1[0] + across(sum1[1].astype(B16), m2).astype(F32)
        bit = GROUP
        while bit < n_dp:
            sum2 = sum2 + across(sum2.astype(B16), bit).astype(F32)
            bit *= 2
        pairs = sum2.reshape((2, 2) + sum2.shape[1:])
        sum3 = pairs[:, 0] + along(pairs[:, 1].astype(B16), 1).astype(F32)
        done = (sum3[0] + along(sum3[1].astype(B16), 2).astype(F32)).astype(B16)
        a = across(done, m2)
        b = across(jnp.stack([done, a]), m1)
        even = [done, a, b]
        arrays = even + [across(e, 1) for e in even]
        place = {0: (0, None), m2: (1, None), m1: (2, 0), 6: (2, 1)}
        where = []
        for j in range(GROUP):
            which, lead = place[j & 6]
            where.append((which + (3 if j & 1 else 0), lead))
        return arrays, where

    def row(v):
        return v.astype(F32).reshape(1, -1)

    sds = jax.ShapeDtypeStruct
    attn_own = jnp.concatenate(
        [key_weight, value_weight, query_projection_weight, output_projection_weight.T], axis=1
    )
    pad = jnp.zeros((table_len,), F32)
    vector = jnp.stack(
        [
            pad.at[: 2 * local].set(jnp.concatenate([query_bias, value_bias]).astype(F32)),
            pad.at[:ff].set(up_projection_bias.astype(F32)),
        ]
    )
    vector = jnp.concatenate([relative_bias, vector])
    vectors = jnp.stack([vector] + [along(vector, k) for k in range(1, blocks)])
    tables = vectors[:, :heads]
    attn_bias = vectors[:, heads : heads + 1, : 2 * local]
    up_bias = vectors[:, heads + 1 : heads + 2, :ff]

    attn_w = gather(attn_own, None)
    up_w = gather(up_projection_weight, (2, 4))
    down_w = gather(down_projection_weight, (4, 2))

    seg = lax.dynamic_slice(segments, (t_index * rows, 0), (rows, seq)).reshape(rows, 1, seq)
    pseg = lax.dynamic_slice(pooled_segments, (t_index * rows, 0), (rows, pooled_len))
    pseg = pseg.reshape(rows, pooled_len, 1)
    hid = hidden.reshape(tokens, model)
    cot = cotangent.reshape(ptokens, model)

    lane = 128
    saved_shapes = [
        sds((blocks, ptokens, local), B16),
        sds((blocks, tokens, 2 * local), B16),
        sds((blocks, ptokens, local), B16),
        sds((blocks, ptokens, lane), F32),
    ]

    def block_specs(offset):
        return [
            pl.BlockSpec((1,) + s.shape[1:], lambda i, offset=offset: (i + offset, 0, 0)) for s in saved_shapes
        ]

    def block(shape, offset=0):
        return pl.BlockSpec((1,) + shape, lambda i: (i + offset,) + (0,) * len(shape))

    attn_flops = 2 * (3 * ptokens + 2 * tokens) * model * local
    own_out = call(
        partial(own_body, dims),
        (1,),
        [whole((tokens, model)), whole((model, 4 * local)), block((1, 2 * local)), block((heads, table_len)),
         whole(pseg.shape), whole(seg.shape)],
        [whole((ptokens, model)), whole((ptokens, model))] + block_specs(0) + [whole((ptokens, model))],
        [sds((ptokens, model), F32), sds((ptokens, model), B16)] + saved_shapes + [sds((ptokens, model), F32)],
        [vmem((tokens, 128), F32), vmem((heads, pooled_len, seq), F32)],
        (hid, attn_own, attn_bias, tables, pseg, seg),
        attn_flops, 8 << 20,
    )
    pooled, pool_low, saved, attended_own = own_out[0], own_out[1], own_out[2:6], own_out[6]

    n_in = 10
    rest_out = call(
        partial(rest_body, dims, attn_w),
        (blocks - 1,),
        [SMEM, whole((tokens, model)), whole((ptokens, model)), block((1, 2 * local), 1),
         block((heads, table_len), 1), whole(pseg.shape), whole(seg.shape), whole((ptokens, model)),
         whole((ptokens, model)), whole((1, model))] + [ANY] * 4 + [ANY] * attn_w.count(),
        block_specs(1) + [whole((ptokens, model)), whole((ptokens, 1))],
        saved_shapes + [sds((ptokens, model), F32), sds((ptokens, 1), F32)],
        [vmem((blocks - 1, model, 4 * local), B16), vmem((heads, pooled_len, seq), F32),
         vmem((ptokens, model), F32), pltpu.SemaphoreType.DMA((blocks - 1, GROUP))],
        (me_arr, hid, pool_low, attn_bias, tables, pseg, seg, attended_own, pooled, row(out_bias),
         *saved, attn_w.own, *attn_w.arrays),
        3 * attn_flops, 16 << 20,
        {n_in + i: i for i in range(4)},
    )
    saved, normed, inverse = rest_out[:4], rest_out[4], rest_out[5]

    gain1, shift1, gain2, shift2 = row(first_gain), row(first_shift), row(second_gain), row(second_shift)
    dims_ff = (blocks, ptokens, ff)
    ff_flops = 2 * blocks * ptokens * ff * model
    vec = whole((1, model))
    act, slope = call(
        partial(up_body, up_w),
        (blocks,),
        [SMEM, whole((ptokens, model)), vec, vec, block((1, ff))] + [ANY] * up_w.count(),
        [block((ptokens, ff)), block((ptokens, ff))],
        [sds(dims_ff, B16), sds(dims_ff, B16)],
        [vmem((blocks, model, ff), B16), vmem((ptokens, model), B16), pltpu.SemaphoreType.DMA((blocks, GROUP))],
        (me_arr, normed, gain1, shift1, up_bias, up_w.own, *up_w.arrays),
        ff_flops, 16 << 20,
    )

    def grad_shape(w):
        return sds((GROUP // 2, blocks, w.rows, w.own.shape[1]), B16)

    def grad_spec(w, index):
        return pl.BlockSpec((GROUP // 2, 1, w.rows, w.own.shape[1]), index)

    def late(phase, step):
        return phase * step

    by_step = lambda p, k: (k, 0, 0)
    by_late = lambda p, k: (p * k, 0, 0)
    output, grad_second, sums2, gpre, up_bias_grad, down_keep, down_send = call(
        partial(down_body, down_w),
        (2, blocks),
        [SMEM, pl.BlockSpec((1, ptokens, ff), by_step), pl.BlockSpec((1, ptokens, ff), by_late),
         whole((ptokens, model)), vec, vec, vec, vec, vec, whole((ptokens, model))] + [ANY] * down_w.count(),
        [whole((ptokens, model)), whole((ptokens, model)), whole((8, model)),
         pl.BlockSpec((1, ptokens, ff), by_late), pl.BlockSpec((1, 1, ff), by_late),
         grad_spec(down_w, lambda p, k: (0, p * k, 0, 0)), grad_spec(down_w, lambda p, k: (0, p * k, 0, 0))],
        [sds((ptokens, model), B16), sds((ptokens, model), F32), sds((8, model), F32), sds(dims_ff, B16),
         sds((blocks, 1, ff), F32), grad_shape(down_w), grad_shape(down_w)],
        [vmem((blocks, ff, model), B16), vmem((ptokens, model), F32), vmem((ptokens, model), B16),
         vmem((ff, model), F32), pltpu.SemaphoreType.DMA((blocks, GROUP))],
        (me_arr, act, slope, normed, gain1, shift1, row(down_bias), gain2, shift2, cot,
         down_w.own, *down_w.arrays),
        3 * ff_flops, 24 << 20,
    )
    down_done = reduce(down_keep, down_send, True)

    grad_first, grad_low, sums1, up_keep, up_send = call(
        partial(up_back_body, up_w),
        (blocks,),
        [SMEM, block((ptokens, ff)), whole((ptokens, model)), whole((ptokens, 1)), vec, vec,
         whole((ptokens, model))] + [ANY] * up_w.count(),
        [whole((ptokens, model)), whole((ptokens, model)), whole((8, model)),
         grad_spec(up_w, lambda k: (0, k, 0, 0)), grad_spec(up_w, lambda k: (0, k, 0, 0))],
        [sds((ptokens, model), F32), sds((ptokens, model), B16), sds((8, model), F32),
         grad_shape(up_w), grad_shape(up_w)],
        [vmem((blocks, model, ff), B16), vmem((ptokens, model), F32), vmem((ptokens, model), B16),
         vmem((model, ff), F32), pltpu.SemaphoreType.DMA((blocks, GROUP))],
        (me_arr, gpre, normed, inverse, gain1, shift1, grad_second, up_w.own, *up_w.arrays),
        2 * ff_flops, 20 << 20,
    )
    up_done = reduce(up_keep, up_send, False)

    saved_in = [pl.BlockSpec((1,) + s.shape[1:], lambda i: (i, 0, 0)) for s in saved_shapes]
    hidden_grad, small, attn_keep, attn_send = call(
        partial(attend_back_body, dims, attn_w),
        (blocks,),
        [SMEM, whole((tokens, model)), whole((ptokens, model)), block((heads, table_len)),
         whole(pseg.shape), whole(seg.shape)] + saved_in
        + [whole((ptokens, model)), whole((ptokens, model))] + [ANY] * attn_w.count(),
        [whole((tokens, model)), block((8, table_len)),
         grad_spec(attn_w, lambda k: (0, k, 0, 0)), grad_spec(attn_w, lambda k: (0, k, 0, 0))],
        [sds((tokens, model), B16), sds((blocks, 8, table_len), F32), grad_shape(attn_w), grad_shape(attn_w)],
        [vmem((blocks, model, 4 * local), B16), vmem((heads, pooled_len, seq), F32),
         vmem((heads, pooled_len, seq), F32), vmem((ptokens, local), B16), vmem((ptokens, local), B16),
         vmem((tokens, 2 * local), B16), vmem((model, 4 * local), F32), vmem((tokens, model), F32),
         vmem((ptokens, model), F32), vmem((tokens, 128), F32), pltpu.SemaphoreType.DMA((blocks, GROUP))],
        (me_arr, hid, pool_low, tables, pseg, seg, *saved, grad_first, grad_low, attn_w.own, *attn_w.arrays),
        12 * attn_flops, 28 << 20,
    )
    attn_done = reduce(attn_keep, attn_send, True)

    def unpack(done, shape):
        arrays, where = done
        return call(
            partial(unpack_body, where), (1,), [SMEM] + [whole(a.shape) for a in arrays], whole(shape),
            sds(shape, F32), [], (me_arr, *arrays), 0, 4 << 20,
        )

    down_weight_gradient = unpack(down_done, (ff, model))
    up_weight_gradient = unpack(up_done, (model, ff))
    arrays, where = attn_done
    key_grad, value_grad, query_grad, out_grad = call(
        partial(unpack_attention_body, where), (1,), [SMEM] + [whole(a.shape) for a in arrays],
        [whole((model, local))] * 3 + [whole((local, model))],
        [sds((model, local), F32)] * 3 + [sds((local, model), F32)],
        [vmem((model, local), F32)], (me_arr, *arrays), 0, 4 << 20,
    )

    shared = jnp.concatenate([sums1[:3], sums2[:3]])
    bit = 1
    while bit < n_dp:
        shared = shared + across(shared, bit)
        bit *= 2
    for k in (1, 2):
        shared = shared + along(shared, k)
    small = jnp.concatenate(
        [small[:, : heads + 2], jnp.pad(up_bias_grad, ((0, 0), (0, 0), (0, table_len - ff)))], axis=1
    )
    bit = 1
    while bit < n_dp:
        small = small + across(small, bit)
        bit *= 2
    pairs = small.reshape((2, 2) + small.shape[1:])
    pairs = pairs[:, 0] + along(pairs[:, 1], 1)
    small = pairs[0] + along(pairs[1], 2)

    return (
        output.reshape(rows, pooled_len, model),
        hidden_grad.reshape(rows, seq, model),
        query_grad,
        small[heads, :local],
        key_grad,
        value_grad,
        small[heads + 1, :local],
        out_grad,
        shared[2],
        small[:heads],
        shared[0],
        shared[1],
        up_weight_gradient,
        small[heads + 2, :ff],
        down_weight_gradient,
        shared[5],
        shared[3],
        shared[4],
    )


def solution(mesh):
    placed = (
        P(("dp", "tensor"), None, None),
        P(("dp", "tensor"), None, None),
        P("dp", None),
        P("dp", None),
        P("dp", None),
        P(None, "tensor"),
        P("tensor"),
        P(None, "tensor"),
        P(None, "tensor"),
        P("tensor"),
        P("tensor", None),
        P(),
        P("tensor", None),
        P(),
        P(),
        P(None, "tensor"),
        P("tensor"),
        P("tensor", None),
        P(),
        P(),
        P(),
    )
    return jax.shard_map(
        partial(per_device, mesh.shape["dp"], mesh.shape["tensor"]),
        mesh=mesh,
        in_specs=placed,
        out_specs=(
            P(("dp", "tensor"), None, None),
            P(("dp", "tensor"), None, None),
            P(None, "tensor"),
            P("tensor"),
            P(None, "tensor"),
            P(None, "tensor"),
            P("tensor"),
            P("tensor", None),
            P(),
            P("tensor", None),
            P(),
            P(),
            P(None, "tensor"),
            P("tensor"),
            P("tensor", None),
            P(),
            P(),
            P(),
        ),
        check_vma=False,
    )
```

```python
from functools import partial

import jax
import jax.numpy as jnp
from jax import lax
from jax.experimental import pallas as pl
from jax.experimental.pallas import tpu as pltpu
from jax.sharding import PartitionSpec as P

EPSILON = 1e-05
MASKED_SCORE = -1000000000.0
GROUP = 8
F32 = jnp.float32
B16 = jnp.bfloat16


def nn(a, b):
    return lax.dot_general(a, b, (((1,), (0,)), ((), ())), preferred_element_type=F32)


def nt(a, b):
    return lax.dot_general(a, b, (((1,), (1,)), ((), ())), preferred_element_type=F32)


def tn(a, b):
    return lax.dot_general(a, b, (((0,), (0,)), ((), ())), preferred_element_type=F32)


def vmem(shape, dtype):
    return pltpu.VMEM(shape, dtype)


ANY = pl.BlockSpec(memory_space=pl.ANY)
SMEM = pl.BlockSpec(memory_space=pltpu.SMEM)


def whole(shape):
    zeros = (0,) * len(shape)
    return pl.BlockSpec(shape, lambda *_: zeros)


def call(body, grid, in_specs, out_specs, out_shape, scratch, args, limit, aliases=None):
    out = pl.pallas_call(
        body,
        grid=grid,
        in_specs=in_specs,
        out_specs=out_specs,
        out_shape=out_shape,
        scratch_shapes=scratch,
        input_output_aliases=aliases or {},
        compiler_params=pltpu.CompilerParams(
            vmem_limit_bytes=60 << 20, dimension_semantics=("arbitrary",) * len(grid)
        ),
        cost_estimate=pl.CostEstimate(flops=1 << 20, bytes_accessed=1 << 16, transcendentals=0),
    )(*args)
    return list(out) if isinstance(out, (list, tuple)) else out


class Gathered:
    def __init__(self, own, arrays, parts):
        self.own, self.arrays, self.parts = own, arrays, parts
        self.rows = own.shape[0] // GROUP

    def count(self):
        return 1 + len(self.arrays)

    def copies(self, refs, block, slot, held, sems, me):
        if block == 0:
            return [pltpu.make_async_copy(refs[0], held.at[slot], sems.at[slot, 0, 0])]
        out = []
        for j, parts in enumerate(self.parts):
            for i, (which, first, count) in enumerate(parts):
                start = pl.multiple_of((me ^ j) * self.rows + first, 8)
                out.append(pltpu.make_async_copy(
                    refs[1 + which].at[block - 1], held.at[slot, pl.ds(start, count)], sems.at[slot, j, i]))
        return out

    def start(self, refs, blocks, held, sems, me):
        for slot, block in enumerate(blocks):
            for c in self.copies(refs, block, slot, held, sems, me):
                c.start()

    def wait(self, refs, blocks, held, sems, me, step):
        for slot, block in enumerate(blocks):

            @pl.when(step == slot)
            def _(slot=slot, block=block):
                for c in self.copies(refs, block, slot, held, sems, me):
                    c.wait()


def put_pieces(me, grad, keep, send, rows):
    for j in range(GROUP):
        start = pl.multiple_of((me ^ j) * rows, rows)
        piece = grad[pl.ds(start, rows), :].astype(B16)
        (send if j % 2 else keep)[j // 2, 0] = piece


def norm(residual):
    center = residual - jnp.mean(residual, axis=-1, keepdims=True)
    variance = jnp.mean(center * center, axis=-1, keepdims=True)
    inverse = lax.rsqrt(variance + EPSILON)
    return center * inverse, inverse


def norm_back(upstream, normed, inverse, gain):
    scaled = upstream * gain
    return (
        scaled
        - jnp.mean(scaled, axis=-1, keepdims=True)
        - normed * jnp.mean(scaled * normed, axis=-1, keepdims=True)
    ) * inverse


def column_sum(x):
    return jnp.sum(x, axis=0, keepdims=True)


def bias_tiles(table, tiles):
    heads, seq, pooled = tiles.shape
    for h in range(heads):
        row = jnp.broadcast_to(table[h : h + 1, :], (pooled, table.shape[1]))
        rolled = pltpu.roll(row, table.shape[1] - seq, 1, stride=2, stride_axis=0)
        tiles[h] = rolled[:, :seq].T


def attend(weight, hid, pool, bias, table, segq, segk, q_out, kv_out, ctx_out, lse_out, tiles, dims):
    rows, seq, pooled, heads, width = dims
    local = heads * width
    scale = width ** (-0.5)
    kv_bias = jnp.concatenate([jnp.zeros((1, local), F32), bias[:, local : 2 * local]], axis=1)
    q_bias = bias[:, :local]
    bias_tiles(table, tiles)

    def project(r, carry):
        at = pl.ds(pl.multiple_of(r * seq, seq), seq)
        kv_out[0, at, :] = (nt(hid[at, :], weight[: 2 * local, :]) + kv_bias).astype(B16)
        at = pl.ds(pl.multiple_of(r * pooled, pooled), pooled)
        q_out[0, at, :] = (nt(pool[at, :], weight[2 * local : 3 * local, :]) + q_bias).astype(B16)
        return carry

    lax.fori_loop(0, rows, project, 0)

    for r in range(rows):
        at = slice(r * seq, (r + 1) * seq)
        qat = slice(r * pooled, (r + 1) * pooled)
        allowed = segk[r] == segq[r]
        for h in range(heads):
            lanes = slice(h * width, (h + 1) * width)
            query = (q_out[0, qat, lanes].astype(F32) * scale).astype(B16)
            scores = nt(kv_out[0, at, lanes], query) + tiles[h]
            scores = jnp.where(allowed, scores, MASKED_SCORE)
            top = jnp.max(scores, axis=0, keepdims=True)
            exponent = jnp.exp(scores - top)
            total = jnp.sum(exponent, axis=0, keepdims=True)
            value = kv_out[0, at, local + h * width : local + (h + 1) * width]
            context = tn(value, exponent.astype(B16)) * (1.0 / total)
            ctx_out[0, qat, lanes] = context.T.astype(B16)
            lse_out[0, h : h + 1, qat] = top + jnp.log(total)


def own_body(dims, me_ref, hidden, weight, bias, table, segq, segk,
             pooled_out, pool_low, q_out, kv_out, ctx_out, lse_out, wide, tiles):
    rows, seq, pooled, heads, width = dims
    n = rows * pooled
    for c in range(0, hidden.shape[1], 128):
        wide[...] = hidden[:, c : c + 128].astype(F32)
        mean = 0.5 * (wide[pl.ds(0, n, stride=2), :] + wide[pl.ds(1, n, stride=2), :])
        pooled_out[:, c : c + 128] = mean
        pool_low[:, c : c + 128] = mean.astype(B16)
    attend(weight, hidden, pool_low, bias[0], table.at[0], segq, segk,
           q_out, kv_out, ctx_out, lse_out, tiles, dims)


def rest_body(dims, gathered, blocks, me_ref, hidden, pool_low, bias, table, segq, segk,
              q_in, kv_in, ctx_in, lse_in, *refs):
    sources = refs[: gathered.count()]
    q_out, kv_out, ctx_out, lse_out, held, tiles, sems = refs[gathered.count() :]
    step = pl.program_id(0)
    me = me_ref[0]

    @pl.when(step == 0)
    def _():
        gathered.start(sources, blocks, held, sems, me)

    gathered.wait(sources, blocks, held, sems, me, step)
    attend(held.at[step], hidden, pool_low, bias[0], table.at[0], segq, segk,
           q_out, kv_out, ctx_out, lse_out, tiles, dims)


def ffn_body(up_w, down_w, me_ref, ctx, pooled, cot, vectors, bias, *refs):
    n_up, n_down = up_w.count(), down_w.count()
    up_refs, down_refs = refs[:n_up], refs[n_up : n_up + n_down]
    (output, grad_first, gctx, bias_grad, sums, down_keep, down_send, up_keep, up_send,
     up_held, down_held, total, normed, inverse, low, grad_low, act, slope, grad, up_grad, up_sems, down_sems) = refs[n_up + n_down :]
    phase, step = pl.program_id(0), pl.program_id(1)
    last = pl.num_programs(1) - 1
    blocks = range(up_held.shape[0])
    model = low.shape[1]
    me = me_ref[0]
    out_bias, gain1, shift1, down_bias, gain2, shift2 = [vectors[i : i + 1, :] for i in range(6)]

    @pl.when(phase == 0)
    def _():
        @pl.when(step == 0)
        def _():
            up_w.start(up_refs, blocks, up_held, up_sems, me)
            down_w.start(down_refs, blocks, down_held, down_sems, me)
            total[...] = pooled[...] + out_bias
            sums[...] = jnp.zeros_like(sums)

        up_w.wait(up_refs, blocks, up_held, up_sems, me, step)
        total[...] += nn(ctx[step], up_held[step, model:, :])

        @pl.when(step == last)
        def _():
            n, s = norm(total[...])
            normed[...] = n
            inverse[...] = s
            first = n * gain1 + shift1
            low[...] = first.astype(B16)
            total[...] = first + down_bias

    @pl.when(phase == 1)
    def _():
        chunk = 256
        for c in range(0, up_held.shape[2], chunk):
            pre = nn(low[...], up_held[step, :model, c : c + chunk]) + bias[0][:, c : c + chunk]
            phi = 0.5 * (1.0 + lax.erf(pre * (0.5**0.5)))
            density = jnp.exp(-0.5 * pre * pre) * 0.3989422804014327
            act[step, :, c : c + chunk] = (pre * phi).astype(B16)
            slope[step, :, c : c + chunk] = (phi + pre * density).astype(B16)
        down_w.wait(down_refs, blocks, down_held, down_sems, me, step)
        total[...] += nn(act[step], down_held[step])

        @pl.when(step == last)
        def _():
            n, s = norm(total[...])
            output[...] = (n * gain2 + shift2).astype(B16)
            upstream = cot[...].astype(F32)
            back = norm_back(upstream, n, s, gain2)
            total[...] = back
            sums[3:4, :] = column_sum(upstream * n)
            sums[4:5, :] = column_sum(upstream)
            sums[5:6, :] = column_sum(back)

    @pl.when(phase == 2)
    def _():
        @pl.when(step == 0)
        def _():
            grad_low[...] = total[...].astype(B16)

        grad[...] = tn(act[step], grad_low[...])
        put_pieces(me, grad, down_keep, down_send, down_w.rows)
        value = (nt(grad_low[...], down_held[step]) * slope[step].astype(F32)).astype(B16)
        bias_grad[0] = column_sum(value.astype(F32))
        up_grad[step, :model, :] = tn(low[...], value).astype(B16)
        total[...] += nt(value, up_held[step, :model, :])

        @pl.when(step == last)
        def _():
            upstream = total[...]
            n = normed[...]
            back = norm_back(upstream, n, inverse[...], gain1)
            grad_first[...] = back
            grad_low[...] = back.astype(B16)
            sums[0:1, :] = column_sum(upstream * n)
            sums[1:2, :] = column_sum(upstream)
            sums[2:3, :] = column_sum(back)

    @pl.when(phase == 3)
    def _():
        gctx[0] = nt(grad_low[...], up_held[step, model:, :]).astype(B16)
        up_grad[step, model:, :] = tn(ctx[step], grad_low[...]).astype(B16)
        put_pieces(me, up_grad.at[step], up_keep, up_send, up_w.rows)


def diagonal_sums(tile, seq, table_len):
    rows = tile.shape[0]
    x = jnp.concatenate([jnp.zeros((rows, table_len - seq), F32), tile], axis=1)
    while rows > 8:
        half = rows // 2
        x = x[:half] + pltpu.roll(x[half:], table_len - 2 * half, 1)
        rows = half
    out = x[0:1]
    for i in range(1, rows):
        out = out + pltpu.roll(x, table_len - 2 * i, 1)[i : i + 1]
    return out


def attend_back_body(dims, me_ref, hidden, pool_low, table, segq, segk, q_in, kv_in, ctx_in, lse_in, gctx,
                     up_bias_grad, sums, dq_out, dkv_out, keep, send, tiles, tile_grad, grad, extra):
    rows, seq, pooled, heads, width = dims
    local = heads * width
    scale = width ** (-0.5)
    me = me_ref[0]
    bias_tiles(table.at[0], tiles)
    product = gctx[0].astype(F32) * ctx_in[0].astype(F32)
    high = product.astype(B16)
    rest = (product - high.astype(F32)).astype(B16)
    line = lax.broadcasted_iota(jnp.int32, (8, local), 0)
    col = lax.broadcasted_iota(jnp.int32, (8, local), 1)
    pick = ((col >= line * width) & (col < (line + 1) * width)).astype(F32).astype(B16)
    inner = nt(pick, high) + nt(pick, rest)

    for r in range(rows):
        at = slice(r * seq, (r + 1) * seq)
        qat = slice(r * pooled, (r + 1) * pooled)
        allowed = segk[r] == segq[r]
        for h in range(heads):
            lanes = slice(h * width, (h + 1) * width)
            vlanes = slice(local + h * width, local + (h + 1) * width)
            query = (q_in[0, qat, lanes].astype(F32) * scale).astype(B16)
            key = kv_in[0, at, lanes]
            scores = nt(key, query) + tiles[h]
            scores = jnp.where(allowed, scores, MASKED_SCORE)
            prob = jnp.exp(scores - lse_in[0, h : h + 1, qat])
            upstream = gctx[0, qat, lanes]
            gprob = nt(kv_in[0, at, vlanes], upstream)
            gscore = (prob * (gprob - inner[h : h + 1, qat])).astype(B16)
            if r == 0:
                tile_grad[h] = gscore.astype(F32)
            else:
                tile_grad[h] += gscore.astype(F32)
            dkv_out[0, at, vlanes] = nn(prob.astype(B16), upstream).astype(B16)
            dkv_out[0, at, lanes] = nn(gscore, query).astype(B16)
            dq_out[0, qat, lanes] = (tn(key, gscore) * scale).T.astype(B16)

    model = hidden.shape[1]
    table_len = table.shape[2]
    extra[...] = jnp.zeros_like(extra)
    for h in range(heads):
        line = diagonal_sums(tile_grad[h].T, seq, table_len)
        for i, at in enumerate(range(0, table_len, model)):
            size = min(model, table_len - at)
            extra[lines_of(table_len, model) * h + i : lines_of(table_len, model) * h + i + 1, :size] = line[:, at : at + size]
    at = lines_of(table_len, model) * heads
    extra[at : at + 1, :local] = column_sum(dq_out[0].astype(F32))
    extra[at + 1 : at + 2, :local] = column_sum(dkv_out[0, :, local:].astype(F32))
    extra[at + 2 : at + 3, : up_bias_grad.shape[2]] = up_bias_grad[0]
    extra[at + 3 : at + 9, :] = sums[:6, :]
    grad[: 2 * local, :] = tn(dkv_out[0], hidden[...])
    grad[2 * local :, :] = tn(dq_out[0], pool_low[...])
    rows = grad.shape[0] // GROUP
    lines = extra.shape[0] // GROUP
    for j in range(GROUP):
        owner = me ^ j
        out = send if j % 2 else keep
        out[j // 2, 0, :rows] = grad[pl.ds(pl.multiple_of(owner * rows, 8), rows), :].astype(B16)
        out[j // 2, 0, rows:] = extra[pl.ds(pl.multiple_of(owner * lines, 8), lines), :].astype(B16)


def lines_of(length, width):
    return -(-length // width)


def hidden_back_body(gathered, orders, me_ref, grad_first, *refs):
    sources = refs[: gathered.count()]
    rest = refs[gathered.count() :]
    n = len(orders)
    dqs, dkvs = rest[:n], rest[n : 2 * n]
    hidden_grad, held, htotal, ptotal, wide, sems = rest[2 * n :]
    me = me_ref[0]
    local = dqs[0].shape[2]
    order = [b for o in orders for b in o]
    gathered.start(sources, order, held, sems, me)
    ptotal[...] = grad_first[...]
    slot = 0
    for i, o in enumerate(orders):
        for at, block in enumerate(o):
            for c in gathered.copies(sources, block, slot, held, sems, me):
                c.wait()
            product = nn(dkvs[i][at], held[slot, : 2 * local, :])
            if slot == 0:
                htotal[...] = product
            else:
                htotal[...] += product
            ptotal[...] += nn(dqs[i][at], held[slot, 2 * local :, :])
            slot += 1
    m = ptotal.shape[0]
    for c in range(0, ptotal.shape[1], 128):
        half = 0.5 * ptotal[:, c : c + 128]
        wide[pl.ds(0, m, stride=2), :] = half
        wide[pl.ds(1, m, stride=2), :] = half
        hidden_grad[:, c : c + 128] = (htotal[:, c : c + 128] + wide[...]).astype(B16)


def take(refs, where):
    which, lead = where
    return refs[which][...] if lead is None else refs[which][lead]


def unpack_ffn_body(where, me_ref, *refs):
    n = max(w for w, _ in where) + 1
    up, out, down, total = refs[n:]
    rows, down_rows = total.shape[0] // GROUP, down.shape[0] // GROUP
    for j in range(GROUP):
        piece = take(refs, where[j]).astype(F32)
        owner = me_ref[0] ^ j
        total[pl.ds(pl.multiple_of(owner * rows, 8), rows), :] = piece[:rows]
        down[pl.ds(pl.multiple_of(owner * down_rows, 8), down_rows), :] = piece[rows:]
    up[...] = total[: up.shape[0], :]
    out[...] = total[up.shape[0] :, :]


def unpack_attention_body(where, heads, me_ref, *refs):
    n = max(w for w, _ in where) + 1
    weights, table, q_bias, v_bias, up_bias, norms, total, extra = refs[n : n + 3], *refs[n + 3 :]
    rows = total.shape[0] // GROUP
    lines = extra.shape[0] // GROUP
    for j in range(GROUP):
        piece = take(refs, where[j]).astype(F32)
        owner = me_ref[0] ^ j
        total[pl.ds(pl.multiple_of(owner * rows, 8), rows), :] = piece[:rows]
        extra[pl.ds(pl.multiple_of(owner * lines, 8), lines), :] = piece[rows:]
    local, model = weights[0].shape
    for i, out in enumerate(weights):
        out[...] = total[i * local : (i + 1) * local, :]
    table_len = table.shape[1]
    per = lines_of(table_len, model)
    for h in range(heads):
        for i, at in enumerate(range(0, table_len, model)):
            size = min(model, table_len - at)
            table[h : h + 1, at : at + size] = extra[per * h + i : per * h + i + 1, :size]
    at = per * heads
    q_bias[...] = extra[at : at + 1, :local]
    v_bias[...] = extra[at + 1 : at + 2, :local]
    up_bias[...] = extra[at + 2 : at + 3, : up_bias.shape[1]]
    norms[...] = extra[at + 3 : at + 9, :]


def per_device(n_dp, n_t, hidden, cotangent, segments, pooled_segments, positions,
               query_projection_weight, query_bias, key_weight, value_weight, value_bias,
               output_projection_weight, out_bias, relative_bias, first_gain, first_shift,
               up_projection_weight, up_projection_bias, down_projection_weight, down_bias,
               second_gain, second_shift):
    rows, seq, model = hidden.shape
    pooled_len = seq // 2
    heads, table_len = relative_bias.shape
    width = query_projection_weight.shape[1] // heads
    local = heads * width
    ff = up_projection_weight.shape[1]
    dims = (rows, seq, pooled_len, heads, width)
    tokens, ptokens = rows * seq, rows * pooled_len
    blocks = n_t
    sds = jax.ShapeDtypeStruct
    t_index = lax.axis_index("tensor")
    me = lax.axis_index("dp") % GROUP
    tok = me.astype(jnp.int32).reshape(1)

    def across(x, mask):
        return lax.ppermute(x, "dp", [(i, i ^ mask) for i in range(n_dp)])

    def along(x, mask):
        return lax.ppermute(x, "tensor", [(i, i ^ mask) for i in range(n_t)])

    def row(v):
        return v.astype(F32).reshape(1, -1)

    def cut(own):
        size = own.shape[0] // GROUP
        return lax.dynamic_slice(own, (me * size, 0), (size, own.shape[1]))

    def spread(piece):
        return [along(piece, k) for k in range(1, blocks)]

    bar = lambda *xs: list(lax.optimization_barrier(tuple(xs)))
    sem = pltpu.SemaphoreType.DMA((blocks, GROUP, 2))
    vec = whole((1, model))
    ptoken = whole((ptokens, model))
    lane = 128
    lse_rows = 8

    tick = [tok]

    def order(*xs):
        tick[0], *out = bar(tick[0], *xs)
        return out

    def plane(base):
        return [across(base, m) for m in (2, 4, 6)]

    def other(xs):
        return [across(x, 1) for x in xs]

    def weight(own, even, core):
        size = own.shape[0] // GROUP
        return Gathered(own, even + core, [[(i, 0, size)] for i in (0, 4, 1, 5, 2, 6, 3, 7)])

    hid = hidden.reshape(tokens, model)
    cot = cotangent.reshape(ptokens, model)
    saved_shapes = [
        sds((blocks, ptokens, local), B16),
        sds((blocks, tokens, 2 * local), B16),
        sds((blocks, ptokens, local), B16),
        sds((blocks, lse_rows, ptokens), F32),
    ]

    def block(shape, first=0, by=1):
        return pl.BlockSpec((1,) + tuple(shape), lambda *i: (first + by * i[-1],) + (0,) * len(shape))

    def saved_specs(first):
        return [block(s.shape[1:], first) for s in saved_shapes]

    tile = vmem((heads, seq, pooled_len), F32)

    def far_first(piece):
        return along(piece, 2)

    def pair(piece, far):
        return jnp.stack([piece, far])

    def foreign(far, near):
        return jnp.stack([near[0], far, near[1]])

    def halves(a, b):
        cut_at = a.shape[1] // 16 * 8
        return cut_at, [b[:, :cut_at], a[:, cut_at:]]

    def halved(own, even, core, cut_at):
        size = own.shape[0] // GROUP
        parts = []
        for j in range(GROUP):
            add = 5 if j & 1 else 0
            if j & 6 == 6:
                parts.append([(3 + add, 0, cut_at), (4 + add, cut_at, size - cut_at)])
            else:
                parts.append([({0: 0, 2: 1, 4: 2}[j & 6] + add, 0, size)])
        return Gathered(own, even + core, parts)

    attn_own = jnp.concatenate([key_weight.T, value_weight.T, query_projection_weight.T], axis=0)
    attn_own, attn_piece = order(attn_own, cut(attn_own))
    attn_parts = spread(attn_piece)
    relative_bias, query_bias, value_bias, up_projection_bias, segments, pooled_segments = order(
        relative_bias, query_bias, value_bias, up_projection_bias, segments, pooled_segments)
    own_bias = jnp.concatenate([query_bias, value_bias]).astype(F32).reshape(1, 1, 2 * local)
    vector = jnp.concatenate(
        [
            relative_bias,
            jnp.pad(own_bias[0], ((0, 0), (0, table_len - 2 * local))),
            jnp.pad(row(up_projection_bias), ((0, 0), (0, table_len - ff))),
        ]
    )
    seg = lax.dynamic_slice(segments, (t_index * rows, 0), (rows, seq)).reshape(rows, seq, 1)
    pseg = lax.dynamic_slice(pooled_segments, (t_index * rows, 0), (rows, pooled_len))
    pseg = pseg.reshape(rows, 1, pooled_len)
    vector, seg, pseg, own_bias = order(vector, seg, pseg, own_bias)
    vector_far = far_first(vector)
    own_out = call(
        partial(own_body, dims),
        (1,),
        [SMEM, whole((tokens, model)), whole(attn_own.shape), block((1, 2 * local)), block((heads, table_len)),
         whole(pseg.shape), whole(seg.shape)],
        [ptoken, ptoken] + saved_specs(0),
        [sds((ptokens, model), F32), sds((ptokens, model), B16)] + saved_shapes,
        [vmem((tokens, 128), F32), tile],
        (tick[0], hid, attn_own, own_bias, relative_bias[None], pseg, seg),
        20,
    )
    pooled, pool_low, saved = own_out[0], own_out[1], list(own_out[2:6])
    saved[3], vector_far, *attn_parts = order(saved[3], vector_far, *attn_parts)

    (attn_base,) = order(jnp.stack(attn_parts))
    attn_even = [attn_base] + plane(attn_base)
    attn_core = [across(attn_base, 1)]
    up_projection_weight, output_projection_weight, vector = order(
        up_projection_weight, output_projection_weight, vector)
    up_own = jnp.concatenate([up_projection_weight, output_projection_weight], axis=0)
    down_own = down_projection_weight
    up_own, up_piece, down_piece, vector_pair = order(up_own, cut(up_own), cut(down_own), pair(vector, vector_far))
    up_far = far_first(up_piece)
    shared_rows = jnp.stack(
        [out_bias, first_gain, first_shift, down_bias, second_gain, second_shift]
    ).astype(F32)
    shared_rows, up_far, *attn_core = order(shared_rows, up_far, *attn_core)
    (up_pair,) = order(pair(up_piece, up_far))
    up_near, vector_near = along(up_pair, 1), along(vector_pair, 1)
    vector_near, *attn_even = order(vector_near, *attn_even)
    attn_core += other(attn_even[1:])
    down_far = far_first(down_piece)
    vectors = jnp.stack([vector, vector_near[0], vector_far, vector_near[1]])
    tables = vectors[:, :heads]
    attn_bias = vectors[:, heads : heads + 1, : 2 * local]
    up_bias = vectors[:, heads + 1 : heads + 2, :ff]
    tables, attn_bias, up_bias = order(tables, attn_bias, up_bias)
    down_far, up_near, *attn_core = order(down_far, up_near, *attn_core)
    attn_w = weight(attn_own, attn_even, attn_core)
    up_base, down_pair = order(foreign(up_far, up_near), pair(down_piece, down_far))
    up_a, up_b, down_near = across(up_base, 2), across(up_base, 4), along(down_pair, 1)
    up_core = [across(up_base, 1)]

    def attend_blocks(saved, which):
        n_in = 7
        return list(call(
            partial(rest_body, dims, attn_w, which),
            (len(which),),
            [SMEM, whole((tokens, model)), ptoken, block((1, 2 * local), which[0]),
             block((heads, table_len), which[0]), whole(pseg.shape), whole(seg.shape)]
            + [ANY] * 4 + [ANY] * attn_w.count(),
            saved_specs(which[0]),
            saved_shapes,
            [vmem((len(which),) + attn_own.shape, B16), tile,
             pltpu.SemaphoreType.DMA((len(which), GROUP, 2))],
            (tick[0], hid, pool_low, attn_bias, tables, pseg, seg, *saved, attn_w.own, *attn_w.arrays),
            24,
            {n_in + i: i for i in range(4)},
        ))

    saved = attend_blocks(saved, (1, 2))
    saved[3], up_a, up_b, down_near, *up_core = order(saved[3], up_a, up_b, down_near, *up_core)
    up_cut, up_halves = halves(up_a, up_b)
    down_base, *up_halves = order(foreign(down_far, down_near), *up_halves)
    up_dx, up_dy = across(up_halves[0], 2), across(up_halves[1], 4)
    down_a, down_b = across(down_base, 2), across(down_base, 4)
    up_core.append(across(up_a, 1))
    (saved[3],) = order(saved[3])
    saved = attend_blocks(saved, (3,))
    saved[3], up_dx, up_dy, *up_core = order(saved[3], up_dx, up_dy, *up_core)
    up_core += other([up_b, up_dx, up_dy])
    down_a, down_b, *up_core = order(down_a, down_b, *up_core)
    down_cut, down_halves = halves(down_a, down_b)
    down_halves = order(*down_halves)
    down_dx, down_dy = across(down_halves[0], 2), across(down_halves[1], 4)
    down_core = other([down_base, down_a, down_b])
    down_dx, down_dy, *down_core = order(down_dx, down_dy, *down_core)
    down_core += other([down_dx, down_dy])
    down_core = order(*down_core)
    up_w = halved(up_own, [up_base, up_a, up_b, up_dx, up_dy], up_core, up_cut)
    down_w = halved(down_own, [down_base, down_a, down_b, down_dx, down_dy], down_core, down_cut)

    phase = lambda n, shape: pl.BlockSpec(
        (1,) + shape,
        lambda p, k: (jnp.where(p < n, 0, jnp.where(p == n, k, blocks - 1)),) + (0,) * len(shape),
    )

    def grad_shape(w):
        return sds((GROUP // 2, blocks, w.rows, model), B16)

    def grad_spec(w, n):
        return pl.BlockSpec(
            (GROUP // 2, 1, w.rows, model),
            lambda p, k: (0, jnp.where(p < n, 0, jnp.where(p == n, k, blocks - 1)), 0, 0),
        )

    (output, grad_first, gctx, up_bias_grad, sums, down_keep, down_send, up_keep, up_send) = call(
        partial(ffn_body, up_w, down_w),
        (4, blocks),
        [SMEM, whole((blocks, ptokens, local)), ptoken, ptoken, whole(shared_rows.shape), phase(1, (1, ff))]
        + [ANY] * (up_w.count() + down_w.count()),
        [ptoken, ptoken, phase(3, (ptokens, local)), phase(2, (1, ff)), whole((8, model)),
         grad_spec(down_w, 2), grad_spec(down_w, 2), grad_spec(up_w, 3), grad_spec(up_w, 3)],
        [sds((ptokens, model), B16), sds((ptokens, model), F32), sds((blocks, ptokens, local), B16),
         sds((blocks, 1, ff), F32), sds((8, model), F32),
         grad_shape(down_w), grad_shape(down_w), grad_shape(up_w), grad_shape(up_w)],
        [vmem((blocks,) + up_own.shape, B16), vmem((blocks,) + down_own.shape, B16),
         vmem((ptokens, model), F32), vmem((ptokens, model), F32), vmem((ptokens, 1), F32),
         vmem((ptokens, model), B16), vmem((ptokens, model), B16),
         vmem((blocks, ptokens, ff), B16), vmem((blocks, ptokens, ff), B16),
         vmem((ff, model), F32), vmem((blocks,) + up_own.shape, B16), sem, sem],
        (tick[0], saved[2], pooled, cot, shared_rows, up_bias, up_w.own, *up_w.arrays, down_w.own, *down_w.arrays),
        60,
    )
    attn_rows = attn_own.shape[0]
    extra_rows = 8 * GROUP

    def attend_back(which):
        by = which[1] - which[0]
        at = lambda shape: block(shape, which[0], by)
        n = len(which)
        piece = (attn_rows + extra_rows) // GROUP
        spec = pl.BlockSpec((GROUP // 2, 1, piece, model), lambda i: (0, i, 0, 0))
        grads = sds((GROUP // 2, n, piece, model), B16)
        return call(
            partial(attend_back_body, dims),
            (n,),
            [SMEM, whole((tokens, model)), ptoken, at((heads, table_len)), whole(pseg.shape), whole(seg.shape)]
            + [at(s.shape[1:]) for s in saved_shapes] + [at((ptokens, local)), at((1, ff)), whole((8, model))],
            [block((ptokens, local)), block((tokens, 2 * local)), spec, spec],
            [sds((n, ptokens, local), B16), sds((n, tokens, 2 * local), B16), grads, grads],
            [tile, tile, vmem((attn_rows, model), F32), vmem((extra_rows, model), F32)],
            (tick[0], hid, pool_low, tables, pseg, seg, *saved, gctx, up_bias_grad, sums),
            32,
        )

    f32 = lambda x: x.astype(F32)

    def halves_out(keep, got):
        total = (f32(keep) + f32(got)).reshape((2, 2) + keep.shape[1:])
        half = total.shape[2] // 2
        a, b = total[:, :, :half], total[:, :, half:]
        return (a[:, 0], b[0]), [a[:, 1].astype(B16), b[1].astype(B16)]

    def halves_more(kept, got):
        a, b = kept[0] + f32(got[0]), kept[1] + f32(got[1])
        return (a[0], b[0]), [a[1].astype(B16), b[1].astype(B16)]

    def wider(x):
        bit = GROUP
        while bit < n_dp:
            x = x + f32(across(x.astype(B16), bit))
            bit *= 2
        return x

    def near_hop(total):
        return (total[0], total[2]), jnp.stack([total[1].astype(B16), total[3].astype(B16)])

    def far_hop(kept, got):
        return kept[0] + f32(got[0]), (kept[1] + f32(got[1])).astype(B16)

    def finish(kept, got):
        return (kept + f32(got)).astype(B16)

    down_got, up_got = across(down_send, 1), across(up_send, 1)
    back_odd = attend_back((3, 1))
    back_odd[0], down_got, up_got = order(back_odd[0], down_got, up_got)
    down_kept, down_out = halves_out(down_keep, down_got)
    down_out = order(*down_out)
    down_got = [across(down_out[0], 2), across(down_out[1], 4)]
    up_kept, up_out = halves_out(up_keep, up_got)
    up_out = order(*up_out)
    up_got = [across(up_out[0], 2), across(up_out[1], 4)]
    odd_got = across(back_odd[3], 1)
    back_even = attend_back((2, 0))
    back_even[0], odd_got, *down_got = order(back_even[0], odd_got, *down_got)
    down_kept, down_out = halves_more(down_kept, down_got)
    down_out = order(*down_out)
    down_got = [across(down_out[0], 4), across(down_out[1], 2)]
    even_got = across(back_even[3], 1)

    orders = ((3, 1), (2, 0))
    backs = [back_odd, back_even]
    hidden_grad = call(
        partial(hidden_back_body, attn_w, orders),
        (1,),
        [SMEM, ptoken] + [ANY] * attn_w.count() + [whole((2, ptokens, local))] * 2
        + [whole((2, tokens, 2 * local))] * 2,
        whole((tokens, model)),
        sds((tokens, model), B16),
        [vmem((blocks,) + attn_own.shape, B16), vmem((tokens, model), F32), vmem((ptokens, model), F32),
         vmem((tokens, 128), F32), sem],
        (tick[0], grad_first, attn_w.own, *attn_w.arrays, *[b[0] for b in backs], *[b[1] for b in backs]),
        40,
    )
    hidden_grad, even_got, *up_got = order(hidden_grad, even_got, *up_got)
    up_kept, up_out = halves_more(up_kept, up_got)
    up_out = order(*up_out)
    up_got = [across(up_out[0], 4), across(up_out[1], 2)]

    def split(keep, got, axis):
        total = (f32(keep) + f32(got)).reshape((2, 2) + keep.shape[1:])
        return (total[:, 0], total[:, 1].astype(B16)) if axis == 2 else (total[0], total[1].astype(B16))

    odd, odd_out = split(back_odd[2], odd_got, 2)
    even, even_out = split(back_even[2], even_got, 4)
    down_got = order(*down_got)
    odd_out, even_out = order(odd_out, even_out)
    odd_got, even_got = across(odd_out, 2), across(even_out, 4)

    def plane_sums(kept, got):
        a, b = wider(kept[0] + f32(got[0])), wider(kept[1] + f32(got[1]))
        return near_hop([a[0], a[1], b[0], b[1]])

    down_kept, down_out = plane_sums(down_kept, down_got)
    (down_out,) = order(down_out)
    down_got = along(down_out, 1)
    (down_got,) = order(down_got)
    down_kept, down_out = far_hop(down_kept, down_got)
    (down_out,) = order(down_out)
    down_got = along(down_out, 2)
    up_got = order(*up_got)
    up_kept, up_out = plane_sums(up_kept, up_got)
    (up_out,) = order(up_out)
    up_got = along(up_out, 1)
    odd_got, even_got = order(odd_got, even_got)
    odd, even = odd + f32(odd_got), even + f32(even_got)
    odd_out, even_out = order(odd[1].astype(B16), even[1].astype(B16))
    odd, even = odd[0], even[0]
    odd_got, even_got = across(odd_out, 4), across(even_out, 2)
    down_got, up_got = order(down_got, up_got)
    up_kept, up_out = far_hop(up_kept, up_got)
    (up_out,) = order(up_out)
    up_got = along(up_out, 2)
    odd_got, even_got = order(odd_got, even_got)
    odd, even = wider(odd + f32(odd_got)), wider(even + f32(even_got))
    attn_kept, attn_out = near_hop([even[1], odd[1], even[0], odd[0]])
    (attn_out,) = order(attn_out)
    attn_got = along(attn_out, 1)
    (up_got,) = order(up_got)
    (ffn_done,) = order(jnp.concatenate([finish(up_kept, up_got), finish(down_kept, down_got)]))
    ffn_even = [ffn_done] + plane(ffn_done)
    (attn_got,) = order(attn_got)
    attn_kept, attn_out = far_hop(attn_kept, attn_got)
    (attn_out,) = order(attn_out)
    attn_got = along(attn_out, 2)
    ffn_even = order(*ffn_even)
    (ffn_stack,) = order(jnp.stack(ffn_even))
    ffn_core = across(ffn_stack, 1)
    (attn_got,) = order(attn_got)
    (attn_done,) = order(finish(attn_kept, attn_got))
    attn_even = [attn_done] + plane(attn_done)
    place = [(0, None), (4, 0), (1, None), (4, 1), (2, None), (4, 2), (3, None), (4, 3)]

    def unpack(body, arrays, outs, scratch):
        return call(
            body, (1,), [SMEM] + [whole(a.shape) for a in arrays], [whole(o) for o in outs],
            [sds(o, F32) for o in outs], [vmem(x, F32) for x in scratch], (tick[0], *arrays), 12,
        )

    (ffn_core,) = order(ffn_core)
    up_weight_gradient, out_grad, down_weight_gradient = unpack(
        partial(unpack_ffn_body, place), ffn_even + [ffn_core], [(model, ff), (local, model), (ff, model)],
        [up_own.shape])
    out_grad, *attn_even = order(out_grad, *attn_even)
    (attn_stack,) = order(jnp.stack(attn_even))
    attn_core = across(attn_stack, 1)
    key_grad, value_grad, query_grad, table_grad, q_bias_grad, v_bias_grad, up_bias_grad, norms = unpack(
        partial(unpack_attention_body, place, heads), attn_even + [attn_core],
        [(local, model)] * 3 + [(heads, table_len), (1, local), (1, local), (1, ff), (6, model)],
        [attn_own.shape, (extra_rows, model)])

    return (
        output.reshape(rows, pooled_len, model),
        hidden_grad.reshape(rows, seq, model),
        query_grad.T,
        q_bias_grad.reshape(-1),
        key_grad.T,
        value_grad.T,
        v_bias_grad.reshape(-1),
        out_grad,
        norms[2],
        table_grad,
        norms[0],
        norms[1],
        up_weight_gradient,
        up_bias_grad.reshape(-1),
        down_weight_gradient,
        norms[5],
        norms[3],
        norms[4],
    )


def solution(mesh):
    placed = (
        P(("dp", "tensor"), None, None),
        P(("dp", "tensor"), None, None),
        P("dp", None),
        P("dp", None),
        P("dp", None),
        P(None, "tensor"),
        P("tensor"),
        P(None, "tensor"),
        P(None, "tensor"),
        P("tensor"),
        P("tensor", None),
        P(),
        P("tensor", None),
        P(),
        P(),
        P(None, "tensor"),
        P("tensor"),
        P("tensor", None),
        P(),
        P(),
        P(),
    )
    return jax.shard_map(
        partial(per_device, mesh.shape["dp"], mesh.shape["tensor"]),
        mesh=mesh,
        in_specs=placed,
        out_specs=(
            P(("dp", "tensor"), None, None),
            P(("dp", "tensor"), None, None),
            P(None, "tensor"),
            P("tensor"),
            P(None, "tensor"),
            P(None, "tensor"),
            P("tensor"),
            P("tensor", None),
            P(),
            P("tensor", None),
            P(),
            P(),
            P(None, "tensor"),
            P("tensor"),
            P("tensor", None),
            P(),
            P(),
            P(),
        ),
        check_vma=False,
    )
```

```python
from functools import partial

import jax
import jax.numpy as jnp
from jax import lax
from jax.experimental import pallas as pl
from jax.experimental.pallas import tpu as pltpu
from jax.sharding import PartitionSpec as P

EPSILON = 1e-05
MASKED_SCORE = -1000000000.0
GROUP = 8
F32 = jnp.float32
B16 = jnp.bfloat16


def nn(a, b):
    return lax.dot_general(a, b, (((1,), (0,)), ((), ())), preferred_element_type=F32)


def nt(a, b):
    return lax.dot_general(a, b, (((1,), (1,)), ((), ())), preferred_element_type=F32)


def tn(a, b):
    return lax.dot_general(a, b, (((0,), (0,)), ((), ())), preferred_element_type=F32)


def vmem(shape, dtype):
    return pltpu.VMEM(shape, dtype)


ANY = pl.BlockSpec(memory_space=pl.ANY)
SMEM = pl.BlockSpec(memory_space=pltpu.SMEM)


def whole(shape):
    zeros = (0,) * len(shape)
    return pl.BlockSpec(shape, lambda *_: zeros)


def call(body, grid, in_specs, out_specs, out_shape, scratch, args, limit, aliases=None):
    out = pl.pallas_call(
        body,
        grid=grid,
        in_specs=in_specs,
        out_specs=out_specs,
        out_shape=out_shape,
        scratch_shapes=scratch,
        input_output_aliases=aliases or {},
        compiler_params=pltpu.CompilerParams(
            vmem_limit_bytes=limit << 20, dimension_semantics=("arbitrary",) * len(grid)
        ),
        cost_estimate=pl.CostEstimate(flops=10 << 30, bytes_accessed=20 << 20, transcendentals=0),
    )(*args)
    return list(out) if isinstance(out, (list, tuple)) else out


class Gathered:
    def __init__(self, own, arrays, parts):
        self.own, self.arrays, self.parts = own, arrays, parts
        self.rows = own.shape[0] // GROUP

    def count(self):
        return 1 + len(self.arrays)

    def copies(self, refs, block, slot, held, sems, me):
        if block == 0:
            return [pltpu.make_async_copy(refs[0], held.at[slot], sems.at[slot, 0, 0])]
        out = []
        for j, parts in enumerate(self.parts):
            for i, (which, first, count) in enumerate(parts):
                start = pl.multiple_of((me ^ j) * self.rows + first, 8)
                out.append(pltpu.make_async_copy(
                    refs[1 + which].at[block - 1], held.at[slot, pl.ds(start, count)], sems.at[slot, j, i]))
        return out

    def start(self, refs, blocks, held, sems, me):
        for slot, block in enumerate(blocks):
            for c in self.copies(refs, block, slot, held, sems, me):
                c.start()

    def wait(self, refs, blocks, held, sems, me, step):
        for slot, block in enumerate(blocks):

            @pl.when(step == slot)
            def _(slot=slot, block=block):
                for c in self.copies(refs, block, slot, held, sems, me):
                    c.wait()


def put_pieces(me, grad, keep, send, rows):
    for j in range(GROUP):
        start = pl.multiple_of((me ^ j) * rows, rows)
        piece = grad[pl.ds(start, rows), :].astype(B16)
        (send if j % 2 else keep)[j // 2, 0] = piece


def norm(residual):
    center = residual - jnp.mean(residual, axis=-1, keepdims=True)
    variance = jnp.mean(center * center, axis=-1, keepdims=True)
    inverse = lax.rsqrt(variance + EPSILON)
    return center * inverse, inverse


def norm_back(upstream, normed, inverse, gain):
    scaled = upstream * gain
    return (
        scaled
        - jnp.mean(scaled, axis=-1, keepdims=True)
        - normed * jnp.mean(scaled * normed, axis=-1, keepdims=True)
    ) * inverse


def column_sum(x):
    return jnp.sum(x, axis=0, keepdims=True)


def bias_tiles(table, tiles):
    heads, seq, pooled = tiles.shape
    for h in range(heads):
        row = jnp.broadcast_to(table[h : h + 1, :], (pooled, table.shape[1]))
        rolled = pltpu.roll(row, table.shape[1] - seq, 1, stride=2, stride_axis=0)
        tiles[h] = rolled[:, :seq].T


def attend(weight, hid, pool, bias, table, segq, segk, q_out, kv_out, ctx_out, lse_out, tiles, dims):
    rows, seq, pooled, heads, width = dims
    local = heads * width
    scale = width ** (-0.5)
    kv_bias = jnp.concatenate([jnp.zeros((1, local), F32), bias[:, local : 2 * local]], axis=1)
    q_bias = bias[:, :local]
    bias_tiles(table, tiles)

    def project(r, carry):
        at = pl.ds(pl.multiple_of(r * seq, seq), seq)
        kv_out[0, at, :] = (nt(hid[at, :], weight[: 2 * local, :]) + kv_bias).astype(B16)
        at = pl.ds(pl.multiple_of(r * pooled, pooled), pooled)
        q_out[0, at, :] = (nt(pool[at, :], weight[2 * local : 3 * local, :]) + q_bias).astype(B16)
        return carry

    lax.fori_loop(0, rows, project, 0)

    for r in range(rows):
        at = slice(r * seq, (r + 1) * seq)
        qat = slice(r * pooled, (r + 1) * pooled)
        allowed = segk[r] == segq[r]
        for h in range(heads):
            lanes = slice(h * width, (h + 1) * width)
            query = (q_out[0, qat, lanes].astype(F32) * scale).astype(B16)
            scores = nt(kv_out[0, at, lanes], query) + tiles[h]
            scores = jnp.where(allowed, scores, MASKED_SCORE)
            top = jnp.max(scores, axis=0, keepdims=True)
            exponent = jnp.exp(scores - top)
            total = jnp.sum(exponent, axis=0, keepdims=True)
            value = kv_out[0, at, local + h * width : local + (h + 1) * width]
            context = tn(value, exponent.astype(B16)) * (1.0 / total)
            ctx_out[0, qat, lanes] = context.T.astype(B16)
            lse_out[0, h : h + 1, qat] = top + jnp.log(total)


def own_body(dims, me_ref, hidden, weight, bias, table, segq, segk,
             pooled_out, pool_low, q_out, kv_out, ctx_out, lse_out, wide, tiles):
    rows, seq, pooled, heads, width = dims
    n = rows * pooled
    for c in range(0, hidden.shape[1], 128):
        wide[...] = hidden[:, c : c + 128].astype(F32)
        mean = 0.5 * (wide[pl.ds(0, n, stride=2), :] + wide[pl.ds(1, n, stride=2), :])
        pooled_out[:, c : c + 128] = mean
        pool_low[:, c : c + 128] = mean.astype(B16)
    attend(weight, hidden, pool_low, bias[0], table.at[0], segq, segk,
           q_out, kv_out, ctx_out, lse_out, tiles, dims)


def rest_body(dims, gathered, blocks, me_ref, hidden, pool_low, bias, table, segq, segk,
              q_in, kv_in, ctx_in, lse_in, *refs):
    sources = refs[: gathered.count()]
    q_out, kv_out, ctx_out, lse_out, held, tiles, sems = refs[gathered.count() :]
    step = pl.program_id(0)
    me = me_ref[0]

    @pl.when(step == 0)
    def _():
        gathered.start(sources, blocks, held, sems, me)

    gathered.wait(sources, blocks, held, sems, me, step)
    attend(held.at[step], hidden, pool_low, bias[0], table.at[0], segq, segk,
           q_out, kv_out, ctx_out, lse_out, tiles, dims)


def ffn_body(up_w, down_w, me_ref, ctx, pooled, cot, vectors, bias, *refs):
    n_up, n_down = up_w.count(), down_w.count()
    up_refs, down_refs = refs[:n_up], refs[n_up : n_up + n_down]
    (output, grad_first, gctx, bias_grad, sums, down_keep, down_send, up_keep, up_send,
     up_held, down_held, total, normed, inverse, low, grad_low, act, slope, grad, up_grad, up_sems, down_sems) = refs[n_up + n_down :]
    phase, step = pl.program_id(0), pl.program_id(1)
    last = pl.num_programs(1) - 1
    blocks = range(up_held.shape[0])
    model = low.shape[1]
    me = me_ref[0]
    out_bias, gain1, shift1, down_bias, gain2, shift2 = [vectors[i : i + 1, :] for i in range(6)]

    @pl.when(phase == 0)
    def _():
        @pl.when(step == 0)
        def _():
            up_w.start(up_refs, blocks, up_held, up_sems, me)
            down_w.start(down_refs, blocks, down_held, down_sems, me)
            total[...] = pooled[...] + out_bias
            sums[...] = jnp.zeros_like(sums)

        up_w.wait(up_refs, blocks, up_held, up_sems, me, step)
        total[...] += nn(ctx[step], up_held[step, model:, :])

        @pl.when(step == last)
        def _():
            n, s = norm(total[...])
            normed[...] = n
            inverse[...] = s
            first = n * gain1 + shift1
            low[...] = first.astype(B16)
            total[...] = first + down_bias

    @pl.when(phase == 1)
    def _():
        chunk = 256
        for c in range(0, up_held.shape[2], chunk):
            pre = nn(low[...], up_held[step, :model, c : c + chunk]) + bias[0][:, c : c + chunk]
            phi = 0.5 * (1.0 + lax.erf(pre * (0.5**0.5)))
            density = jnp.exp(-0.5 * pre * pre) * 0.3989422804014327
            act[step, :, c : c + chunk] = (pre * phi).astype(B16)
            slope[step, :, c : c + chunk] = (phi + pre * density).astype(B16)
        down_w.wait(down_refs, blocks, down_held, down_sems, me, step)
        total[...] += nn(act[step], down_held[step])

        @pl.when(step == last)
        def _():
            n, s = norm(total[...])
            output[...] = (n * gain2 + shift2).astype(B16)
            upstream = cot[...].astype(F32)
            back = norm_back(upstream, n, s, gain2)
            total[...] = back
            sums[3:4, :] = column_sum(upstream * n)
            sums[4:5, :] = column_sum(upstream)
            sums[5:6, :] = column_sum(back)

    @pl.when(phase == 2)
    def _():
        @pl.when(step == 0)
        def _():
            grad_low[...] = total[...].astype(B16)

        grad[...] = tn(act[step], grad_low[...])
        put_pieces(me, grad, down_keep, down_send, down_w.rows)
        value = (nt(grad_low[...], down_held[step]) * slope[step].astype(F32)).astype(B16)
        bias_grad[0] = column_sum(value.astype(F32))
        up_grad[step, :model, :] = tn(low[...], value).astype(B16)
        total[...] += nt(value, up_held[step, :model, :])

        @pl.when(step == last)
        def _():
            upstream = total[...]
            n = normed[...]
            back = norm_back(upstream, n, inverse[...], gain1)
            grad_first[...] = back
            grad_low[...] = back.astype(B16)
            sums[0:1, :] = column_sum(upstream * n)
            sums[1:2, :] = column_sum(upstream)
            sums[2:3, :] = column_sum(back)

    @pl.when(phase == 3)
    def _():
        gctx[0] = nt(grad_low[...], up_held[step, model:, :]).astype(B16)
        up_grad[step, model:, :] = tn(ctx[step], grad_low[...]).astype(B16)
        put_pieces(me, up_grad.at[step], up_keep, up_send, up_w.rows)


def diagonal_sums(tile, seq, table_len):
    rows = tile.shape[0]
    x = jnp.concatenate([jnp.zeros((rows, table_len - seq), F32), tile], axis=1)
    while rows > 8:
        half = rows // 2
        x = x[:half] + pltpu.roll(x[half:], table_len - 2 * half, 1)
        rows = half
    out = x[0:1]
    for i in range(1, rows):
        out = out + pltpu.roll(x, table_len - 2 * i, 1)[i : i + 1]
    return out


def attend_back_body(dims, skip, me_ref, hidden, pool_low, table, segq, segk, q_in, kv_in, ctx_in, lse_in, gctx,
                     up_bias_grad, sums, *refs):
    rows, seq, pooled, heads, width = dims
    local = heads * width
    scale = width ** (-0.5)
    me = me_ref[0]
    model = hidden.shape[1]
    dq_out, dkv_out, keep, send, tiles, tile_grad, grad, extra = refs[skip:]
    bias_tiles(table.at[0], tiles)
    product = gctx[0].astype(F32) * ctx_in[0].astype(F32)
    high = product.astype(B16)
    rest = (product - high.astype(F32)).astype(B16)
    line = lax.broadcasted_iota(jnp.int32, (8, local), 0)
    col = lax.broadcasted_iota(jnp.int32, (8, local), 1)
    pick = ((col >= line * width) & (col < (line + 1) * width)).astype(F32).astype(B16)
    inner = nt(pick, high) + nt(pick, rest)

    for r in range(rows):
        at = slice(r * seq, (r + 1) * seq)
        qat = slice(r * pooled, (r + 1) * pooled)
        allowed = segk[r] == segq[r]
        for h in range(heads):
            lanes = slice(h * width, (h + 1) * width)
            vlanes = slice(local + h * width, local + (h + 1) * width)
            query = (q_in[0, qat, lanes].astype(F32) * scale).astype(B16)
            key = kv_in[0, at, lanes]
            scores = nt(key, query) + tiles[h]
            scores = jnp.where(allowed, scores, MASKED_SCORE)
            prob = jnp.exp(scores - lse_in[0, h : h + 1, qat])
            upstream = gctx[0, qat, lanes]
            gprob = nt(kv_in[0, at, vlanes], upstream)
            gscore = (prob * (gprob - inner[h : h + 1, qat])).astype(B16)
            if r == 0:
                tile_grad[h] = gscore.astype(F32)
            else:
                tile_grad[h] += gscore.astype(F32)
            dkv_out[0, at, vlanes] = nn(prob.astype(B16), upstream).astype(B16)
            dkv_out[0, at, lanes] = nn(gscore, query).astype(B16)
            dq_out[0, qat, lanes] = (tn(key, gscore) * scale).T.astype(B16)

    table_len = table.shape[2]
    extra[...] = jnp.zeros_like(extra)
    for h in range(heads):
        line = diagonal_sums(tile_grad[h].T, seq, table_len)
        for i, at in enumerate(range(0, table_len, model)):
            size = min(model, table_len - at)
            extra[lines_of(table_len, model) * h + i : lines_of(table_len, model) * h + i + 1, :size] = line[:, at : at + size]
    at = lines_of(table_len, model) * heads
    extra[at : at + 1, :local] = column_sum(dq_out[0].astype(F32))
    extra[at + 1 : at + 2, :local] = column_sum(dkv_out[0, :, local:].astype(F32))
    extra[at + 2 : at + 3, : up_bias_grad.shape[2]] = up_bias_grad[0]
    extra[at + 3 : at + 9, :] = sums[:6, :]
    grad[: 2 * local, :] = tn(dkv_out[0], hidden[...])
    grad[2 * local :, :] = tn(dq_out[0], pool_low[...])
    rows = grad.shape[0] // GROUP
    lines = extra.shape[0] // GROUP
    for j in range(GROUP):
        owner = me ^ j
        out = send if j % 2 else keep
        out[j // 2, 0, :rows] = grad[pl.ds(pl.multiple_of(owner * rows, 8), rows), :].astype(B16)
        out[j // 2, 0, rows:] = extra[pl.ds(pl.multiple_of(owner * lines, 8), lines), :].astype(B16)


def lines_of(length, width):
    return -(-length // width)


def hidden_back_body(gathered, orders, me_ref, grad_first, *refs):
    sources = refs[: gathered.count()]
    rest = refs[gathered.count() :]
    n = len(orders)
    dqs, dkvs = rest[:n], rest[n : 2 * n]
    hidden_grad, held, htotal, ptotal, wide, sems = rest[2 * n :]
    me = me_ref[0]
    local = dqs[0].shape[2]
    order = [b for o in orders for b in o]
    gathered.start(sources, order, held, sems, me)
    ptotal[...] = grad_first[...]
    slot = 0
    for i, o in enumerate(orders):
        for at, block in enumerate(o):
            for c in gathered.copies(sources, block, slot, held, sems, me):
                c.wait()
            product = nn(dkvs[i][at], held[slot, : 2 * local, :])
            if slot == 0:
                htotal[...] = product
            else:
                htotal[...] += product
            ptotal[...] += nn(dqs[i][at], held[slot, 2 * local :, :])
            slot += 1
    m = ptotal.shape[0]
    for c in range(0, ptotal.shape[1], 128):
        half = 0.5 * ptotal[:, c : c + 128]
        wide[pl.ds(0, m, stride=2), :] = half
        wide[pl.ds(1, m, stride=2), :] = half
        hidden_grad[:, c : c + 128] = (htotal[:, c : c + 128] + wide[...]).astype(B16)


def take(refs, where):
    which, lead = where
    return refs[which][...] if lead is None else refs[which][lead]


def unpack_ffn_body(where, me_ref, *refs):
    n = max(w for w, _ in where) + 1
    up, out, down, total = refs[n:]
    rows, down_rows = total.shape[0] // GROUP, down.shape[0] // GROUP
    for j in range(GROUP):
        piece = take(refs, where[j]).astype(F32)
        owner = me_ref[0] ^ j
        total[pl.ds(pl.multiple_of(owner * rows, 8), rows), :] = piece[:rows]
        down[pl.ds(pl.multiple_of(owner * down_rows, 8), down_rows), :] = piece[rows:]
    up[...] = total[: up.shape[0], :]
    out[...] = total[up.shape[0] :, :]


def unpack_attention_body(where, heads, me_ref, *refs):
    n = max(w for w, _ in where) + 1
    weights, table, q_bias, v_bias, up_bias, norms, total, extra = refs[n : n + 3], *refs[n + 3 :]
    rows = total.shape[0] // GROUP
    lines = extra.shape[0] // GROUP
    for j in range(GROUP):
        piece = take(refs, where[j]).astype(F32)
        owner = me_ref[0] ^ j
        total[pl.ds(pl.multiple_of(owner * rows, 8), rows), :] = piece[:rows]
        extra[pl.ds(pl.multiple_of(owner * lines, 8), lines), :] = piece[rows:]
    local, model = weights[0].shape
    for i, out in enumerate(weights):
        out[...] = total[i * local : (i + 1) * local, :]
    table_len = table.shape[1]
    per = lines_of(table_len, model)
    for h in range(heads):
        for i, at in enumerate(range(0, table_len, model)):
            size = min(model, table_len - at)
            table[h : h + 1, at : at + size] = extra[per * h + i : per * h + i + 1, :size]
    at = per * heads
    q_bias[...] = extra[at : at + 1, :local]
    v_bias[...] = extra[at + 1 : at + 2, :local]
    up_bias[...] = extra[at + 2 : at + 3, : up_bias.shape[1]]
    norms[...] = extra[at + 3 : at + 9, :]


def per_device(n_dp, n_t, hidden, cotangent, segments, pooled_segments, positions,
               query_projection_weight, query_bias, key_weight, value_weight, value_bias,
               output_projection_weight, out_bias, relative_bias, first_gain, first_shift,
               up_projection_weight, up_projection_bias, down_projection_weight, down_bias,
               second_gain, second_shift):
    rows, seq, model = hidden.shape
    pooled_len = seq // 2
    heads, table_len = relative_bias.shape
    width = query_projection_weight.shape[1] // heads
    local = heads * width
    ff = up_projection_weight.shape[1]
    dims = (rows, seq, pooled_len, heads, width)
    tokens, ptokens = rows * seq, rows * pooled_len
    blocks = n_t
    sds = jax.ShapeDtypeStruct
    t_index = lax.axis_index("tensor")
    me = lax.axis_index("dp") % GROUP
    tok = me.astype(jnp.int32).reshape(1)

    def across(x, mask):
        return lax.ppermute(x, "dp", [(i, i ^ mask) for i in range(n_dp)])

    def along(x, mask):
        return lax.ppermute(x, "tensor", [(i, i ^ mask) for i in range(n_t)])

    def row(v):
        return v.astype(F32).reshape(1, -1)

    def cut(own):
        size = own.shape[0] // GROUP
        return lax.dynamic_slice(own, (me * size, 0), (size, own.shape[1]))

    def spread(piece):
        return [along(piece, k) for k in range(1, blocks)]

    bar = lambda *xs: list(lax.optimization_barrier(tuple(xs)))
    sem = pltpu.SemaphoreType.DMA((blocks, GROUP, 2))
    vec = whole((1, model))
    ptoken = whole((ptokens, model))
    lane = 128
    lse_rows = 8

    tick = [tok]

    def order(*xs):
        tick[0], *out = bar(tick[0], *xs)
        return out

    def plane(base):
        return [across(base, m) for m in (2, 4, 6)]

    def other(xs):
        return [across(x, 1) for x in xs]

    def weight(own, even, core):
        size = own.shape[0] // GROUP
        return Gathered(own, even + core, [[(i, 0, size)] for i in (0, 4, 1, 5, 2, 6, 3, 7)])

    hid = hidden.reshape(tokens, model)
    cot = cotangent.reshape(ptokens, model)
    saved_shapes = [
        sds((blocks, ptokens, local), B16),
        sds((blocks, tokens, 2 * local), B16),
        sds((blocks, ptokens, local), B16),
        sds((blocks, lse_rows, ptokens), F32),
    ]

    def block(shape, first=0, by=1):
        return pl.BlockSpec((1,) + tuple(shape), lambda *i: (first + by * i[-1],) + (0,) * len(shape))

    def saved_specs(first):
        return [block(s.shape[1:], first) for s in saved_shapes]

    tile = vmem((heads, seq, pooled_len), F32)

    def far_first(piece):
        return along(piece, 2)

    def pair(piece, far):
        return jnp.stack([piece, far])

    def foreign(far, near):
        return jnp.stack([near[0], far, near[1]])

    def halves(a, b):
        cut_at = a.shape[1] // 16 * 8
        return cut_at, [b[:, :cut_at], a[:, cut_at:]]

    def halved(own, even, core, cut_at):
        size = own.shape[0] // GROUP
        parts = []
        for j in range(GROUP):
            add = 5 if j & 1 else 0
            if j & 6 == 6:
                parts.append([(3 + add, 0, cut_at), (4 + add, cut_at, size - cut_at)])
            else:
                parts.append([({0: 0, 2: 1, 4: 2}[j & 6] + add, 0, size)])
        return Gathered(own, even + core, parts)

    attn_own = jnp.concatenate([key_weight.T, value_weight.T, query_projection_weight.T], axis=0)
    attn_own, attn_piece = order(attn_own, cut(attn_own))
    attn_parts = spread(attn_piece)
    relative_bias, query_bias, value_bias, up_projection_bias, segments, pooled_segments = order(
        relative_bias, query_bias, value_bias, up_projection_bias, segments, pooled_segments)
    own_bias = jnp.concatenate([query_bias, value_bias]).astype(F32).reshape(1, 1, 2 * local)
    seg = lax.dynamic_slice(segments, (t_index * rows, 0), (rows, seq)).reshape(rows, seq, 1)
    pseg = lax.dynamic_slice(pooled_segments, (t_index * rows, 0), (rows, pooled_len))
    pseg = pseg.reshape(rows, 1, pooled_len)
    seg, pseg, own_bias = order(seg, pseg, own_bias)
    own_out = call(
        partial(own_body, dims),
        (1,),
        [SMEM, whole((tokens, model)), whole(attn_own.shape), block((1, 2 * local)), block((heads, table_len)),
         whole(pseg.shape), whole(seg.shape)],
        [ptoken, ptoken] + saved_specs(0),
        [sds((ptokens, model), F32), sds((ptokens, model), B16)] + saved_shapes,
        [vmem((tokens, 128), F32), tile],
        (tick[0], hid, attn_own, own_bias, relative_bias[None], pseg, seg),
        20,
    )
    pooled, pool_low, saved = own_out[0], own_out[1], list(own_out[2:6])
    saved[3], up_projection_weight, output_projection_weight, down_projection_weight, *attn_parts = order(
        saved[3], up_projection_weight, output_projection_weight, down_projection_weight, *attn_parts)

    (attn_base,) = order(jnp.stack(attn_parts))
    attn_even = [attn_base] + plane(attn_base)
    attn_core = [across(attn_base, 1)]
    up_own = jnp.concatenate([up_projection_weight, output_projection_weight], axis=0)
    up_own, up_piece = order(up_own, cut(up_own))
    up_far = far_first(up_piece)
    down_own = down_projection_weight
    vector = jnp.concatenate(
        [
            relative_bias,
            jnp.pad(own_bias[0], ((0, 0), (0, table_len - 2 * local))),
            jnp.pad(row(up_projection_bias), ((0, 0), (0, table_len - ff))),
        ]
    )
    vector, down_piece, *attn_core = order(vector, cut(down_own), *attn_core)
    vector_far = far_first(vector)
    (up_far,) = order(up_far)
    (up_pair,) = order(pair(up_piece, up_far))
    up_near = along(up_pair, 1)
    (vector_far,) = order(vector_far)
    (vector_pair,) = order(pair(vector, vector_far))
    vector_near = along(vector_pair, 1)
    shared_rows = jnp.stack(
        [out_bias, first_gain, first_shift, down_bias, second_gain, second_shift]
    ).astype(F32)
    shared_rows, vector_near = order(shared_rows, vector_near)
    attn_base, *attn_even = order(*attn_even)
    attn_even = [attn_base] + attn_even
    attn_core += other(attn_even[1:])
    (down_piece,) = order(down_piece)
    down_far = far_first(down_piece)
    vectors = jnp.stack([vector, vector_near[0], vector_far, vector_near[1]])
    tables = vectors[:, :heads]
    attn_bias = vectors[:, heads : heads + 1, : 2 * local]
    up_bias = vectors[:, heads + 1 : heads + 2, :ff]
    tables, attn_bias, up_bias, up_near = order(tables, attn_bias, up_bias, up_near)
    attn_core = order(*attn_core)
    attn_w = weight(attn_own, attn_even, attn_core)
    (up_base,) = order(foreign(up_far, up_near))
    up_a, up_b, up_core = across(up_base, 2), across(up_base, 4), [across(up_base, 1)]

    def attend_blocks(saved, which):
        n_in = 7
        return list(call(
            partial(rest_body, dims, attn_w, which),
            (len(which),),
            [SMEM, whole((tokens, model)), ptoken, block((1, 2 * local), which[0]),
             block((heads, table_len), which[0]), whole(pseg.shape), whole(seg.shape)]
            + [ANY] * 4 + [ANY] * attn_w.count(),
            saved_specs(which[0]),
            saved_shapes,
            [vmem((len(which),) + attn_own.shape, B16), tile,
             pltpu.SemaphoreType.DMA((len(which), GROUP, 2))],
            (tick[0], hid, pool_low, attn_bias, tables, pseg, seg, *saved, attn_w.own, *attn_w.arrays),
            24,
            {n_in + i: i for i in range(4)},
        ))

    (down_far,) = order(down_far)
    (down_pair,) = order(pair(down_piece, down_far))
    down_near = along(down_pair, 1)
    saved = attend_blocks(saved, (1, 2))
    saved[3], up_a, up_b, down_near, *up_core = order(saved[3], up_a, up_b, down_near, *up_core)
    up_cut, up_halves = halves(up_a, up_b)
    down_base, *up_halves = order(foreign(down_far, down_near), *up_halves)
    up_dx, up_dy = across(up_halves[0], 2), across(up_halves[1], 4)
    down_a, down_b = across(down_base, 2), across(down_base, 4)
    up_core.append(across(up_a, 1))
    saved = attend_blocks(saved, (3,))
    saved[3], up_dx, up_dy, up_core[1], down_a, down_b = order(
        saved[3], up_dx, up_dy, up_core[1], down_a, down_b)
    down_cut, down_halves = halves(down_a, down_b)
    up_b, down_base, *down_halves = order(up_b, down_base, *down_halves)
    down_dx, down_dy = across(down_halves[0], 2), across(down_halves[1], 4)
    up_core += other([up_b, up_dx, up_dy])
    up_core = order(*up_core)
    down_base, down_a, down_b = order(down_base, down_a, down_b)
    down_core = other([down_base, down_a, down_b])
    down_dx, down_dy, *down_core = order(down_dx, down_dy, *down_core)
    down_core += other([down_dx, down_dy])
    down_core = order(*down_core)
    up_w = halved(up_own, [up_base, up_a, up_b, up_dx, up_dy], up_core, up_cut)
    down_w = halved(down_own, [down_base, down_a, down_b, down_dx, down_dy], down_core, down_cut)

    phase = lambda n, shape: pl.BlockSpec(
        (1,) + shape,
        lambda p, k: (jnp.where(p < n, 0, jnp.where(p == n, k, blocks - 1)),) + (0,) * len(shape),
    )

    def grad_shape(w):
        return sds((GROUP // 2, blocks, w.rows, model), B16)

    def grad_spec(w, n):
        return pl.BlockSpec(
            (GROUP // 2, 1, w.rows, model),
            lambda p, k: (0, jnp.where(p < n, 0, jnp.where(p == n, k, blocks - 1)), 0, 0),
        )

    (output, grad_first, gctx, up_bias_grad, sums, down_keep, down_send, up_keep, up_send) = call(
        partial(ffn_body, up_w, down_w),
        (4, blocks),
        [SMEM, whole((blocks, ptokens, local)), ptoken, ptoken, whole(shared_rows.shape), phase(1, (1, ff))]
        + [ANY] * (up_w.count() + down_w.count()),
        [ptoken, ptoken, phase(3, (ptokens, local)), phase(2, (1, ff)), whole((8, model)),
         grad_spec(down_w, 2), grad_spec(down_w, 2), grad_spec(up_w, 3), grad_spec(up_w, 3)],
        [sds((ptokens, model), B16), sds((ptokens, model), F32), sds((blocks, ptokens, local), B16),
         sds((blocks, 1, ff), F32), sds((8, model), F32),
         grad_shape(down_w), grad_shape(down_w), grad_shape(up_w), grad_shape(up_w)],
        [vmem((blocks,) + up_own.shape, B16), vmem((blocks,) + down_own.shape, B16),
         vmem((ptokens, model), F32), vmem((ptokens, model), F32), vmem((ptokens, 1), F32),
         vmem((ptokens, model), B16), vmem((ptokens, model), B16),
         vmem((blocks, ptokens, ff), B16), vmem((blocks, ptokens, ff), B16),
         vmem((ff, model), F32), vmem((blocks,) + up_own.shape, B16), sem, sem],
        (tick[0], saved[2], pooled, cot, shared_rows, up_bias, up_w.own, *up_w.arrays, down_w.own, *down_w.arrays),
        60,
    )
    attn_rows = attn_own.shape[0]
    extra_rows = 8 * GROUP

    def attend_back(which, slots, into=None):
        by = which[1] - which[0] if len(which) > 1 else 0
        at = lambda shape: block(shape, which[0], by)
        first, n = slots
        piece = (attn_rows + extra_rows) // GROUP
        spec = pl.BlockSpec((GROUP // 2, 1, piece, model), lambda i: (0, first + i, 0, 0))
        grads = sds((GROUP // 2, n, piece, model), B16)
        n_in = 12
        return call(
            partial(attend_back_body, dims, 4 if into else 0),
            (len(which),),
            [SMEM, whole((tokens, model)), ptoken, at((heads, table_len)), whole(pseg.shape), whole(seg.shape)]
            + [at(s.shape[1:]) for s in saved_shapes]
            + [at((ptokens, local)), at((1, ff)), whole((8, model))] + ([ANY] * 4 if into else []),
            [block((ptokens, local), first), block((tokens, 2 * local), first), spec, spec],
            [sds((n, ptokens, local), B16), sds((n, tokens, 2 * local), B16), grads, grads],
            [tile, tile, vmem((attn_rows, model), F32), vmem((extra_rows, model), F32)],
            (tick[0], hid, pool_low, tables, pseg, seg, *saved, gctx, up_bias_grad, sums, *(into or ())),
            32,
            {13 + i: i for i in range(4)} if into else None,
        )

    f32 = lambda x: x.astype(F32)

    class Sum:
        def __init__(self, *arrays):
            self.arrays = arrays

        def __getitem__(self, at):
            return Sum(*[a[at] for a in self.arrays])

        def plus(self, *more):
            return Sum(*self.arrays, *more)

        def value(self):
            total = f32(self.arrays[0])
            for a in self.arrays[1:]:
                total = total + f32(a)
            return total

        def low(self):
            return self.value().astype(B16)

    def by_plane(keep, got):
        return Sum(*[a.reshape((2, 2) + a.shape[1:]) for a in (keep, got)])

    def wider(total):
        bit = GROUP
        while bit < n_dp:
            total = total.plus(across(total.low(), bit))
            bit *= 2
        return total

    def go_first(total):
        half = total.arrays[0].shape[2] // 2
        a, b = total[:, :, :half], total[:, :, half:]
        out = order(a[:, 1].low(), b[1].low())
        return (a[:, 0], b[0]), [across(out[0], 2), across(out[1], 4)]

    def go_second(kept, got):
        a, b = kept[0].plus(got[0]), kept[1].plus(got[1])
        out = order(a[1].low(), b[1].low())
        return (a[0], b[0]), [across(out[0], 4), across(out[1], 2)]

    def near_hop(blocks_of):
        (out,) = order(jnp.stack([blocks_of[1].low(), blocks_of[3].low()]))
        return (blocks_of[0], blocks_of[2]), along(out, 1)

    def far_hop(kept, got):
        (out,) = order(kept[1].plus(got[1]).low())
        return kept[0].plus(got[0]), along(out, 2)

    def hop_first(kept):
        a, b = wider(kept[0]), wider(kept[1])
        return near_hop([a[0], a[1], b[0], b[1]])

    gctx, down_send, up_send = order(gctx, down_send, up_send)
    down_got, up_got = across(down_send, 1), across(up_send, 1)
    back = attend_back((3,), (0, 4))
    back[0], down_got = order(back[0], down_got)
    down_kept, down_got = go_first(by_plane(down_keep, down_got))
    back = attend_back((1,), (1, 4), back)
    back[0], up_got = order(back[0], up_got)
    up_kept, up_got = go_first(by_plane(up_keep, up_got))
    back = attend_back((2, 0), (2, 4), back)
    back[0], back[3], *down_got = order(back[0], back[3], *down_got)
    attn_got = across(back[3], 1)
    down_kept, down_got = go_second(down_kept, down_got)
    up_got = order(*up_got)
    (attn_got,) = order(attn_got)
    attn_kept, attn_got = go_first(by_plane(back[2], attn_got))
    down_got = order(*down_got)
    up_kept, up_got = go_second(up_kept, up_got)
    down_kept, down_got = hop_first([k.plus(g) for k, g in zip(down_kept, down_got)])

    hidden_grad = call(
        partial(hidden_back_body, attn_w, ((3, 1, 2, 0),)),
        (1,),
        [SMEM, ptoken] + [ANY] * attn_w.count() + [whole((blocks, ptokens, local)), whole((blocks, tokens, 2 * local))],
        whole((tokens, model)),
        sds((tokens, model), B16),
        [vmem((blocks,) + attn_own.shape, B16), vmem((tokens, model), F32), vmem((ptokens, model), F32),
         vmem((tokens, 128), F32), sem],
        (tick[0], grad_first, attn_w.own, *attn_w.arrays, back[0], back[1]),
        40,
    )
    hidden_grad, down_got, *attn_got = order(hidden_grad, down_got, *attn_got)
    attn_kept, attn_got = go_second(attn_kept, attn_got)
    down_kept, down_got = far_hop(down_kept, down_got)
    up_got = order(*up_got)
    up_kept, up_got = hop_first([k.plus(g) for k, g in zip(up_kept, up_got)])
    (down_got,) = order(down_got)
    (down_done,) = order(down_kept.plus(down_got).low())
    attn_got = order(*attn_got)
    odd, even = wider(attn_kept[0].plus(attn_got[0])), wider(attn_kept[1].plus(attn_got[1]))
    attn_out = order(even[0].low(), odd[0].low(), odd[1].low())
    attn_got = [along(attn_out[0], 2), along(attn_out[1], 3), along(attn_out[2], 1)]
    attn_kept = even[1]
    (up_got,) = order(up_got)
    up_kept, up_got = far_hop(up_kept, up_got)
    attn_got = order(*attn_got)
    (attn_done,) = order(attn_kept.plus(*attn_got).low())
    attn_even = [attn_done] + plane(attn_done)
    (up_got,) = order(up_got)
    (up_done,) = order(up_kept.plus(up_got).low())
    attn_even = order(*attn_even)
    (attn_stack,) = order(jnp.stack(attn_even))
    (ffn_done,) = order(jnp.concatenate([up_done, down_done]))
    attn_core = across(attn_stack, 1)
    ffn_even = [ffn_done] + plane(ffn_done)
    (attn_core,) = order(attn_core)
    place = [(0, None), (4, 0), (1, None), (4, 1), (2, None), (4, 2), (3, None), (4, 3)]

    def unpack(body, arrays, outs, scratch):
        return call(
            body, (1,), [SMEM] + [whole(a.shape) for a in arrays], [whole(o) for o in outs],
            [sds(o, F32) for o in outs], [vmem(x, F32) for x in scratch], (tick[0], *arrays), 12,
        )

    key_grad, value_grad, query_grad, table_grad, q_bias_grad, v_bias_grad, up_bias_grad, norms = unpack(
        partial(unpack_attention_body, place, heads), attn_even + [attn_core],
        [(local, model)] * 3 + [(heads, table_len), (1, local), (1, local), (1, ff), (6, model)],
        [attn_own.shape, (extra_rows, model)])
    norms, *ffn_even = order(norms, *ffn_even)
    (ffn_stack,) = order(jnp.stack(ffn_even))
    ffn_core = across(ffn_stack, 1)
    up_weight_gradient, out_grad, down_weight_gradient = unpack(
        partial(unpack_ffn_body, place), ffn_even + [ffn_core], [(model, ff), (local, model), (ff, model)],
        [up_own.shape])

    return (
        output.reshape(rows, pooled_len, model),
        hidden_grad.reshape(rows, seq, model),
        query_grad.T,
        q_bias_grad.reshape(-1),
        key_grad.T,
        value_grad.T,
        v_bias_grad.reshape(-1),
        out_grad,
        norms[2],
        table_grad,
        norms[0],
        norms[1],
        up_weight_gradient,
        up_bias_grad.reshape(-1),
        down_weight_gradient,
        norms[5],
        norms[3],
        norms[4],
    )


def solution(mesh):
    placed = (
        P(("dp", "tensor"), None, None),
        P(("dp", "tensor"), None, None),
        P("dp", None),
        P("dp", None),
        P("dp", None),
        P(None, "tensor"),
        P("tensor"),
        P(None, "tensor"),
        P(None, "tensor"),
        P("tensor"),
        P("tensor", None),
        P(),
        P("tensor", None),
        P(),
        P(),
        P(None, "tensor"),
        P("tensor"),
        P("tensor", None),
        P(),
        P(),
        P(),
    )
    return jax.shard_map(
        partial(per_device, mesh.shape["dp"], mesh.shape["tensor"]),
        mesh=mesh,
        in_specs=placed,
        out_specs=(
            P(("dp", "tensor"), None, None),
            P(("dp", "tensor"), None, None),
            P(None, "tensor"),
            P("tensor"),
            P(None, "tensor"),
            P(None, "tensor"),
            P("tensor"),
            P("tensor", None),
            P(),
            P("tensor", None),
            P(),
            P(),
            P(None, "tensor"),
            P("tensor"),
            P("tensor", None),
            P(),
            P(),
            P(),
        ),
        check_vma=False,
    )
```

```python
from functools import partial

import jax
import jax.numpy as jnp
from jax import lax
from jax.experimental import pallas as pl
from jax.experimental.pallas import tpu as pltpu
from jax.sharding import PartitionSpec as P

EPSILON = 1e-05
MASKED_SCORE = -1000000000.0
GROUP = 8
F32 = jnp.float32
B16 = jnp.bfloat16


def nn(a, b):
    return lax.dot_general(a, b, (((1,), (0,)), ((), ())), preferred_element_type=F32)


def nt(a, b):
    return lax.dot_general(a, b, (((1,), (1,)), ((), ())), preferred_element_type=F32)


def tn(a, b):
    return lax.dot_general(a, b, (((0,), (0,)), ((), ())), preferred_element_type=F32)


def vmem(shape, dtype):
    return pltpu.VMEM(shape, dtype)


ANY = pl.BlockSpec(memory_space=pl.ANY)
SMEM = pl.BlockSpec(memory_space=pltpu.SMEM)


def whole(shape):
    zeros = (0,) * len(shape)
    return pl.BlockSpec(shape, lambda *_: zeros)


def call(body, grid, in_specs, out_specs, out_shape, scratch, args, limit, aliases=None):
    out = pl.pallas_call(
        body,
        grid=grid,
        in_specs=in_specs,
        out_specs=out_specs,
        out_shape=out_shape,
        scratch_shapes=scratch,
        input_output_aliases=aliases or {},
        compiler_params=pltpu.CompilerParams(
            vmem_limit_bytes=limit << 20, dimension_semantics=("arbitrary",) * len(grid)
        ),
        cost_estimate=pl.CostEstimate(flops=10 << 30, bytes_accessed=20 << 20, transcendentals=0),
    )(*args)
    return list(out) if isinstance(out, (list, tuple)) else out


class Gathered:
    def __init__(self, own, arrays, parts):
        self.own, self.arrays, self.parts = own, arrays, parts
        self.rows = own.shape[0] // GROUP

    def count(self):
        return 1 + len(self.arrays)

    def copies(self, refs, block, slot, held, sems, me):
        if block == 0:
            return [pltpu.make_async_copy(refs[0], held.at[slot], sems.at[slot, 0, 0])]
        out = []
        for j, parts in enumerate(self.parts):
            for i, (which, first, count) in enumerate(parts):
                start = pl.multiple_of((me ^ j) * self.rows + first, 8)
                out.append(pltpu.make_async_copy(
                    refs[1 + which].at[block - 1], held.at[slot, pl.ds(start, count)], sems.at[slot, j, i]))
        return out

    def start(self, refs, blocks, held, sems, me):
        for slot, block in enumerate(blocks):
            for c in self.copies(refs, block, slot, held, sems, me):
                c.start()

    def wait(self, refs, blocks, held, sems, me, step):
        for slot, block in enumerate(blocks):

            @pl.when(step == slot)
            def _(slot=slot, block=block):
                for c in self.copies(refs, block, slot, held, sems, me):
                    c.wait()


def piece_copies(me, grad, keep, send, step, rows, sems):
    out = []
    for j in range(GROUP):
        start = pl.multiple_of((me ^ j) * rows, 8)
        target = (send if j % 2 else keep).at[j // 2, step]
        out.append(pltpu.make_async_copy(grad.at[step, pl.ds(start, rows)], target, sems.at[step, j]))
    return out


def by_rows(count, body, chunk=128):
    def one(i, carry):
        body(pl.ds(pl.multiple_of(i * chunk, chunk), chunk))
        return carry

    lax.fori_loop(0, count // chunk, one, 0)


def norm(residual):
    center = residual - jnp.mean(residual, axis=-1, keepdims=True)
    variance = jnp.mean(center * center, axis=-1, keepdims=True)
    inverse = lax.rsqrt(variance + EPSILON)
    return center * inverse, inverse


def norm_back(upstream, normed, inverse, gain):
    scaled = upstream * gain
    return (
        scaled
        - jnp.mean(scaled, axis=-1, keepdims=True)
        - normed * jnp.mean(scaled * normed, axis=-1, keepdims=True)
    ) * inverse


def column_sum(x):
    return jnp.sum(x, axis=0, keepdims=True)


def bias_tiles(table, tiles):
    heads, seq, pooled = tiles.shape
    for h in range(heads):
        row = jnp.broadcast_to(table[h : h + 1, :], (pooled, table.shape[1]))
        rolled = pltpu.roll(row, table.shape[1] - seq, 1, stride=2, stride_axis=0)
        tiles[h] = rolled[:, :seq].T


def attend(weight, hid, pool, bias, table, segq, segk, q_out, kv_out, ctx_out, lse_out, tiles, dims):
    rows, seq, pooled, heads, width = dims
    local = heads * width
    scale = width ** (-0.5)
    kv_bias = jnp.concatenate([jnp.zeros((1, local), F32), bias[:, local : 2 * local]], axis=1)
    q_bias = bias[:, :local]
    bias_tiles(table, tiles)

    def project(r, carry):
        at = pl.ds(pl.multiple_of(r * seq, seq), seq)
        kv_out[0, at, :] = (nt(hid[at, :], weight[: 2 * local, :]) + kv_bias).astype(B16)
        at = pl.ds(pl.multiple_of(r * pooled, pooled), pooled)
        q_out[0, at, :] = (nt(pool[at, :], weight[2 * local : 3 * local, :]) + q_bias).astype(B16)
        return carry

    lax.fori_loop(0, rows, project, 0)

    for r in range(rows):
        at = slice(r * seq, (r + 1) * seq)
        qat = slice(r * pooled, (r + 1) * pooled)
        allowed = segk[r] == segq[r]
        for h in range(heads):
            lanes = slice(h * width, (h + 1) * width)
            query = (q_out[0, qat, lanes].astype(F32) * scale).astype(B16)
            scores = nt(kv_out[0, at, lanes], query) + tiles[h]
            scores = jnp.where(allowed, scores, MASKED_SCORE)
            top = jnp.max(scores, axis=0, keepdims=True)
            exponent = jnp.exp(scores - top)
            total = jnp.sum(exponent, axis=0, keepdims=True)
            value = kv_out[0, at, local + h * width : local + (h + 1) * width]
            context = tn(value, exponent.astype(B16)) * (1.0 / total)
            ctx_out[0, qat, lanes] = context.T.astype(B16)
            lse_out[0, h : h + 1, qat] = top + jnp.log(total)


def own_body(dims, me_ref, hidden, weight, bias, table, segq, segk,
             pooled_out, pool_low, q_out, kv_out, ctx_out, lse_out, wide, tiles):
    rows, seq, pooled, heads, width = dims
    n = rows * pooled

    def one(i, carry):
        at = pl.ds(pl.multiple_of(i * 128, 128), 128)
        wide[...] = hidden[:, at].astype(F32)
        mean = 0.5 * (wide[pl.ds(0, n, stride=2), :] + wide[pl.ds(1, n, stride=2), :])
        pooled_out[:, at] = mean
        pool_low[:, at] = mean.astype(B16)
        return carry

    lax.fori_loop(0, hidden.shape[1] // 128, one, 0)
    attend(weight, hidden, pool_low, bias[0], table.at[0], segq, segk,
           q_out, kv_out, ctx_out, lse_out, tiles, dims)


def rest_body(dims, gathered, blocks, me_ref, hidden, pool_low, bias, table, segq, segk,
              q_in, kv_in, ctx_in, lse_in, *refs):
    sources = refs[: gathered.count()]
    q_out, kv_out, ctx_out, lse_out, held, tiles, sems = refs[gathered.count() :]
    step = pl.program_id(0)
    me = me_ref[0]

    @pl.when(step == 0)
    def _():
        gathered.start(sources, blocks, held, sems, me)

    gathered.wait(sources, blocks, held, sems, me, step)
    attend(held.at[step], hidden, pool_low, bias[0], table.at[0], segq, segk,
           q_out, kv_out, ctx_out, lse_out, tiles, dims)


def up_body(up_w, me_ref, ctx, pooled, vectors, bias, *refs):
    up_refs = refs[: up_w.count()]
    normed, inverse, low, act, slope, held, total, sems = refs[up_w.count() :]
    phase, step = pl.program_id(0), pl.program_id(1)
    blocks = range(held.shape[0])
    model = low.shape[1]
    me = me_ref[0]
    out_bias, gain, shift = [vectors[i : i + 1, :] for i in range(3)]

    @pl.when(phase == 0)
    def _():
        @pl.when(step == 0)
        def _():
            up_w.start(up_refs, blocks, held, sems, me)
            total[...] = pooled[...] + out_bias

        up_w.wait(up_refs, blocks, held, sems, me, step)
        total[...] += nn(ctx[step], held[step, model:, :])

        @pl.when(step == pl.num_programs(1) - 1)
        def _():
            def one(at):
                n, s = norm(total[at, :])
                normed[at, :] = n
                inverse[at, :] = s
                low[at, :] = (n * gain + shift).astype(B16)

            by_rows(total.shape[0], one)

    @pl.when(phase == 1)
    def _():
        chunk = 256

        def one(i, carry):
            at = pl.ds(pl.multiple_of(i * chunk, chunk), chunk)
            pre = nn(low[...], held[step, :model, at]) + bias[0, :, at]
            phi = 0.5 * (1.0 + lax.erf(pre * (0.5**0.5)))
            density = jnp.exp(-0.5 * pre * pre) * 0.3989422804014327
            act[0, :, at] = (pre * phi).astype(B16)
            slope[0, :, at] = (phi + pre * density).astype(B16)
            return carry

        lax.fori_loop(0, held.shape[2] // chunk, one, 0)


def ffn_body(up_w, down_w, me_ref, act, slope, ctx, normed, inverse, low, cot, vectors, *refs):
    n_up, n_down = up_w.count(), down_w.count()
    up_refs, down_refs = refs[:n_up], refs[n_up : n_up + n_down]
    (output, grad_first, gctx, bias_grad, sums, down_keep, down_send, up_keep, up_send,
     up_held, down_held, total, grad_low, down_grad, up_grad, up_sems, down_sems, down_out, up_out) = refs[n_up + n_down :]
    phase, step = pl.program_id(0), pl.program_id(1)
    last = pl.num_programs(1) - 1
    blocks = range(up_held.shape[0])
    model = low.shape[1]
    count = low.shape[0]
    me = me_ref[0]
    _, gain1, shift1, down_bias, gain2, shift2 = [vectors[i : i + 1, :] for i in range(6)]

    def down_copies(k):
        return piece_copies(me, down_grad, down_keep, down_send, k, down_w.rows, down_out)

    def up_copies(k):
        return piece_copies(me, up_grad, up_keep, up_send, k, up_w.rows, up_out)

    @pl.when(phase == 0)
    def _():
        @pl.when(step == 0)
        def _():
            down_w.start(down_refs, blocks, down_held, down_sems, me)
            up_w.start(up_refs, blocks, up_held, up_sems, me)
            total[...] = normed[...] * gain1 + shift1 + down_bias
            sums[...] = jnp.zeros_like(sums)

        down_w.wait(down_refs, blocks, down_held, down_sems, me, step)
        total[...] += nn(act[0], down_held[step])

        @pl.when(step == last)
        def _():
            def one(at):
                n, s = norm(total[at, :])
                output[at, :] = (n * gain2 + shift2).astype(B16)
                upstream = cot[at, :].astype(F32)
                back = norm_back(upstream, n, s, gain2)
                total[at, :] = back
                grad_low[at, :] = back.astype(B16)
                sums[3:4, :] += column_sum(upstream * n)
                sums[4:5, :] += column_sum(upstream)
                sums[5:6, :] += column_sum(back)

            by_rows(count, one)

    @pl.when(phase == 1)
    def _():
        down_grad[step] = tn(act[0], grad_low[...]).astype(B16)
        for c in down_copies(step):
            c.start()
        value = (nt(grad_low[...], down_held[step]) * slope[0].astype(F32)).astype(B16)
        bias_grad[0] = column_sum(value.astype(F32))
        up_w.wait(up_refs, blocks, up_held, up_sems, me, step)
        up_grad[step, :model, :] = tn(low[...], value).astype(B16)
        for j, c in enumerate(up_copies(step)):
            pl.when(((me ^ j) + 1) * up_w.rows <= model)(c.start)
        total[...] += nt(value, up_held[step, :model, :])

        @pl.when(step == last)
        def _():
            def one(at):
                upstream = total[at, :]
                n = normed[at, :]
                back = norm_back(upstream, n, inverse[at, :], gain1)
                grad_first[at, :] = back
                grad_low[at, :] = back.astype(B16)
                sums[0:1, :] += column_sum(upstream * n)
                sums[1:2, :] += column_sum(upstream)
                sums[2:3, :] += column_sum(back)

            by_rows(count, one)

    @pl.when(phase == 2)
    def _():
        gctx[0] = nt(grad_low[...], up_held[step, model:, :]).astype(B16)
        up_grad[step, model:, :] = tn(ctx[step], grad_low[...]).astype(B16)
        for j, c in enumerate(up_copies(step)):
            pl.when(((me ^ j) + 1) * up_w.rows > model)(c.start)

        @pl.when(step == last)
        def _():
            for k in blocks:
                for c in down_copies(k) + up_copies(k):
                    c.wait()


def diagonal_sums(tile, seq, table_len):
    rows = tile.shape[0]
    x = jnp.concatenate([jnp.zeros((rows, table_len - seq), F32), tile], axis=1)
    while rows > 8:
        half = rows // 2
        x = x[:half] + pltpu.roll(x[half:], table_len - 2 * half, 1)
        rows = half
    out = x[0:1]
    for i in range(1, rows):
        out = out + pltpu.roll(x, table_len - 2 * i, 1)[i : i + 1]
    return out


def attend_back_body(dims, skip, me_ref, hidden, pool_low, table, segq, segk, q_in, kv_in, ctx_in, lse_in, gctx,
                     up_bias_grad, sums, *refs):
    rows, seq, pooled, heads, width = dims
    local = heads * width
    scale = width ** (-0.5)
    me = me_ref[0]
    model = hidden.shape[1]
    dq_out, dkv_out, keep, send, tiles, tile_grad, grad, extra = refs[skip:]
    bias_tiles(table.at[0], tiles)
    product = gctx[0].astype(F32) * ctx_in[0].astype(F32)
    high = product.astype(B16)
    rest = (product - high.astype(F32)).astype(B16)
    line = lax.broadcasted_iota(jnp.int32, (8, local), 0)
    col = lax.broadcasted_iota(jnp.int32, (8, local), 1)
    pick = ((col >= line * width) & (col < (line + 1) * width)).astype(F32).astype(B16)
    inner = nt(pick, high) + nt(pick, rest)

    for r in range(rows):
        at = slice(r * seq, (r + 1) * seq)
        qat = slice(r * pooled, (r + 1) * pooled)
        allowed = segk[r] == segq[r]
        for h in range(heads):
            lanes = slice(h * width, (h + 1) * width)
            vlanes = slice(local + h * width, local + (h + 1) * width)
            query = (q_in[0, qat, lanes].astype(F32) * scale).astype(B16)
            key = kv_in[0, at, lanes]
            scores = nt(key, query) + tiles[h]
            scores = jnp.where(allowed, scores, MASKED_SCORE)
            prob = jnp.exp(scores - lse_in[0, h : h + 1, qat])
            upstream = gctx[0, qat, lanes]
            gprob = nt(kv_in[0, at, vlanes], upstream)
            gscore = (prob * (gprob - inner[h : h + 1, qat])).astype(B16)
            if r == 0:
                tile_grad[h] = gscore.astype(F32)
            else:
                tile_grad[h] += gscore.astype(F32)
            dkv_out[0, at, vlanes] = nn(prob.astype(B16), upstream).astype(B16)
            dkv_out[0, at, lanes] = nn(gscore, query).astype(B16)
            dq_out[0, qat, lanes] = (tn(key, gscore) * scale).T.astype(B16)

    table_len = table.shape[2]
    extra[...] = jnp.zeros_like(extra)
    for h in range(heads):
        line = diagonal_sums(tile_grad[h].T, seq, table_len)
        for i, at in enumerate(range(0, table_len, model)):
            size = min(model, table_len - at)
            extra[lines_of(table_len, model) * h + i : lines_of(table_len, model) * h + i + 1, :size] = line[:, at : at + size]
    at = lines_of(table_len, model) * heads
    extra[at : at + 1, :local] = column_sum(dq_out[0].astype(F32))
    extra[at + 1 : at + 2, :local] = column_sum(dkv_out[0, :, local:].astype(F32))
    extra[at + 2 : at + 3, : up_bias_grad.shape[2]] = up_bias_grad[0]
    extra[at + 3 : at + 9, :] = sums[:6, :]
    grad[: 2 * local, :] = tn(dkv_out[0], hidden[...])
    grad[2 * local :, :] = tn(dq_out[0], pool_low[...])
    rows = grad.shape[0] // GROUP
    lines = extra.shape[0] // GROUP
    for j in range(GROUP):
        owner = me ^ j
        out = send if j % 2 else keep
        out[j // 2, 0, :rows] = grad[pl.ds(pl.multiple_of(owner * rows, 8), rows), :].astype(B16)
        out[j // 2, 0, rows:] = extra[pl.ds(pl.multiple_of(owner * lines, 8), lines), :].astype(B16)


def lines_of(length, width):
    return -(-length // width)


def hidden_back_body(gathered, order, me_ref, grad_first, *refs):
    sources = refs[: gathered.count()]
    dq, dkv, hidden_grad, held, htotal, ptotal, wide, sems = refs[gathered.count() :]
    me = me_ref[0]
    step = pl.program_id(0)
    local = dq.shape[2]

    @pl.when(step == 0)
    def _():
        gathered.start(sources, order, held, sems, me)
        ptotal[...] = grad_first[...]
        htotal[...] = jnp.zeros_like(htotal)

    gathered.wait(sources, order, held, sems, me, step)
    htotal[...] += nn(dkv[0], held[step, : 2 * local, :])
    ptotal[...] += nn(dq[0], held[step, 2 * local :, :])

    @pl.when(step == pl.num_programs(0) - 1)
    def _():
        m = ptotal.shape[0]

        def one(i, carry):
            at = pl.ds(pl.multiple_of(i * 128, 128), 128)
            half = 0.5 * ptotal[:, at]
            wide[pl.ds(0, m, stride=2), :] = half
            wide[pl.ds(1, m, stride=2), :] = half
            hidden_grad[:, at] = (htotal[:, at] + wide[...]).astype(B16)
            return carry

        lax.fori_loop(0, ptotal.shape[1] // 128, one, 0)


def take(refs, where):
    which, lead = where
    return refs[which][...] if lead is None else refs[which][lead]


def unpack_rows_body(where, me_ref, *refs):
    n = max(w for w, _ in where) + 1
    outs, total = refs[n:-1], refs[-1]
    rows = total.shape[0] // GROUP
    for j in range(GROUP):
        total[pl.ds(pl.multiple_of((me_ref[0] ^ j) * rows, 8), rows), :] = take(refs, where[j]).astype(F32)
    at = 0
    for out in outs:
        out[...] = total[at : at + out.shape[0], :]
        at += out.shape[0]


def unpack_attention_body(where, heads, me_ref, *refs):
    n = max(w for w, _ in where) + 1
    weights, table, q_bias, v_bias, up_bias, norms, total, extra = refs[n : n + 3], *refs[n + 3 :]
    rows = total.shape[0] // GROUP
    lines = extra.shape[0] // GROUP
    for j in range(GROUP):
        piece = take(refs, where[j]).astype(F32)
        owner = me_ref[0] ^ j
        total[pl.ds(pl.multiple_of(owner * rows, 8), rows), :] = piece[:rows]
        extra[pl.ds(pl.multiple_of(owner * lines, 8), lines), :] = piece[rows:]
    local, model = weights[0].shape
    for i, out in enumerate(weights):
        out[...] = total[i * local : (i + 1) * local, :]
    table_len = table.shape[1]
    per = lines_of(table_len, model)
    for h in range(heads):
        for i, at in enumerate(range(0, table_len, model)):
            size = min(model, table_len - at)
            table[h : h + 1, at : at + size] = extra[per * h + i : per * h + i + 1, :size]
    at = per * heads
    q_bias[...] = extra[at : at + 1, :local]
    v_bias[...] = extra[at + 1 : at + 2, :local]
    up_bias[...] = extra[at + 2 : at + 3, : up_bias.shape[1]]
    norms[...] = extra[at + 3 : at + 9, :]


def per_device(n_dp, n_t, hidden, cotangent, segments, pooled_segments, positions,
               query_projection_weight, query_bias, key_weight, value_weight, value_bias,
               output_projection_weight, out_bias, relative_bias, first_gain, first_shift,
               up_projection_weight, up_projection_bias, down_projection_weight, down_bias,
               second_gain, second_shift):
    rows, seq, model = hidden.shape
    pooled_len = seq // 2
    heads, table_len = relative_bias.shape
    width = query_projection_weight.shape[1] // heads
    local = heads * width
    ff = up_projection_weight.shape[1]
    dims = (rows, seq, pooled_len, heads, width)
    tokens, ptokens = rows * seq, rows * pooled_len
    blocks = n_t
    sds = jax.ShapeDtypeStruct
    t_index = lax.axis_index("tensor")
    me = lax.axis_index("dp") % GROUP
    tok = me.astype(jnp.int32).reshape(1)

    def across(x, mask):
        return lax.ppermute(x, "dp", [(i, i ^ mask) for i in range(n_dp)])

    def along(x, mask):
        return lax.ppermute(x, "tensor", [(i, i ^ mask) for i in range(n_t)])

    def row(v):
        return v.astype(F32).reshape(1, -1)

    def cut(own):
        size = own.shape[0] // GROUP
        return lax.dynamic_slice(own, (me * size, 0), (size, own.shape[1]))

    def spread(piece):
        return [along(piece, k) for k in range(1, blocks)]

    bar = lambda *xs: list(lax.optimization_barrier(tuple(xs)))
    sem = pltpu.SemaphoreType.DMA((blocks, GROUP, 2))
    vec = whole((1, model))
    ptoken = whole((ptokens, model))
    lane = 128
    lse_rows = 8

    tick = [tok]

    def order(*xs):
        tick[0], *out = bar(tick[0], *xs)
        return out

    def plane(base):
        return [across(base, m) for m in (2, 4, 6)]

    def other(xs):
        return [across(x, 1) for x in xs]

    def weight(own, even, core):
        size = own.shape[0] // GROUP
        return Gathered(own, even + core, [[(i, 0, size)] for i in (0, 4, 1, 5, 2, 6, 3, 7)])

    hid = hidden.reshape(tokens, model)
    cot = cotangent.reshape(ptokens, model)
    saved_shapes = [
        sds((blocks, ptokens, local), B16),
        sds((blocks, tokens, 2 * local), B16),
        sds((blocks, ptokens, local), B16),
        sds((blocks, lse_rows, ptokens), F32),
    ]

    def block(shape, first=0, by=1):
        return pl.BlockSpec((1,) + tuple(shape), lambda *i: (first + by * i[-1],) + (0,) * len(shape))

    def saved_specs(first):
        return [block(s.shape[1:], first) for s in saved_shapes]

    tile = vmem((heads, seq, pooled_len), F32)

    def far_first(piece):
        return along(piece, 2)

    def pair(piece, far):
        return jnp.stack([piece, far])

    def foreign(far, near):
        return jnp.stack([near[0], far, near[1]])

    def halves(a, b):
        cut_at = a.shape[1] // 16 * 8
        return cut_at, [b[:, :cut_at], a[:, cut_at:]]

    def halved(own, even, core, cut_at):
        size = own.shape[0] // GROUP
        parts = []
        for j in range(GROUP):
            add = 5 if j & 1 else 0
            if j & 6 == 6:
                parts.append([(3 + add, 0, cut_at), (4 + add, cut_at, size - cut_at)])
            else:
                parts.append([({0: 0, 2: 1, 4: 2}[j & 6] + add, 0, size)])
        return Gathered(own, even + core, parts)

    attn_own = jnp.concatenate([key_weight.T, value_weight.T, query_projection_weight.T], axis=0)
    attn_own, attn_piece = order(attn_own, cut(attn_own))
    attn_parts = spread(attn_piece)
    relative_bias, query_bias, value_bias, up_projection_bias, segments, pooled_segments = order(
        relative_bias, query_bias, value_bias, up_projection_bias, segments, pooled_segments)
    own_bias = jnp.concatenate([query_bias, value_bias]).astype(F32).reshape(1, 1, 2 * local)
    seg = lax.dynamic_slice(segments, (t_index * rows, 0), (rows, seq)).reshape(rows, seq, 1)
    pseg = lax.dynamic_slice(pooled_segments, (t_index * rows, 0), (rows, pooled_len))
    pseg = pseg.reshape(rows, 1, pooled_len)
    seg, pseg, own_bias = order(seg, pseg, own_bias)
    own_out = call(
        partial(own_body, dims),
        (1,),
        [SMEM, whole((tokens, model)), whole(attn_own.shape), block((1, 2 * local)), block((heads, table_len)),
         whole(pseg.shape), whole(seg.shape)],
        [ptoken, ptoken] + saved_specs(0),
        [sds((ptokens, model), F32), sds((ptokens, model), B16)] + saved_shapes,
        [vmem((tokens, 128), F32), tile],
        (tick[0], hid, attn_own, own_bias, relative_bias[None], pseg, seg),
        20,
    )
    pooled, pool_low, saved = own_out[0], own_out[1], list(own_out[2:6])
    saved[3], up_projection_weight, output_projection_weight, down_projection_weight, *attn_parts = order(
        saved[3], up_projection_weight, output_projection_weight, down_projection_weight, *attn_parts)

    (attn_base,) = order(jnp.stack(attn_parts))
    attn_even = [attn_base] + plane(attn_base)
    attn_core = [across(attn_base, 1)]
    up_own = jnp.concatenate([up_projection_weight, output_projection_weight], axis=0)
    up_own, up_piece = order(up_own, cut(up_own))
    up_far = far_first(up_piece)
    down_own = down_projection_weight
    vector = jnp.concatenate(
        [
            relative_bias,
            jnp.pad(own_bias[0], ((0, 0), (0, table_len - 2 * local))),
            jnp.pad(row(up_projection_bias), ((0, 0), (0, table_len - ff))),
        ]
    )
    vector, down_piece, *attn_core = order(vector, cut(down_own), *attn_core)
    vector_far = far_first(vector)
    (up_far,) = order(up_far)
    (up_pair,) = order(pair(up_piece, up_far))
    up_near = along(up_pair, 1)
    (vector_far,) = order(vector_far)
    (vector_pair,) = order(pair(vector, vector_far))
    vector_near = along(vector_pair, 1)
    shared_rows = jnp.stack(
        [out_bias, first_gain, first_shift, down_bias, second_gain, second_shift]
    ).astype(F32)
    shared_rows, vector_near = order(shared_rows, vector_near)
    attn_base, *attn_even = order(*attn_even)
    attn_even = [attn_base] + attn_even
    attn_core += other(attn_even[1:])
    (down_piece,) = order(down_piece)
    down_far = far_first(down_piece)
    vectors = jnp.stack([vector, vector_near[0], vector_far, vector_near[1]])
    tables = vectors[:, :heads]
    attn_bias = vectors[:, heads : heads + 1, : 2 * local]
    up_bias = vectors[:, heads + 1 : heads + 2, :ff]
    tables, attn_bias, up_bias, up_near = order(tables, attn_bias, up_bias, up_near)
    attn_core = order(*attn_core)
    attn_w = weight(attn_own, attn_even, attn_core)
    (up_base,) = order(foreign(up_far, up_near))
    up_a, up_b, up_core = across(up_base, 2), across(up_base, 4), [across(up_base, 1)]

    def attend_blocks(saved, which):
        n_in = 7
        return list(call(
            partial(rest_body, dims, attn_w, which),
            (len(which),),
            [SMEM, whole((tokens, model)), ptoken, block((1, 2 * local), which[0]),
             block((heads, table_len), which[0]), whole(pseg.shape), whole(seg.shape)]
            + [ANY] * 4 + [ANY] * attn_w.count(),
            saved_specs(which[0]),
            saved_shapes,
            [vmem((len(which),) + attn_own.shape, B16), tile,
             pltpu.SemaphoreType.DMA((len(which), GROUP, 2))],
            (tick[0], hid, pool_low, attn_bias, tables, pseg, seg, *saved, attn_w.own, *attn_w.arrays),
            24,
            {n_in + i: i for i in range(4)},
        ))

    (down_far,) = order(down_far)
    (down_pair,) = order(pair(down_piece, down_far))
    down_near = along(down_pair, 1)
    saved = attend_blocks(saved, (1, 2))
    saved[3], up_a, up_b, down_near, *up_core = order(saved[3], up_a, up_b, down_near, *up_core)
    up_cut, up_halves = halves(up_a, up_b)
    down_base, *up_halves = order(foreign(down_far, down_near), *up_halves)
    up_dx, up_dy = across(up_halves[0], 2), across(up_halves[1], 4)
    down_a, down_b = across(down_base, 2), across(down_base, 4)
    up_core.append(across(up_a, 1))
    saved = attend_blocks(saved, (3,))
    saved[3], up_dx, up_dy, up_core[1], down_a, down_b = order(
        saved[3], up_dx, up_dy, up_core[1], down_a, down_b)
    (up_b,) = order(up_b)
    up_core += other([up_b, up_dx, up_dy])
    down_cut, down_halves = halves(down_a, down_b)
    down_base, *down_halves = order(down_base, *down_halves)
    down_dx, down_dy = across(down_halves[0], 2), across(down_halves[1], 4)
    up_core = order(*up_core)
    up_w = halved(up_own, [up_base, up_a, up_b, up_dx, up_dy], up_core, up_cut)
    down_base, down_a, down_b = order(down_base, down_a, down_b)
    down_core = other([down_base, down_a, down_b])

    phase = lambda n, shape: pl.BlockSpec(
        (1,) + shape,
        lambda p, k: (jnp.where(p < n, 0, jnp.where(p == n, k, blocks - 1)),) + (0,) * len(shape),
    )

    def held_once(shape):
        zeros = (0,) * len(shape)
        return pl.BlockSpec(shape, lambda *_: zeros, pipeline_mode=pl.Buffered(1))

    once = held_once((ptokens, model))
    dims_ff = (blocks, ptokens, ff)
    ctx_spec = held_once((blocks, ptokens, local))
    normed, inverse, low, act, slope = call(
        partial(up_body, up_w),
        (2, blocks),
        [SMEM, ctx_spec, once, whole(shared_rows.shape), phase(1, (1, ff))] + [ANY] * up_w.count(),
        [once, held_once((ptokens, 1)), once, phase(1, (ptokens, ff)), phase(1, (ptokens, ff))],
        [sds((ptokens, model), F32), sds((ptokens, 1), F32), sds((ptokens, model), B16), sds(dims_ff, B16),
         sds(dims_ff, B16)],
        [vmem((blocks,) + up_own.shape, B16), vmem((ptokens, model), F32), sem],
        (tick[0], saved[2], pooled, shared_rows, up_bias, up_w.own, *up_w.arrays),
        60,
    )
    act, down_dx, down_dy, *down_core = order(act, down_dx, down_dy, *down_core)
    down_core += other([down_dx, down_dy])
    down_core = order(*down_core)
    down_w = halved(down_own, [down_base, down_a, down_b, down_dx, down_dy], down_core, down_cut)

    def grad_shape(w):
        return sds((GROUP // 2, blocks, w.rows, model), B16)

    out_sem = pltpu.SemaphoreType.DMA((blocks, GROUP))
    (output, grad_first, gctx, up_bias_grad, sums, down_keep, down_send, up_keep, up_send) = call(
        partial(ffn_body, up_w, down_w),
        (3, blocks),
        [SMEM, pl.BlockSpec((1, ptokens, ff), lambda p, k: (jnp.where(p == 2, blocks - 1, k), 0, 0)),
         phase(1, (ptokens, ff)), ctx_spec, once, held_once((ptokens, 1)), once, once, whole(shared_rows.shape)]
        + [ANY] * (up_w.count() + down_w.count()),
        [once, once, phase(2, (ptokens, local)), phase(1, (1, ff)), whole((8, model)), ANY, ANY, ANY, ANY],
        [sds((ptokens, model), B16), sds((ptokens, model), F32), sds((blocks, ptokens, local), B16),
         sds((blocks, 1, ff), F32), sds((8, model), F32),
         grad_shape(down_w), grad_shape(down_w), grad_shape(up_w), grad_shape(up_w)],
        [vmem((blocks,) + up_own.shape, B16), vmem((blocks,) + down_own.shape, B16),
         vmem((ptokens, model), F32), vmem((ptokens, model), B16), vmem((blocks, ff, model), B16),
         vmem((blocks,) + up_own.shape, B16), sem, sem, out_sem, out_sem],
        (tick[0], act, slope, saved[2], normed, inverse, low, cot, shared_rows,
         up_w.own, *up_w.arrays, down_w.own, *down_w.arrays),
        60,
    )
    attn_rows = attn_own.shape[0]
    extra_rows = 8 * GROUP

    def attend_back(which, slots, into=None):
        by = which[1] - which[0] if len(which) > 1 else 0
        at = lambda shape: block(shape, which[0], by)
        first, n = slots
        piece = (attn_rows + extra_rows) // GROUP
        spec = pl.BlockSpec((GROUP // 2, 1, piece, model), lambda i: (0, first + i, 0, 0))
        grads = sds((GROUP // 2, n, piece, model), B16)
        n_in = 12
        return call(
            partial(attend_back_body, dims, 4 if into else 0),
            (len(which),),
            [SMEM, whole((tokens, model)), ptoken, at((heads, table_len)), whole(pseg.shape), whole(seg.shape)]
            + [at(s.shape[1:]) for s in saved_shapes]
            + [at((ptokens, local)), at((1, ff)), whole((8, model))] + ([ANY] * 4 if into else []),
            [block((ptokens, local), first), block((tokens, 2 * local), first), spec, spec],
            [sds((n, ptokens, local), B16), sds((n, tokens, 2 * local), B16), grads, grads],
            [tile, tile, vmem((attn_rows, model), F32), vmem((extra_rows, model), F32)],
            (tick[0], hid, pool_low, tables, pseg, seg, *saved, gctx, up_bias_grad, sums, *(into or ())),
            32,
            {13 + i: i for i in range(4)} if into else None,
        )

    f32 = lambda x: x.astype(F32)

    class Sum:
        def __init__(self, *arrays):
            self.arrays = arrays

        def __getitem__(self, at):
            return Sum(*[a[at] for a in self.arrays])

        def plus(self, *more):
            return Sum(*self.arrays, *more)

        def value(self):
            total = f32(self.arrays[0])
            for a in self.arrays[1:]:
                total = total + f32(a)
            return total

        def low(self):
            return self.value().astype(B16)

    def by_plane(keep, got):
        return Sum(*[a.reshape((2, 2) + a.shape[1:]) for a in (keep, got)])

    def wider(total):
        bit = GROUP
        while bit < n_dp:
            total = total.plus(across(total.low(), bit))
            bit *= 2
        return total

    def go_first(total):
        half = total.arrays[0].shape[2] // 2
        a, b = total[:, :, :half], total[:, :, half:]
        out = order(a[:, 1].low(), b[1].low())
        return (a[:, 0], b[0]), [across(out[0], 2), across(out[1], 4)]

    def go_second(kept, got):
        a, b = kept[0].plus(got[0]), kept[1].plus(got[1])
        out = order(a[1].low(), b[1].low())
        return (a[0], b[0]), [across(out[0], 4), across(out[1], 2)]

    def near_hop(blocks_of):
        (out,) = order(jnp.stack([blocks_of[1].low(), blocks_of[3].low()]))
        return (blocks_of[0], blocks_of[2]), along(out, 1)

    def far_hop(kept, got):
        (out,) = order(kept[1].plus(got[1]).low())
        return kept[0].plus(got[0]), along(out, 2)

    def hop_first(kept):
        a, b = wider(kept[0]), wider(kept[1])
        return near_hop([a[0], a[1], b[0], b[1]])

    gctx, down_send, up_send = order(gctx, down_send, up_send)
    down_got, up_got = across(down_send, 1), across(up_send, 1)
    (down_got,) = order(down_got)
    down_kept, down_got = go_first(by_plane(down_keep, down_got))
    back = attend_back((3, 1), (0, 4))
    back[0], up_got = order(back[0], up_got)
    up_kept, up_got = go_first(by_plane(up_keep, up_got))
    back = attend_back((2, 0), (2, 4), back)
    back[0], back[3], *got = order(back[0], back[3], *down_got, *up_got)
    down_got, up_got = got[:2], got[2:]
    attn_got = across(back[3], 1)
    down_kept, down_got = go_second(down_kept, down_got)
    up_kept, up_got = go_second(up_kept, up_got)
    (attn_got,) = order(attn_got)
    down_got = order(*down_got)
    attn_kept, attn_got = go_first(by_plane(back[2], attn_got))
    down_kept, down_got = hop_first([k.plus(g) for k, g in zip(down_kept, down_got)])

    hidden_grad = call(
        partial(hidden_back_body, attn_w, (3, 1, 2, 0)),
        (blocks,),
        [SMEM, ptoken] + [ANY] * attn_w.count() + [block((ptokens, local)), block((tokens, 2 * local))],
        whole((tokens, model)),
        sds((tokens, model), B16),
        [vmem((blocks,) + attn_own.shape, B16), vmem((tokens, model), F32), vmem((ptokens, model), F32),
         vmem((tokens, 128), F32), sem],
        (tick[0], grad_first, attn_w.own, *attn_w.arrays, back[0], back[1]),
        28,
    )
    hidden_grad, down_got, *up_got = order(hidden_grad, down_got, *up_got)
    down_kept, down_got = far_hop(down_kept, down_got)
    up_kept, up_got = hop_first([k.plus(g) for k, g in zip(up_kept, up_got)])
    attn_got = order(*attn_got)
    attn_kept, attn_got = go_second(attn_kept, attn_got)
    (down_got,) = order(down_got)
    (down_done,) = order(down_kept.plus(down_got).low())
    down_y = across(down_done, 4)
    (up_got,) = order(up_got)
    up_kept, up_got = far_hop(up_kept, up_got)
    attn_got = order(*attn_got)
    odd, even = wider(attn_kept[0].plus(attn_got[0])), wider(attn_kept[1].plus(attn_got[1]))
    attn_out = order(even[0].low(), odd[0].low(), odd[1].low())
    attn_got = [along(attn_out[0], 2), along(attn_out[1], 3), along(attn_out[2], 1)]
    attn_kept = even[1]
    (down_y,) = order(down_y)
    (down_pair,) = order(jnp.stack([down_done, down_y]))
    down_x = across(down_pair, 2)
    (up_got,) = order(up_got)
    (up_done,) = order(up_kept.plus(up_got).low())
    attn_got = order(*attn_got)
    (attn_done,) = order(attn_kept.plus(*attn_got).low())
    attn_even = [attn_done] + plane(attn_done)
    (down_x,) = order(down_x)
    (down_four,) = order(jnp.concatenate([down_pair, down_x]))
    down_core = across(down_four, 1)
    attn_even = order(*attn_even)
    up_even = [up_done] + plane(order(up_done)[0])
    (attn_stack,) = order(jnp.stack(attn_even))
    attn_core = across(attn_stack, 1)
    (down_core,) = order(down_core)
    down_place = [None] * GROUP
    for i, m in enumerate((0, 4, 2, 6)):
        down_place[m], down_place[m ^ 1] = (0, i), (1, i)
    place = [(0, None), (4, 0), (1, None), (4, 1), (2, None), (4, 2), (3, None), (4, 3)]

    def unpack(body, arrays, outs, scratch):
        return call(
            body, (1,), [SMEM] + [whole(a.shape) for a in arrays], [whole(o) for o in outs],
            [sds(o, F32) for o in outs], [vmem(x, F32) for x in scratch], (tick[0], *arrays), 12,
        )

    (down_weight_gradient,) = unpack(
        partial(unpack_rows_body, down_place), [down_four, down_core], [(ff, model)], [down_own.shape])
    down_weight_gradient, attn_core = order(down_weight_gradient, attn_core)
    key_grad, value_grad, query_grad, table_grad, q_bias_grad, v_bias_grad, up_bias_grad, norms = unpack(
        partial(unpack_attention_body, place, heads), attn_even + [attn_core],
        [(local, model)] * 3 + [(heads, table_len), (1, local), (1, local), (1, ff), (6, model)],
        [attn_own.shape, (extra_rows, model)])
    norms, *up_even = order(norms, *up_even)
    (up_stack,) = order(jnp.stack(up_even))
    up_core = across(up_stack, 1)
    up_weight_gradient, out_grad = unpack(
        partial(unpack_rows_body, place), up_even + [up_core], [(model, ff), (local, model)], [up_own.shape])

    return (
        output.reshape(rows, pooled_len, model),
        hidden_grad.reshape(rows, seq, model),
        query_grad.T,
        q_bias_grad.reshape(-1),
        key_grad.T,
        value_grad.T,
        v_bias_grad.reshape(-1),
        out_grad,
        norms[2],
        table_grad,
        norms[0],
        norms[1],
        up_weight_gradient,
        up_bias_grad.reshape(-1),
        down_weight_gradient,
        norms[5],
        norms[3],
        norms[4],
    )


def solution(mesh):
    placed = (
        P(("dp", "tensor"), None, None),
        P(("dp", "tensor"), None, None),
        P("dp", None),
        P("dp", None),
        P("dp", None),
        P(None, "tensor"),
        P("tensor"),
        P(None, "tensor"),
        P(None, "tensor"),
        P("tensor"),
        P("tensor", None),
        P(),
        P("tensor", None),
        P(),
        P(),
        P(None, "tensor"),
        P("tensor"),
        P("tensor", None),
        P(),
        P(),
        P(),
    )
    return jax.shard_map(
        partial(per_device, mesh.shape["dp"], mesh.shape["tensor"]),
        mesh=mesh,
        in_specs=placed,
        out_specs=(
            P(("dp", "tensor"), None, None),
            P(("dp", "tensor"), None, None),
            P(None, "tensor"),
            P("tensor"),
            P(None, "tensor"),
            P(None, "tensor"),
            P("tensor"),
            P("tensor", None),
            P(),
            P("tensor", None),
            P(),
            P(),
            P(None, "tensor"),
            P("tensor"),
            P("tensor", None),
            P(),
            P(),
            P(),
        ),
        check_vma=False,
    )
```

```python
from functools import partial

import jax
import jax.numpy as jnp
from jax import lax
from jax.experimental import pallas as pl
from jax.experimental.pallas import tpu as pltpu
from jax.sharding import PartitionSpec as P

EPSILON = 1e-05
MASKED_SCORE = -1000000000.0
GROUP = 8
F32 = jnp.float32
B16 = jnp.bfloat16


def nn(a, b):
    return lax.dot_general(a, b, (((1,), (0,)), ((), ())), preferred_element_type=F32)


def nt(a, b):
    return lax.dot_general(a, b, (((1,), (1,)), ((), ())), preferred_element_type=F32)


def tn(a, b):
    return lax.dot_general(a, b, (((0,), (0,)), ((), ())), preferred_element_type=F32)


def vmem(shape, dtype):
    return pltpu.VMEM(shape, dtype)


ANY = pl.BlockSpec(memory_space=pl.ANY)
SMEM = pl.BlockSpec(memory_space=pltpu.SMEM)


def whole(shape):
    zeros = (0,) * len(shape)
    return pl.BlockSpec(shape, lambda *_: zeros)


def call(body, grid, in_specs, out_specs, out_shape, scratch, args, limit, aliases=None):
    out = pl.pallas_call(
        body,
        grid=grid,
        in_specs=in_specs,
        out_specs=out_specs,
        out_shape=out_shape,
        scratch_shapes=scratch,
        input_output_aliases=aliases or {},
        compiler_params=pltpu.CompilerParams(
            vmem_limit_bytes=limit << 20, dimension_semantics=("arbitrary",) * len(grid)
        ),
        cost_estimate=pl.CostEstimate(flops=10 << 30, bytes_accessed=20 << 20, transcendentals=0),
    )(*args)
    return list(out) if isinstance(out, (list, tuple)) else out


class Gathered:
    def __init__(self, own, arrays, parts):
        self.own, self.arrays, self.parts = own, arrays, parts
        self.rows = own.shape[0] // GROUP

    def count(self):
        return 1 + len(self.arrays)

    def copies(self, refs, block, slot, held, sems, me):
        if block == 0:
            return [pltpu.make_async_copy(refs[0], held.at[slot], sems.at[slot, 0, 0])]
        out = []
        for j, parts in enumerate(self.parts):
            for i, (which, first, count) in enumerate(parts):
                start = pl.multiple_of((me ^ j) * self.rows + first, 8)
                out.append(pltpu.make_async_copy(
                    refs[1 + which].at[block - 1], held.at[slot, pl.ds(start, count)], sems.at[slot, j, i]))
        return out

    def start(self, refs, blocks, held, sems, me):
        for slot, block in enumerate(blocks):
            for c in self.copies(refs, block, slot, held, sems, me):
                c.start()

    def wait(self, refs, blocks, held, sems, me, step):
        for slot, block in enumerate(blocks):

            @pl.when(step == slot)
            def _(slot=slot, block=block):
                for c in self.copies(refs, block, slot, held, sems, me):
                    c.wait()


def piece_copies(me, grad, keep, send, step, rows, sems):
    out = []
    for j in range(GROUP):
        start = pl.multiple_of((me ^ j) * rows, 8)
        target = (send if j % 2 else keep).at[j // 2, step]
        out.append(pltpu.make_async_copy(grad.at[step, pl.ds(start, rows)], target, sems.at[step, j]))
    return out


def by_rows(count, body, chunk=128):
    def one(i, carry):
        body(pl.ds(pl.multiple_of(i * chunk, chunk), chunk))
        return carry

    lax.fori_loop(0, count // chunk, one, 0)


def norm(residual):
    center = residual - jnp.mean(residual, axis=-1, keepdims=True)
    variance = jnp.mean(center * center, axis=-1, keepdims=True)
    inverse = lax.rsqrt(variance + EPSILON)
    return center * inverse, inverse


def norm_back(upstream, normed, inverse, gain):
    scaled = upstream * gain
    return (
        scaled
        - jnp.mean(scaled, axis=-1, keepdims=True)
        - normed * jnp.mean(scaled * normed, axis=-1, keepdims=True)
    ) * inverse


def column_sum(x):
    return jnp.sum(x, axis=0, keepdims=True)


def bias_tiles(table, tiles):
    heads, seq, pooled = tiles.shape
    for h in range(heads):
        row = jnp.broadcast_to(table[h : h + 1, :], (pooled, table.shape[1]))
        rolled = pltpu.roll(row, table.shape[1] - seq, 1, stride=2, stride_axis=0)
        tiles[h] = rolled[:, :seq].T


def attend(weight, hid, pool, bias, table, segq, segk, q_out, kv_out, ctx_out, lse_out, tiles, dims):
    rows, seq, pooled, heads, width = dims
    local = heads * width
    scale = width ** (-0.5)
    kv_bias = jnp.concatenate([jnp.zeros((1, local), F32), bias[:, local : 2 * local]], axis=1)
    q_bias = bias[:, :local]
    bias_tiles(table, tiles)

    def project(r, carry):
        at = pl.ds(pl.multiple_of(r * seq, seq), seq)
        kv_out[0, at, :] = (nt(hid[at, :], weight[: 2 * local, :]) + kv_bias).astype(B16)
        at = pl.ds(pl.multiple_of(r * pooled, pooled), pooled)
        q_out[0, at, :] = (nt(pool[at, :], weight[2 * local : 3 * local, :]) + q_bias).astype(B16)
        return carry

    lax.fori_loop(0, rows, project, 0)

    for r in range(rows):
        at = slice(r * seq, (r + 1) * seq)
        qat = slice(r * pooled, (r + 1) * pooled)
        allowed = segk[r] == segq[r]
        for h in range(heads):
            lanes = slice(h * width, (h + 1) * width)
            query = (q_out[0, qat, lanes].astype(F32) * scale).astype(B16)
            scores = nt(kv_out[0, at, lanes], query) + tiles[h]
            scores = jnp.where(allowed, scores, MASKED_SCORE)
            top = jnp.max(scores, axis=0, keepdims=True)
            exponent = jnp.exp(scores - top)
            total = jnp.sum(exponent, axis=0, keepdims=True)
            value = kv_out[0, at, local + h * width : local + (h + 1) * width]
            context = tn(value, exponent.astype(B16)) * (1.0 / total)
            ctx_out[0, qat, lanes] = context.T.astype(B16)
            lse_out[0, h : h + 1, qat] = top + jnp.log(total)


def own_body(dims, me_ref, hidden, weight, bias, table, segq, segk,
             pooled_out, pool_low, q_out, kv_out, ctx_out, lse_out, wide, tiles):
    rows, seq, pooled, heads, width = dims
    n = rows * pooled

    def one(i, carry):
        at = pl.ds(pl.multiple_of(i * 128, 128), 128)
        wide[...] = hidden[:, at].astype(F32)
        mean = 0.5 * (wide[pl.ds(0, n, stride=2), :] + wide[pl.ds(1, n, stride=2), :])
        pooled_out[:, at] = mean
        pool_low[:, at] = mean.astype(B16)
        return carry

    lax.fori_loop(0, hidden.shape[1] // 128, one, 0)
    attend(weight, hidden, pool_low, bias[0], table.at[0], segq, segk,
           q_out, kv_out, ctx_out, lse_out, tiles, dims)


def rest_body(dims, gathered, blocks, me_ref, hidden, pool_low, bias, table, segq, segk,
              q_in, kv_in, ctx_in, lse_in, *refs):
    sources = refs[: gathered.count()]
    q_out, kv_out, ctx_out, lse_out, held, tiles, sems = refs[gathered.count() :]
    step = pl.program_id(0)
    me = me_ref[0]

    @pl.when(step == 0)
    def _():
        gathered.start(sources, blocks, held, sems, me)

    gathered.wait(sources, blocks, held, sems, me, step)
    attend(held.at[step], hidden, pool_low, bias[0], table.at[0], segq, segk,
           q_out, kv_out, ctx_out, lse_out, tiles, dims)


def up_body(up_w, me_ref, ctx, pooled, vectors, bias, *refs):
    up_refs = refs[: up_w.count()]
    normed, inverse, low, act, slope, held, total, sems = refs[up_w.count() :]
    phase, step = pl.program_id(0), pl.program_id(1)
    blocks = range(held.shape[0])
    model = low.shape[1]
    me = me_ref[0]
    out_bias, gain, shift = [vectors[i : i + 1, :] for i in range(3)]

    @pl.when(phase == 0)
    def _():
        @pl.when(step == 0)
        def _():
            up_w.start(up_refs, blocks, held, sems, me)
            total[...] = pooled[...] + out_bias

        up_w.wait(up_refs, blocks, held, sems, me, step)
        total[...] += nn(ctx[step], held[step, model:, :])

        @pl.when(step == pl.num_programs(1) - 1)
        def _():
            def one(at):
                n, s = norm(total[at, :])
                normed[at, :] = n
                inverse[at, :] = s
                low[at, :] = (n * gain + shift).astype(B16)

            by_rows(total.shape[0], one)

    @pl.when(phase == 1)
    def _():
        chunk = 256

        def one(i, carry):
            at = pl.ds(pl.multiple_of(i * chunk, chunk), chunk)
            pre = nn(low[...], held[step, :model, at]) + bias[0, :, at]
            phi = 0.5 * (1.0 + lax.erf(pre * (0.5**0.5)))
            density = jnp.exp(-0.5 * pre * pre) * 0.3989422804014327
            act[0, :, at] = (pre * phi).astype(B16)
            slope[0, :, at] = (phi + pre * density).astype(B16)
            return carry

        lax.fori_loop(0, held.shape[2] // chunk, one, 0)


def ffn_body(up_w, down_w, me_ref, act, slope, ctx, normed, inverse, low, cot, vectors, *refs):
    n_up, n_down = up_w.count(), down_w.count()
    up_refs, down_refs = refs[:n_up], refs[n_up : n_up + n_down]
    (output, grad_first, gctx, bias_grad, sums, down_keep, down_send, up_keep, up_send,
     up_held, down_held, total, grad_low, down_grad, up_grad, up_sems, down_sems, down_out, up_out) = refs[n_up + n_down :]
    phase, step = pl.program_id(0), pl.program_id(1)
    last = pl.num_programs(1) - 1
    blocks = range(up_held.shape[0])
    model = low.shape[1]
    count = low.shape[0]
    me = me_ref[0]
    _, gain1, shift1, down_bias, gain2, shift2 = [vectors[i : i + 1, :] for i in range(6)]

    def down_copies(k):
        return piece_copies(me, down_grad, down_keep, down_send, k, down_w.rows, down_out)

    def up_copies(k):
        return piece_copies(me, up_grad, up_keep, up_send, k, up_w.rows, up_out)

    @pl.when(phase == 0)
    def _():
        @pl.when(step == 0)
        def _():
            down_w.start(down_refs, blocks, down_held, down_sems, me)
            up_w.start(up_refs, blocks, up_held, up_sems, me)
            total[...] = normed[...] * gain1 + shift1 + down_bias
            sums[...] = jnp.zeros_like(sums)

        down_w.wait(down_refs, blocks, down_held, down_sems, me, step)
        total[...] += nn(act[0], down_held[step])

        @pl.when(step == last)
        def _():
            def one(at):
                n, s = norm(total[at, :])
                output[at, :] = (n * gain2 + shift2).astype(B16)
                upstream = cot[at, :].astype(F32)
                back = norm_back(upstream, n, s, gain2)
                total[at, :] = back
                grad_low[at, :] = back.astype(B16)
                sums[3:4, :] += column_sum(upstream * n)
                sums[4:5, :] += column_sum(upstream)
                sums[5:6, :] += column_sum(back)

            by_rows(count, one)

    @pl.when(phase == 1)
    def _():
        down_grad[step] = tn(act[0], grad_low[...]).astype(B16)
        for c in down_copies(step):
            c.start()
        value = (nt(grad_low[...], down_held[step]) * slope[0].astype(F32)).astype(B16)
        bias_grad[0] = column_sum(value.astype(F32))
        up_w.wait(up_refs, blocks, up_held, up_sems, me, step)
        up_grad[step, :model, :] = tn(low[...], value).astype(B16)
        for j, c in enumerate(up_copies(step)):
            pl.when(((me ^ j) + 1) * up_w.rows <= model)(c.start)
        total[...] += nt(value, up_held[step, :model, :])

        @pl.when(step == last)
        def _():
            def one(at):
                upstream = total[at, :]
                n = normed[at, :]
                back = norm_back(upstream, n, inverse[at, :], gain1)
                grad_first[at, :] = back
                grad_low[at, :] = back.astype(B16)
                sums[0:1, :] += column_sum(upstream * n)
                sums[1:2, :] += column_sum(upstream)
                sums[2:3, :] += column_sum(back)

            by_rows(count, one)

    @pl.when(phase == 2)
    def _():
        gctx[0] = nt(grad_low[...], up_held[step, model:, :]).astype(B16)
        up_grad[step, model:, :] = tn(ctx[step], grad_low[...]).astype(B16)
        for j, c in enumerate(up_copies(step)):
            pl.when(((me ^ j) + 1) * up_w.rows > model)(c.start)

        @pl.when(step == last)
        def _():
            for k in blocks:
                for c in down_copies(k) + up_copies(k):
                    c.wait()


def diagonal_sums(tile, seq, table_len):
    rows = tile.shape[0]
    x = jnp.concatenate([jnp.zeros((rows, table_len - seq), F32), tile], axis=1)
    while rows > 8:
        half = rows // 2
        x = x[:half] + pltpu.roll(x[half:], table_len - 2 * half, 1)
        rows = half
    out = x[0:1]
    for i in range(1, rows):
        out = out + pltpu.roll(x, table_len - 2 * i, 1)[i : i + 1]
    return out


def attend_back_body(dims, skip, me_ref, hidden, pool_low, table, segq, segk, q_in, kv_in, ctx_in, lse_in, gctx,
                     up_bias_grad, sums, *refs):
    rows, seq, pooled, heads, width = dims
    local = heads * width
    scale = width ** (-0.5)
    me = me_ref[0]
    model = hidden.shape[1]
    dq_out, dkv_out, keep, send, tiles, tile_grad, grad, extra = refs[skip:]
    bias_tiles(table.at[0], tiles)
    product = gctx[0].astype(F32) * ctx_in[0].astype(F32)
    high = product.astype(B16)
    rest = (product - high.astype(F32)).astype(B16)
    line = lax.broadcasted_iota(jnp.int32, (8, local), 0)
    col = lax.broadcasted_iota(jnp.int32, (8, local), 1)
    pick = ((col >= line * width) & (col < (line + 1) * width)).astype(F32).astype(B16)
    inner = nt(pick, high) + nt(pick, rest)

    for r in range(rows):
        at = slice(r * seq, (r + 1) * seq)
        qat = slice(r * pooled, (r + 1) * pooled)
        allowed = segk[r] == segq[r]
        for h in range(heads):
            lanes = slice(h * width, (h + 1) * width)
            vlanes = slice(local + h * width, local + (h + 1) * width)
            query = (q_in[0, qat, lanes].astype(F32) * scale).astype(B16)
            key = kv_in[0, at, lanes]
            scores = nt(key, query) + tiles[h]
            scores = jnp.where(allowed, scores, MASKED_SCORE)
            prob = jnp.exp(scores - lse_in[0, h : h + 1, qat])
            upstream = gctx[0, qat, lanes]
            gprob = nt(kv_in[0, at, vlanes], upstream)
            gscore = (prob * (gprob - inner[h : h + 1, qat])).astype(B16)
            if r == 0:
                tile_grad[h] = gscore.astype(F32)
            else:
                tile_grad[h] += gscore.astype(F32)
            dkv_out[0, at, vlanes] = nn(prob.astype(B16), upstream).astype(B16)
            dkv_out[0, at, lanes] = nn(gscore, query).astype(B16)
            dq_out[0, qat, lanes] = (tn(key, gscore) * scale).T.astype(B16)

    table_len = table.shape[2]
    extra[...] = jnp.zeros_like(extra)
    for h in range(heads):
        line = diagonal_sums(tile_grad[h].T, seq, table_len)
        for i, at in enumerate(range(0, table_len, model)):
            size = min(model, table_len - at)
            extra[lines_of(table_len, model) * h + i : lines_of(table_len, model) * h + i + 1, :size] = line[:, at : at + size]
    at = lines_of(table_len, model) * heads
    extra[at : at + 1, :local] = column_sum(dq_out[0].astype(F32))
    extra[at + 1 : at + 2, :local] = column_sum(dkv_out[0, :, local:].astype(F32))
    extra[at + 2 : at + 3, : up_bias_grad.shape[2]] = up_bias_grad[0]
    extra[at + 3 : at + 9, :] = sums[:6, :]
    grad[: 2 * local, :] = tn(dkv_out[0], hidden[...])
    grad[2 * local :, :] = tn(dq_out[0], pool_low[...])
    rows = grad.shape[0] // GROUP
    lines = extra.shape[0] // GROUP
    for j in range(GROUP):
        owner = me ^ j
        out = send if j % 2 else keep
        out[j // 2, 0, :rows] = grad[pl.ds(pl.multiple_of(owner * rows, 8), rows), :].astype(B16)
        out[j // 2, 0, rows:] = extra[pl.ds(pl.multiple_of(owner * lines, 8), lines), :].astype(B16)


def lines_of(length, width):
    return -(-length // width)


def hidden_back_body(gathered, order, me_ref, grad_first, *refs):
    sources = refs[: gathered.count()]
    dq, dkv, hidden_grad, held, htotal, ptotal, wide, sems = refs[gathered.count() :]
    me = me_ref[0]
    step = pl.program_id(0)
    local = dq.shape[2]

    @pl.when(step == 0)
    def _():
        gathered.start(sources, order, held, sems, me)
        ptotal[...] = grad_first[...]
        htotal[...] = jnp.zeros_like(htotal)

    gathered.wait(sources, order, held, sems, me, step)
    htotal[...] += nn(dkv[0], held[step, : 2 * local, :])
    ptotal[...] += nn(dq[0], held[step, 2 * local :, :])

    @pl.when(step == pl.num_programs(0) - 1)
    def _():
        m = ptotal.shape[0]

        def one(i, carry):
            at = pl.ds(pl.multiple_of(i * 128, 128), 128)
            half = 0.5 * ptotal[:, at]
            wide[pl.ds(0, m, stride=2), :] = half
            wide[pl.ds(1, m, stride=2), :] = half
            hidden_grad[:, at] = (htotal[:, at] + wide[...]).astype(B16)
            return carry

        lax.fori_loop(0, ptotal.shape[1] // 128, one, 0)


def take(refs, where):
    which, lead = where
    return refs[which][...] if lead is None else refs[which][lead]


def unpack_rows_body(where, me_ref, *refs):
    n = max(w for w, _ in where) + 1
    outs, total = refs[n:-1], refs[-1]
    rows = total.shape[0] // GROUP
    for j in range(GROUP):
        total[pl.ds(pl.multiple_of((me_ref[0] ^ j) * rows, 8), rows), :] = take(refs, where[j]).astype(F32)
    at = 0
    for out in outs:
        out[...] = total[at : at + out.shape[0], :]
        at += out.shape[0]


def unpack_attention_body(where, heads, me_ref, *refs):
    n = max(w for w, _ in where) + 1
    weights, table, q_bias, v_bias, up_bias, norms, total, extra = refs[n : n + 3], *refs[n + 3 :]
    rows = total.shape[0] // GROUP
    lines = extra.shape[0] // GROUP
    for j in range(GROUP):
        piece = take(refs, where[j]).astype(F32)
        owner = me_ref[0] ^ j
        total[pl.ds(pl.multiple_of(owner * rows, 8), rows), :] = piece[:rows]
        extra[pl.ds(pl.multiple_of(owner * lines, 8), lines), :] = piece[rows:]
    local, model = weights[0].shape
    for i, out in enumerate(weights):
        out[...] = total[i * local : (i + 1) * local, :]
    table_len = table.shape[1]
    per = lines_of(table_len, model)
    for h in range(heads):
        for i, at in enumerate(range(0, table_len, model)):
            size = min(model, table_len - at)
            table[h : h + 1, at : at + size] = extra[per * h + i : per * h + i + 1, :size]
    at = per * heads
    q_bias[...] = extra[at : at + 1, :local]
    v_bias[...] = extra[at + 1 : at + 2, :local]
    up_bias[...] = extra[at + 2 : at + 3, : up_bias.shape[1]]
    norms[...] = extra[at + 3 : at + 9, :]


def per_device(n_dp, n_t, hidden, cotangent, segments, pooled_segments, positions,
               query_projection_weight, query_bias, key_weight, value_weight, value_bias,
               output_projection_weight, out_bias, relative_bias, first_gain, first_shift,
               up_projection_weight, up_projection_bias, down_projection_weight, down_bias,
               second_gain, second_shift):
    rows, seq, model = hidden.shape
    pooled_len = seq // 2
    heads, table_len = relative_bias.shape
    width = query_projection_weight.shape[1] // heads
    local = heads * width
    ff = up_projection_weight.shape[1]
    dims = (rows, seq, pooled_len, heads, width)
    tokens, ptokens = rows * seq, rows * pooled_len
    blocks = n_t
    sds = jax.ShapeDtypeStruct
    t_index = lax.axis_index("tensor")
    me = lax.axis_index("dp") % GROUP
    tok = me.astype(jnp.int32).reshape(1)

    def across(x, mask):
        return lax.ppermute(x, "dp", [(i, i ^ mask) for i in range(n_dp)])

    def along(x, mask):
        return lax.ppermute(x, "tensor", [(i, i ^ mask) for i in range(n_t)])

    def row(v):
        return v.astype(F32).reshape(1, -1)

    def cut(own):
        size = own.shape[0] // GROUP
        return lax.dynamic_slice(own, (me * size, 0), (size, own.shape[1]))

    def spread(piece):
        return [along(piece, k) for k in range(1, blocks)]

    bar = lambda *xs: list(lax.optimization_barrier(tuple(xs)))
    sem = pltpu.SemaphoreType.DMA((blocks, GROUP, 2))
    vec = whole((1, model))
    ptoken = whole((ptokens, model))
    lane = 128
    lse_rows = 8

    tick = [tok]

    def order(*xs):
        tick[0], *out = bar(tick[0], *xs)
        return out

    def plane(base):
        return [across(base, m) for m in (2, 4, 6)]

    def other(xs):
        return [across(x, 1) for x in xs]

    def weight(own, even, core):
        size = own.shape[0] // GROUP
        return Gathered(own, even + core, [[(i, 0, size)] for i in (0, 4, 1, 5, 2, 6, 3, 7)])

    hid = hidden.reshape(tokens, model)
    cot = cotangent.reshape(ptokens, model)
    saved_shapes = [
        sds((blocks, ptokens, local), B16),
        sds((blocks, tokens, 2 * local), B16),
        sds((blocks, ptokens, local), B16),
        sds((blocks, lse_rows, ptokens), F32),
    ]

    def block(shape, first=0, by=1):
        return pl.BlockSpec((1,) + tuple(shape), lambda *i: (first + by * i[-1],) + (0,) * len(shape))

    def saved_specs(first):
        return [block(s.shape[1:], first) for s in saved_shapes]

    tile = vmem((heads, seq, pooled_len), F32)

    def far_first(piece):
        return along(piece, 2)

    def pair(piece, far):
        return jnp.stack([piece, far])

    def foreign(far, near):
        return jnp.stack([near[0], far, near[1]])

    def halves(a, b):
        cut_at = a.shape[1] // 16 * 8
        return cut_at, [b[:, :cut_at], a[:, cut_at:]]

    def halved(own, even, core, cut_at):
        size = own.shape[0] // GROUP
        parts = []
        for j in range(GROUP):
            add = 5 if j & 1 else 0
            if j & 6 == 6:
                parts.append([(3 + add, 0, cut_at), (4 + add, cut_at, size - cut_at)])
            else:
                parts.append([({0: 0, 2: 1, 4: 2}[j & 6] + add, 0, size)])
        return Gathered(own, even + core, parts)

    attn_own = jnp.concatenate([key_weight.T, value_weight.T, query_projection_weight.T], axis=0)
    attn_own, attn_piece = order(attn_own, cut(attn_own))
    attn_parts = spread(attn_piece)
    relative_bias, query_bias, value_bias, up_projection_bias, segments, pooled_segments = order(
        relative_bias, query_bias, value_bias, up_projection_bias, segments, pooled_segments)
    own_bias = jnp.concatenate([query_bias, value_bias]).astype(F32).reshape(1, 1, 2 * local)
    seg = lax.dynamic_slice(segments, (t_index * rows, 0), (rows, seq)).reshape(rows, seq, 1)
    pseg = lax.dynamic_slice(pooled_segments, (t_index * rows, 0), (rows, pooled_len))
    pseg = pseg.reshape(rows, 1, pooled_len)
    seg, pseg, own_bias = order(seg, pseg, own_bias)
    own_out = call(
        partial(own_body, dims),
        (1,),
        [SMEM, whole((tokens, model)), whole(attn_own.shape), block((1, 2 * local)), block((heads, table_len)),
         whole(pseg.shape), whole(seg.shape)],
        [ptoken, ptoken] + saved_specs(0),
        [sds((ptokens, model), F32), sds((ptokens, model), B16)] + saved_shapes,
        [vmem((tokens, 128), F32), tile],
        (tick[0], hid, attn_own, own_bias, relative_bias[None], pseg, seg),
        20,
    )
    pooled, pool_low, saved = own_out[0], own_out[1], list(own_out[2:6])
    saved[3], up_projection_weight, output_projection_weight, down_projection_weight, *attn_parts = order(
        saved[3], up_projection_weight, output_projection_weight, down_projection_weight, *attn_parts)

    (attn_base,) = order(jnp.stack(attn_parts))
    attn_even = [attn_base] + plane(attn_base)
    attn_core = [across(attn_base, 1)]
    up_own = jnp.concatenate([up_projection_weight, output_projection_weight], axis=0)
    up_own, up_piece = order(up_own, cut(up_own))
    up_far = far_first(up_piece)
    down_own = down_projection_weight
    vector = jnp.concatenate(
        [
            relative_bias,
            jnp.pad(own_bias[0], ((0, 0), (0, table_len - 2 * local))),
            jnp.pad(row(up_projection_bias), ((0, 0), (0, table_len - ff))),
        ]
    )
    vector, down_piece, *attn_core = order(vector, cut(down_own), *attn_core)
    vector_far = far_first(vector)
    (up_far,) = order(up_far)
    (up_pair,) = order(pair(up_piece, up_far))
    up_near = along(up_pair, 1)
    (vector_far,) = order(vector_far)
    (vector_pair,) = order(pair(vector, vector_far))
    vector_near = along(vector_pair, 1)
    shared_rows = jnp.stack(
        [out_bias, first_gain, first_shift, down_bias, second_gain, second_shift]
    ).astype(F32)
    shared_rows, vector_near = order(shared_rows, vector_near)
    attn_base, *attn_even = order(*attn_even)
    attn_even = [attn_base] + attn_even
    attn_core += other(attn_even[1:])
    (down_piece,) = order(down_piece)
    down_far = far_first(down_piece)
    vectors = jnp.stack([vector, vector_near[0], vector_far, vector_near[1]])
    tables = vectors[:, :heads]
    attn_bias = vectors[:, heads : heads + 1, : 2 * local]
    up_bias = vectors[:, heads + 1 : heads + 2, :ff]
    tables, attn_bias, up_bias, up_near = order(tables, attn_bias, up_bias, up_near)
    attn_core = order(*attn_core)
    attn_w = weight(attn_own, attn_even, attn_core)
    (up_base,) = order(foreign(up_far, up_near))
    up_a, up_b, up_core = across(up_base, 2), across(up_base, 4), [across(up_base, 1)]

    def attend_blocks(saved, which):
        n_in = 7
        return list(call(
            partial(rest_body, dims, attn_w, which),
            (len(which),),
            [SMEM, whole((tokens, model)), ptoken, block((1, 2 * local), which[0]),
             block((heads, table_len), which[0]), whole(pseg.shape), whole(seg.shape)]
            + [ANY] * 4 + [ANY] * attn_w.count(),
            saved_specs(which[0]),
            saved_shapes,
            [vmem((len(which),) + attn_own.shape, B16), tile,
             pltpu.SemaphoreType.DMA((len(which), GROUP, 2))],
            (tick[0], hid, pool_low, attn_bias, tables, pseg, seg, *saved, attn_w.own, *attn_w.arrays),
            24,
            {n_in + i: i for i in range(4)},
        ))

    (down_far,) = order(down_far)
    (down_pair,) = order(pair(down_piece, down_far))
    down_near = along(down_pair, 1)
    saved = attend_blocks(saved, (1, 2))
    saved[3], up_a, up_b, down_near, *up_core = order(saved[3], up_a, up_b, down_near, *up_core)
    up_cut, up_halves = halves(up_a, up_b)
    down_base, *up_halves = order(foreign(down_far, down_near), *up_halves)
    up_dx, up_dy = across(up_halves[0], 2), across(up_halves[1], 4)
    up_core.append(across(up_a, 1))
    saved = attend_blocks(saved, (3,))
    saved[3], up_dx, up_dy, up_core[1], up_b, down_base = order(
        saved[3], up_dx, up_dy, up_core[1], up_b, down_base)
    up_core += other([up_b, up_dx, up_dy])
    down_even = [down_base] + plane(down_base)
    up_core = order(*up_core)
    up_w = halved(up_own, [up_base, up_a, up_b, up_dx, up_dy], up_core, up_cut)

    phase = lambda n, shape: pl.BlockSpec(
        (1,) + shape,
        lambda p, k: (jnp.where(p < n, 0, jnp.where(p == n, k, blocks - 1)),) + (0,) * len(shape),
    )

    def held_once(shape):
        zeros = (0,) * len(shape)
        return pl.BlockSpec(shape, lambda *_: zeros, pipeline_mode=pl.Buffered(1))

    once = held_once((ptokens, model))
    dims_ff = (blocks, ptokens, ff)
    ctx_spec = held_once((blocks, ptokens, local))
    normed, inverse, low, act, slope = call(
        partial(up_body, up_w),
        (2, blocks),
        [SMEM, ctx_spec, once, whole(shared_rows.shape), phase(1, (1, ff))] + [ANY] * up_w.count(),
        [once, held_once((ptokens, 1)), once, phase(1, (ptokens, ff)), phase(1, (ptokens, ff))],
        [sds((ptokens, model), F32), sds((ptokens, 1), F32), sds((ptokens, model), B16), sds(dims_ff, B16),
         sds(dims_ff, B16)],
        [vmem((blocks,) + up_own.shape, B16), vmem((ptokens, model), F32), sem],
        (tick[0], saved[2], pooled, shared_rows, up_bias, up_w.own, *up_w.arrays),
        60,
    )
    act, *down_even = order(act, *down_even)
    down_w = weight(down_own, down_even, order(*other(down_even)))

    def grad_shape(w):
        return sds((GROUP // 2, blocks, w.rows, model), B16)

    out_sem = pltpu.SemaphoreType.DMA((blocks, GROUP))
    (output, grad_first, gctx, up_bias_grad, sums, down_keep, down_send, up_keep, up_send) = call(
        partial(ffn_body, up_w, down_w),
        (3, blocks),
        [SMEM, pl.BlockSpec((1, ptokens, ff), lambda p, k: (jnp.where(p == 2, blocks - 1, k), 0, 0)),
         phase(1, (ptokens, ff)), ctx_spec, once, held_once((ptokens, 1)), once, once, whole(shared_rows.shape)]
        + [ANY] * (up_w.count() + down_w.count()),
        [once, once, phase(2, (ptokens, local)), phase(1, (1, ff)), whole((8, model)), ANY, ANY, ANY, ANY],
        [sds((ptokens, model), B16), sds((ptokens, model), F32), sds((blocks, ptokens, local), B16),
         sds((blocks, 1, ff), F32), sds((8, model), F32),
         grad_shape(down_w), grad_shape(down_w), grad_shape(up_w), grad_shape(up_w)],
        [vmem((blocks,) + up_own.shape, B16), vmem((blocks,) + down_own.shape, B16),
         vmem((ptokens, model), F32), vmem((ptokens, model), B16), vmem((blocks, ff, model), B16),
         vmem((blocks,) + up_own.shape, B16), sem, sem, out_sem, out_sem],
        (tick[0], act, slope, saved[2], normed, inverse, low, cot, shared_rows,
         up_w.own, *up_w.arrays, down_w.own, *down_w.arrays),
        60,
    )
    attn_rows = attn_own.shape[0]
    extra_rows = 8 * GROUP

    def attend_back(which, slots, into=None):
        by = which[1] - which[0] if len(which) > 1 else 0
        at = lambda shape: block(shape, which[0], by)
        first, n = slots
        piece = (attn_rows + extra_rows) // GROUP
        spec = pl.BlockSpec((GROUP // 2, 1, piece, model), lambda i: (0, first + i, 0, 0))
        grads = sds((GROUP // 2, n, piece, model), B16)
        n_in = 12
        return call(
            partial(attend_back_body, dims, 4 if into else 0),
            (len(which),),
            [SMEM, whole((tokens, model)), ptoken, at((heads, table_len)), whole(pseg.shape), whole(seg.shape)]
            + [at(s.shape[1:]) for s in saved_shapes]
            + [at((ptokens, local)), at((1, ff)), whole((8, model))] + ([ANY] * 4 if into else []),
            [block((ptokens, local), first), block((tokens, 2 * local), first), spec, spec],
            [sds((n, ptokens, local), B16), sds((n, tokens, 2 * local), B16), grads, grads],
            [tile, tile, vmem((attn_rows, model), F32), vmem((extra_rows, model), F32)],
            (tick[0], hid, pool_low, tables, pseg, seg, *saved, gctx, up_bias_grad, sums, *(into or ())),
            32,
            {13 + i: i for i in range(4)} if into else None,
        )

    f32 = lambda x: x.astype(F32)

    class Sum:
        def __init__(self, *arrays):
            self.arrays = arrays

        def __getitem__(self, at):
            return Sum(*[a[at] for a in self.arrays])

        def plus(self, *more):
            return Sum(*self.arrays, *more)

        def value(self):
            total = f32(self.arrays[0])
            for a in self.arrays[1:]:
                total = total + f32(a)
            return total

        def low(self):
            return self.value().astype(B16)

    def by_plane(keep, got):
        return Sum(*[a.reshape((2, 2) + a.shape[1:]) for a in (keep, got)])

    def wider(total):
        bit = GROUP
        while bit < n_dp:
            total = total.plus(across(total.low(), bit))
            bit *= 2
        return total

    def go_first(total):
        half = total.arrays[0].shape[2] // 2
        a, b = total[:, :, :half], total[:, :, half:]
        out = order(a[:, 1].low(), b[1].low())
        return (a[:, 0], b[0]), [across(out[0], 2), across(out[1], 4)]

    def go_second(kept, got):
        a, b = kept[0].plus(got[0]), kept[1].plus(got[1])
        out = order(a[1].low(), b[1].low())
        return (a[0], b[0]), [across(out[0], 4), across(out[1], 2)]

    def near_hop(blocks_of):
        (out,) = order(jnp.stack([blocks_of[1].low(), blocks_of[3].low()]))
        return (blocks_of[0], blocks_of[2]), along(out, 1)

    def far_hop(kept, got):
        (out,) = order(kept[1].plus(got[1]).low())
        return kept[0].plus(got[0]), along(out, 2)

    def hop_first(kept):
        a, b = wider(kept[0]), wider(kept[1])
        return near_hop([a[0], a[1], b[0], b[1]])

    gctx, down_send, up_send = order(gctx, down_send, up_send)
    down_got, up_got = across(down_send, 1), across(up_send, 1)
    (down_got,) = order(down_got)
    down_kept, down_got = go_first(by_plane(down_keep, down_got))
    back = attend_back((3, 1), (0, 4))
    back[0], up_got = order(back[0], up_got)
    up_kept, up_got = go_first(by_plane(up_keep, up_got))
    back = attend_back((2, 0), (2, 4), back)
    back[0], back[3], *got = order(back[0], back[3], *down_got, *up_got)
    down_got, up_got = got[:2], got[2:]
    attn_got = across(back[3], 1)
    down_kept, down_got = go_second(down_kept, down_got)
    up_kept, up_got = go_second(up_kept, up_got)
    (attn_got,) = order(attn_got)
    down_got = order(*down_got)
    attn_kept, attn_got = go_first(by_plane(back[2], attn_got))
    down_kept, down_got = hop_first([k.plus(g) for k, g in zip(down_kept, down_got)])

    hidden_grad = call(
        partial(hidden_back_body, attn_w, (3, 1, 2, 0)),
        (blocks,),
        [SMEM, ptoken] + [ANY] * attn_w.count() + [block((ptokens, local)), block((tokens, 2 * local))],
        whole((tokens, model)),
        sds((tokens, model), B16),
        [vmem((blocks,) + attn_own.shape, B16), vmem((tokens, model), F32), vmem((ptokens, model), F32),
         vmem((tokens, 128), F32), sem],
        (tick[0], grad_first, attn_w.own, *attn_w.arrays, back[0], back[1]),
        28,
    )
    hidden_grad, down_got, *up_got = order(hidden_grad, down_got, *up_got)
    down_kept, down_got = far_hop(down_kept, down_got)
    up_kept, up_got = hop_first([k.plus(g) for k, g in zip(up_kept, up_got)])
    attn_got = order(*attn_got)
    attn_kept, attn_got = go_second(attn_kept, attn_got)
    (down_got,) = order(down_got)
    (down_done,) = order(down_kept.plus(down_got).low())
    down_y = across(down_done, 4)
    (up_got,) = order(up_got)
    up_kept, up_got = far_hop(up_kept, up_got)
    attn_got = order(*attn_got)
    odd, even = wider(attn_kept[0].plus(attn_got[0])), wider(attn_kept[1].plus(attn_got[1]))
    attn_out = order(even[0].low(), odd[0].low(), odd[1].low())
    attn_got = [along(attn_out[0], 2), along(attn_out[1], 3), along(attn_out[2], 1)]
    attn_kept = even[1]
    (down_y,) = order(down_y)
    (down_pair,) = order(jnp.stack([down_done, down_y]))
    down_x = across(down_pair, 2)
    (up_got,) = order(up_got)
    (up_done,) = order(up_kept.plus(up_got).low())
    attn_got = order(*attn_got)
    (attn_done,) = order(attn_kept.plus(*attn_got).low())
    attn_even = [attn_done] + plane(attn_done)
    (down_x,) = order(down_x)
    (down_four,) = order(jnp.concatenate([down_pair, down_x]))
    down_core = across(down_four, 1)
    attn_even = order(*attn_even)
    up_even = [up_done] + plane(order(up_done)[0])
    (attn_stack,) = order(jnp.stack(attn_even))
    attn_core = across(attn_stack, 1)
    (down_core,) = order(down_core)
    down_place = [None] * GROUP
    for i, m in enumerate((0, 4, 2, 6)):
        down_place[m], down_place[m ^ 1] = (0, i), (1, i)
    place = [(0, None), (4, 0), (1, None), (4, 1), (2, None), (4, 2), (3, None), (4, 3)]

    def unpack(body, arrays, outs, scratch):
        return call(
            body, (1,), [SMEM] + [whole(a.shape) for a in arrays], [whole(o) for o in outs],
            [sds(o, F32) for o in outs], [vmem(x, F32) for x in scratch], (tick[0], *arrays), 12,
        )

    (down_weight_gradient,) = unpack(
        partial(unpack_rows_body, down_place), [down_four, down_core], [(ff, model)], [down_own.shape])
    down_weight_gradient, attn_core = order(down_weight_gradient, attn_core)
    key_grad, value_grad, query_grad, table_grad, q_bias_grad, v_bias_grad, up_bias_grad, norms = unpack(
        partial(unpack_attention_body, place, heads), attn_even + [attn_core],
        [(local, model)] * 3 + [(heads, table_len), (1, local), (1, local), (1, ff), (6, model)],
        [attn_own.shape, (extra_rows, model)])
    norms, *up_even = order(norms, *up_even)
    (up_stack,) = order(jnp.stack(up_even))
    up_core = across(up_stack, 1)
    up_weight_gradient, out_grad = unpack(
        partial(unpack_rows_body, place), up_even + [up_core], [(model, ff), (local, model)], [up_own.shape])

    return (
        output.reshape(rows, pooled_len, model),
        hidden_grad.reshape(rows, seq, model),
        query_grad.T,
        q_bias_grad.reshape(-1),
        key_grad.T,
        value_grad.T,
        v_bias_grad.reshape(-1),
        out_grad,
        norms[2],
        table_grad,
        norms[0],
        norms[1],
        up_weight_gradient,
        up_bias_grad.reshape(-1),
        down_weight_gradient,
        norms[5],
        norms[3],
        norms[4],
    )


def solution(mesh):
    placed = (
        P(("dp", "tensor"), None, None),
        P(("dp", "tensor"), None, None),
        P("dp", None),
        P("dp", None),
        P("dp", None),
        P(None, "tensor"),
        P("tensor"),
        P(None, "tensor"),
        P(None, "tensor"),
        P("tensor"),
        P("tensor", None),
        P(),
        P("tensor", None),
        P(),
        P(),
        P(None, "tensor"),
        P("tensor"),
        P("tensor", None),
        P(),
        P(),
        P(),
    )
    return jax.shard_map(
        partial(per_device, mesh.shape["dp"], mesh.shape["tensor"]),
        mesh=mesh,
        in_specs=placed,
        out_specs=(
            P(("dp", "tensor"), None, None),
            P(("dp", "tensor"), None, None),
            P(None, "tensor"),
            P("tensor"),
            P(None, "tensor"),
            P(None, "tensor"),
            P("tensor"),
            P("tensor", None),
            P(),
            P("tensor", None),
            P(),
            P(),
            P(None, "tensor"),
            P("tensor"),
            P("tensor", None),
            P(),
            P(),
            P(),
        ),
        check_vma=False,
    )
```

```python
from functools import partial

import jax
import jax.numpy as jnp
from jax import lax
from jax.experimental import pallas as pl
from jax.experimental.pallas import tpu as pltpu
from jax.sharding import PartitionSpec as P

EPSILON = 1e-05
MASKED_SCORE = -1000000000.0
GROUP = 8
F32 = jnp.float32
B16 = jnp.bfloat16


def nn(a, b):
    return lax.dot_general(a, b, (((1,), (0,)), ((), ())), preferred_element_type=F32)


def nt(a, b):
    return lax.dot_general(a, b, (((1,), (1,)), ((), ())), preferred_element_type=F32)


def tn(a, b):
    return lax.dot_general(a, b, (((0,), (0,)), ((), ())), preferred_element_type=F32)


def vmem(shape, dtype):
    return pltpu.VMEM(shape, dtype)


ANY = pl.BlockSpec(memory_space=pl.ANY)
SMEM = pl.BlockSpec(memory_space=pltpu.SMEM)


def whole(shape):
    zeros = (0,) * len(shape)
    return pl.BlockSpec(shape, lambda *_: zeros)


def call(body, grid, in_specs, out_specs, out_shape, scratch, args, limit, aliases=None):
    out = pl.pallas_call(
        body,
        grid=grid,
        in_specs=in_specs,
        out_specs=out_specs,
        out_shape=out_shape,
        scratch_shapes=scratch,
        input_output_aliases=aliases or {},
        compiler_params=pltpu.CompilerParams(
            vmem_limit_bytes=limit << 20, dimension_semantics=("arbitrary",) * len(grid)
        ),
        cost_estimate=pl.CostEstimate(flops=10 << 30, bytes_accessed=20 << 20, transcendentals=0),
    )(*args)
    return list(out) if isinstance(out, (list, tuple)) else out


class Gathered:
    def __init__(self, own, arrays, parts):
        self.own, self.arrays, self.parts = own, arrays, parts
        self.rows = own.shape[0] // GROUP

    def count(self):
        return 1 + len(self.arrays)

    def copies(self, refs, block, slot, held, sems, me):
        if block == 0:
            return [pltpu.make_async_copy(refs[0], held.at[slot], sems.at[slot, 0, 0])]
        out = []
        for j, parts in enumerate(self.parts):
            for i, (which, first, count) in enumerate(parts):
                start = pl.multiple_of((me ^ j) * self.rows + first, 8)
                out.append(pltpu.make_async_copy(
                    refs[1 + which].at[block - 1], held.at[slot, pl.ds(start, count)], sems.at[slot, j, i]))
        return out

    def start(self, refs, blocks, held, sems, me):
        for slot, block in enumerate(blocks):
            for c in self.copies(refs, block, slot, held, sems, me):
                c.start()

    def wait(self, refs, blocks, held, sems, me, step):
        for slot, block in enumerate(blocks):

            @pl.when(step == slot)
            def _(slot=slot, block=block):
                for c in self.copies(refs, block, slot, held, sems, me):
                    c.wait()


def piece_copies(me, grad, keep, send, step, rows, sems):
    out = []
    for j in range(GROUP):
        start = pl.multiple_of((me ^ j) * rows, 8)
        target = (send if j % 2 else keep).at[j // 2, step]
        out.append(pltpu.make_async_copy(grad.at[step, pl.ds(start, rows)], target, sems.at[step, j]))
    return out


def by_rows(count, body, chunk=128):
    def one(i, carry):
        body(pl.ds(pl.multiple_of(i * chunk, chunk), chunk))
        return carry

    lax.fori_loop(0, count // chunk, one, 0)


def norm(residual):
    center = residual - jnp.mean(residual, axis=-1, keepdims=True)
    variance = jnp.mean(center * center, axis=-1, keepdims=True)
    inverse = lax.rsqrt(variance + EPSILON)
    return center * inverse, inverse


def norm_back(upstream, normed, inverse, gain):
    scaled = upstream * gain
    return (
        scaled
        - jnp.mean(scaled, axis=-1, keepdims=True)
        - normed * jnp.mean(scaled * normed, axis=-1, keepdims=True)
    ) * inverse


def column_sum(x):
    return jnp.sum(x, axis=0, keepdims=True)


def bias_tiles(table, tiles):
    heads, seq, pooled = tiles.shape
    for h in range(heads):
        row = jnp.broadcast_to(table[h : h + 1, :], (pooled, table.shape[1]))
        rolled = pltpu.roll(row, table.shape[1] - seq, 1, stride=2, stride_axis=0)
        tiles[h] = rolled[:, :seq].T


def attend(weight, hid, pool, bias, table, segq, segk, q_out, kv_out, ctx_out, lse_out, tiles, dims):
    rows, seq, pooled, heads, width = dims
    local = heads * width
    scale = width ** (-0.5)
    kv_bias = jnp.concatenate([jnp.zeros((1, local), F32), bias[:, local : 2 * local]], axis=1)
    q_bias = bias[:, :local]
    bias_tiles(table, tiles)

    def project(r, carry):
        at = pl.ds(pl.multiple_of(r * seq, seq), seq)
        kv_out[0, at, :] = (nt(hid[at, :], weight[: 2 * local, :]) + kv_bias).astype(B16)
        at = pl.ds(pl.multiple_of(r * pooled, pooled), pooled)
        q_out[0, at, :] = (nt(pool[at, :], weight[2 * local : 3 * local, :]) + q_bias).astype(B16)
        return carry

    lax.fori_loop(0, rows, project, 0)

    for r in range(rows):
        at = slice(r * seq, (r + 1) * seq)
        qat = slice(r * pooled, (r + 1) * pooled)
        allowed = segk[r] == segq[r]
        for h in range(heads):
            lanes = slice(h * width, (h + 1) * width)
            query = (q_out[0, qat, lanes].astype(F32) * scale).astype(B16)
            scores = nt(kv_out[0, at, lanes], query) + tiles[h]
            scores = jnp.where(allowed, scores, MASKED_SCORE)
            top = jnp.max(scores, axis=0, keepdims=True)
            exponent = jnp.exp(scores - top)
            total = jnp.sum(exponent, axis=0, keepdims=True)
            value = kv_out[0, at, local + h * width : local + (h + 1) * width]
            context = tn(value, exponent.astype(B16)) * (1.0 / total)
            ctx_out[0, qat, lanes] = context.T.astype(B16)
            lse_out[0, h : h + 1, qat] = top + jnp.log(total)


def own_body(dims, me_ref, hidden, weight, bias, table, segq, segk,
             pooled_out, pool_low, q_out, kv_out, ctx_out, lse_out, wide, tiles):
    rows, seq, pooled, heads, width = dims
    n = rows * pooled

    def one(i, carry):
        at = pl.ds(pl.multiple_of(i * 128, 128), 128)
        wide[...] = hidden[:, at].astype(F32)
        mean = 0.5 * (wide[pl.ds(0, n, stride=2), :] + wide[pl.ds(1, n, stride=2), :])
        pooled_out[:, at] = mean
        pool_low[:, at] = mean.astype(B16)
        return carry

    lax.fori_loop(0, hidden.shape[1] // 128, one, 0)
    attend(weight, hidden, pool_low, bias[0], table.at[0], segq, segk,
           q_out, kv_out, ctx_out, lse_out, tiles, dims)


def rest_body(dims, gathered, blocks, me_ref, hidden, pool_low, bias, table, segq, segk,
              q_in, kv_in, ctx_in, lse_in, *refs):
    sources = refs[: gathered.count()]
    q_out, kv_out, ctx_out, lse_out, held, tiles, sems = refs[gathered.count() :]
    step = pl.program_id(0)
    me = me_ref[0]

    @pl.when(step == 0)
    def _():
        gathered.start(sources, blocks, held, sems, me)

    gathered.wait(sources, blocks, held, sems, me, step)
    attend(held.at[step], hidden, pool_low, bias[0], table.at[0], segq, segk,
           q_out, kv_out, ctx_out, lse_out, tiles, dims)


def up_body(up_w, me_ref, ctx, pooled, vectors, bias, *refs):
    up_refs = refs[: up_w.count()]
    normed, inverse, low, act, slope, held, total, sems = refs[up_w.count() :]
    phase, step = pl.program_id(0), pl.program_id(1)
    blocks = range(held.shape[0])
    model = low.shape[1]
    me = me_ref[0]
    out_bias, gain, shift = [vectors[i : i + 1, :] for i in range(3)]

    @pl.when(phase == 0)
    def _():
        @pl.when(step == 0)
        def _():
            up_w.start(up_refs, blocks, held, sems, me)
            total[...] = pooled[...] + out_bias

        up_w.wait(up_refs, blocks, held, sems, me, step)
        total[...] += nn(ctx[step], held[step, model:, :])

        @pl.when(step == pl.num_programs(1) - 1)
        def _():
            def one(at):
                n, s = norm(total[at, :])
                normed[at, :] = n
                inverse[at, :] = s
                low[at, :] = (n * gain + shift).astype(B16)

            by_rows(total.shape[0], one)

    @pl.when(phase == 1)
    def _():
        chunk = 256

        def one(i, carry):
            at = pl.ds(pl.multiple_of(i * chunk, chunk), chunk)
            pre = nn(low[...], held[step, :model, at]) + bias[0, :, at]
            phi = 0.5 * (1.0 + lax.erf(pre * (0.5**0.5)))
            density = jnp.exp(-0.5 * pre * pre) * 0.3989422804014327
            act[0, :, at] = (pre * phi).astype(B16)
            slope[0, :, at] = (phi + pre * density).astype(B16)
            return carry

        lax.fori_loop(0, held.shape[2] // chunk, one, 0)


def ffn_body(up_w, down_w, me_ref, act, slope, ctx, normed, inverse, low, cot, vectors, *refs):
    n_up, n_down = up_w.count(), down_w.count()
    up_refs, down_refs = refs[:n_up], refs[n_up : n_up + n_down]
    (output, grad_first, gctx, bias_grad, sums, down_keep, down_send, up_keep, up_send,
     up_held, down_held, total, grad_low, down_grad, up_grad, up_sems, down_sems, down_out, up_out) = refs[n_up + n_down :]
    phase, step = pl.program_id(0), pl.program_id(1)
    last = pl.num_programs(1) - 1
    blocks = range(up_held.shape[0])
    model = low.shape[1]
    count = low.shape[0]
    me = me_ref[0]
    _, gain1, shift1, down_bias, gain2, shift2 = [vectors[i : i + 1, :] for i in range(6)]

    def down_copies(k):
        return piece_copies(me, down_grad, down_keep, down_send, k, down_w.rows, down_out)

    def up_copies(k):
        return piece_copies(me, up_grad, up_keep, up_send, k, up_w.rows, up_out)

    @pl.when(phase == 0)
    def _():
        @pl.when(step == 0)
        def _():
            down_w.start(down_refs, blocks, down_held, down_sems, me)
            up_w.start(up_refs, blocks, up_held, up_sems, me)
            total[...] = normed[...] * gain1 + shift1 + down_bias
            sums[...] = jnp.zeros_like(sums)

        down_w.wait(down_refs, blocks, down_held, down_sems, me, step)
        total[...] += nn(act[0], down_held[step])

        @pl.when(step == last)
        def _():
            def one(at):
                n, s = norm(total[at, :])
                output[at, :] = (n * gain2 + shift2).astype(B16)
                upstream = cot[at, :].astype(F32)
                back = norm_back(upstream, n, s, gain2)
                total[at, :] = back
                grad_low[at, :] = back.astype(B16)
                sums[3:4, :] += column_sum(upstream * n)
                sums[4:5, :] += column_sum(upstream)
                sums[5:6, :] += column_sum(back)

            by_rows(count, one)

    @pl.when(phase == 1)
    def _():
        down_grad[step] = tn(act[0], grad_low[...]).astype(B16)
        for c in down_copies(step):
            c.start()
        value = (nt(grad_low[...], down_held[step]) * slope[0].astype(F32)).astype(B16)
        bias_grad[0] = column_sum(value.astype(F32))
        up_w.wait(up_refs, blocks, up_held, up_sems, me, step)
        up_grad[step, :model, :] = tn(low[...], value).astype(B16)
        for j, c in enumerate(up_copies(step)):
            pl.when(((me ^ j) + 1) * up_w.rows <= model)(c.start)
        total[...] += nt(value, up_held[step, :model, :])

        @pl.when(step == last)
        def _():
            def one(at):
                upstream = total[at, :]
                n = normed[at, :]
                back = norm_back(upstream, n, inverse[at, :], gain1)
                grad_first[at, :] = back
                grad_low[at, :] = back.astype(B16)
                sums[0:1, :] += column_sum(upstream * n)
                sums[1:2, :] += column_sum(upstream)
                sums[2:3, :] += column_sum(back)

            by_rows(count, one)

    @pl.when(phase == 2)
    def _():
        gctx[0] = nt(grad_low[...], up_held[step, model:, :]).astype(B16)
        up_grad[step, model:, :] = tn(ctx[step], grad_low[...]).astype(B16)
        for j, c in enumerate(up_copies(step)):
            pl.when(((me ^ j) + 1) * up_w.rows > model)(c.start)

        @pl.when(step == last)
        def _():
            for k in blocks:
                for c in down_copies(k) + up_copies(k):
                    c.wait()


def diagonal_sums(tile, seq, table_len):
    rows = tile.shape[0]
    x = jnp.concatenate([jnp.zeros((rows, table_len - seq), F32), tile], axis=1)
    while rows > 8:
        half = rows // 2
        x = x[:half] + pltpu.roll(x[half:], table_len - 2 * half, 1)
        rows = half
    out = x[0:1]
    for i in range(1, rows):
        out = out + pltpu.roll(x, table_len - 2 * i, 1)[i : i + 1]
    return out


def attend_back_body(dims, skip, me_ref, hidden, pool_low, table, segq, segk, q_in, kv_in, ctx_in, lse_in, gctx,
                     up_bias_grad, sums, *refs):
    rows, seq, pooled, heads, width = dims
    local = heads * width
    scale = width ** (-0.5)
    me = me_ref[0]
    model = hidden.shape[1]
    dq_out, dkv_out, keep, send, tiles, tile_grad, grad, extra = refs[skip:]
    bias_tiles(table.at[0], tiles)
    product = gctx[0].astype(F32) * ctx_in[0].astype(F32)
    high = product.astype(B16)
    rest = (product - high.astype(F32)).astype(B16)
    line = lax.broadcasted_iota(jnp.int32, (8, local), 0)
    col = lax.broadcasted_iota(jnp.int32, (8, local), 1)
    pick = ((col >= line * width) & (col < (line + 1) * width)).astype(F32).astype(B16)
    inner = nt(pick, high) + nt(pick, rest)

    for r in range(rows):
        at = slice(r * seq, (r + 1) * seq)
        qat = slice(r * pooled, (r + 1) * pooled)
        allowed = segk[r] == segq[r]
        for h in range(heads):
            lanes = slice(h * width, (h + 1) * width)
            vlanes = slice(local + h * width, local + (h + 1) * width)
            query = (q_in[0, qat, lanes].astype(F32) * scale).astype(B16)
            key = kv_in[0, at, lanes]
            scores = nt(key, query) + tiles[h]
            scores = jnp.where(allowed, scores, MASKED_SCORE)
            prob = jnp.exp(scores - lse_in[0, h : h + 1, qat])
            upstream = gctx[0, qat, lanes]
            gprob = nt(kv_in[0, at, vlanes], upstream)
            gscore = (prob * (gprob - inner[h : h + 1, qat])).astype(B16)
            if r == 0:
                tile_grad[h] = gscore.astype(F32)
            else:
                tile_grad[h] += gscore.astype(F32)
            dkv_out[0, at, vlanes] = nn(prob.astype(B16), upstream).astype(B16)
            dkv_out[0, at, lanes] = nn(gscore, query).astype(B16)
            dq_out[0, qat, lanes] = (tn(key, gscore) * scale).T.astype(B16)

    table_len = table.shape[2]
    extra[...] = jnp.zeros_like(extra)
    for h in range(heads):
        line = diagonal_sums(tile_grad[h].T, seq, table_len)
        for i, at in enumerate(range(0, table_len, model)):
            size = min(model, table_len - at)
            extra[lines_of(table_len, model) * h + i : lines_of(table_len, model) * h + i + 1, :size] = line[:, at : at + size]
    at = lines_of(table_len, model) * heads
    extra[at : at + 1, :local] = column_sum(dq_out[0].astype(F32))
    extra[at + 1 : at + 2, :local] = column_sum(dkv_out[0, :, local:].astype(F32))
    extra[at + 2 : at + 3, : up_bias_grad.shape[2]] = up_bias_grad[0]
    extra[at + 3 : at + 9, :] = sums[:6, :]
    grad[: 2 * local, :] = tn(dkv_out[0], hidden[...])
    grad[2 * local :, :] = tn(dq_out[0], pool_low[...])
    rows = grad.shape[0] // GROUP
    lines = extra.shape[0] // GROUP
    for j in range(GROUP):
        owner = me ^ j
        out = send if j % 2 else keep
        out[j // 2, 0, :rows] = grad[pl.ds(pl.multiple_of(owner * rows, 8), rows), :].astype(B16)
        out[j // 2, 0, rows:] = extra[pl.ds(pl.multiple_of(owner * lines, 8), lines), :].astype(B16)


def lines_of(length, width):
    return -(-length // width)


def hidden_back_body(gathered, order, me_ref, grad_first, *refs):
    sources = refs[: gathered.count()]
    dq, dkv, hidden_grad, held, htotal, ptotal, wide, sems = refs[gathered.count() :]
    me = me_ref[0]
    step = pl.program_id(0)
    local = dq.shape[2]

    @pl.when(step == 0)
    def _():
        gathered.start(sources, order, held, sems, me)
        ptotal[...] = grad_first[...]
        htotal[...] = jnp.zeros_like(htotal)

    gathered.wait(sources, order, held, sems, me, step)
    htotal[...] += nn(dkv[0], held[step, : 2 * local, :])
    ptotal[...] += nn(dq[0], held[step, 2 * local :, :])

    @pl.when(step == pl.num_programs(0) - 1)
    def _():
        m = ptotal.shape[0]

        def one(i, carry):
            at = pl.ds(pl.multiple_of(i * 128, 128), 128)
            half = 0.5 * ptotal[:, at]
            wide[pl.ds(0, m, stride=2), :] = half
            wide[pl.ds(1, m, stride=2), :] = half
            hidden_grad[:, at] = (htotal[:, at] + wide[...]).astype(B16)
            return carry

        lax.fori_loop(0, ptotal.shape[1] // 128, one, 0)


def take(refs, where):
    which, lead = where
    return refs[which][...] if lead is None else refs[which][lead]


def unpack_rows_body(where, me_ref, *refs):
    n = max(w for w, _ in where) + 1
    outs, total = refs[n:-1], refs[-1]
    rows = total.shape[0] // GROUP
    for j in range(GROUP):
        total[pl.ds(pl.multiple_of((me_ref[0] ^ j) * rows, 8), rows), :] = take(refs, where[j]).astype(F32)
    at = 0
    for out in outs:
        out[...] = total[at : at + out.shape[0], :]
        at += out.shape[0]


def unpack_attention_body(where, heads, me_ref, *refs):
    n = max(w for w, _ in where) + 1
    weights, table, q_bias, v_bias, up_bias, norms, total, extra = refs[n : n + 3], *refs[n + 3 :]
    rows = total.shape[0] // GROUP
    lines = extra.shape[0] // GROUP
    for j in range(GROUP):
        piece = take(refs, where[j]).astype(F32)
        owner = me_ref[0] ^ j
        total[pl.ds(pl.multiple_of(owner * rows, 8), rows), :] = piece[:rows]
        extra[pl.ds(pl.multiple_of(owner * lines, 8), lines), :] = piece[rows:]
    local, model = weights[0].shape
    for i, out in enumerate(weights):
        out[...] = total[i * local : (i + 1) * local, :]
    table_len = table.shape[1]
    per = lines_of(table_len, model)
    for h in range(heads):
        for i, at in enumerate(range(0, table_len, model)):
            size = min(model, table_len - at)
            table[h : h + 1, at : at + size] = extra[per * h + i : per * h + i + 1, :size]
    at = per * heads
    q_bias[...] = extra[at : at + 1, :local]
    v_bias[...] = extra[at + 1 : at + 2, :local]
    up_bias[...] = extra[at + 2 : at + 3, : up_bias.shape[1]]
    norms[...] = extra[at + 3 : at + 9, :]


def per_device(n_dp, n_t, hidden, cotangent, segments, pooled_segments, positions,
               query_projection_weight, query_bias, key_weight, value_weight, value_bias,
               output_projection_weight, out_bias, relative_bias, first_gain, first_shift,
               up_projection_weight, up_projection_bias, down_projection_weight, down_bias,
               second_gain, second_shift):
    rows, seq, model = hidden.shape
    pooled_len = seq // 2
    heads, table_len = relative_bias.shape
    width = query_projection_weight.shape[1] // heads
    local = heads * width
    ff = up_projection_weight.shape[1]
    dims = (rows, seq, pooled_len, heads, width)
    tokens, ptokens = rows * seq, rows * pooled_len
    blocks = n_t
    sds = jax.ShapeDtypeStruct
    t_index = lax.axis_index("tensor")
    me = lax.axis_index("dp") % GROUP
    tok = me.astype(jnp.int32).reshape(1)

    def across(x, mask):
        return lax.ppermute(x, "dp", [(i, i ^ mask) for i in range(n_dp)])

    def along(x, mask):
        return lax.ppermute(x, "tensor", [(i, i ^ mask) for i in range(n_t)])

    def row(v):
        return v.astype(F32).reshape(1, -1)

    def cut(own):
        size = own.shape[0] // GROUP
        return lax.dynamic_slice(own, (me * size, 0), (size, own.shape[1]))

    def spread(piece):
        return [along(piece, k) for k in range(1, blocks)]

    bar = lambda *xs: list(lax.optimization_barrier(tuple(xs)))
    sem = pltpu.SemaphoreType.DMA((blocks, GROUP, 2))
    vec = whole((1, model))
    ptoken = whole((ptokens, model))
    lane = 128
    lse_rows = 8

    tick = [tok]

    def order(*xs):
        tick[0], *out = bar(tick[0], *xs)
        return out

    def plane(base):
        return [across(base, m) for m in (2, 4, 6)]

    def other(xs):
        return [across(x, 1) for x in xs]

    def weight(own, even, core):
        size = own.shape[0] // GROUP
        return Gathered(own, even + core, [[(i, 0, size)] for i in (0, 4, 1, 5, 2, 6, 3, 7)])

    hid = hidden.reshape(tokens, model)
    cot = cotangent.reshape(ptokens, model)
    saved_shapes = [
        sds((blocks, ptokens, local), B16),
        sds((blocks, tokens, 2 * local), B16),
        sds((blocks, ptokens, local), B16),
        sds((blocks, lse_rows, ptokens), F32),
    ]

    def block(shape, first=0, by=1):
        return pl.BlockSpec((1,) + tuple(shape), lambda *i: (first + by * i[-1],) + (0,) * len(shape))

    def saved_specs(first):
        return [block(s.shape[1:], first) for s in saved_shapes]

    tile = vmem((heads, seq, pooled_len), F32)

    def far_first(piece):
        return along(piece, 2)

    def pair(piece, far):
        return jnp.stack([piece, far])

    def foreign(far, near):
        return jnp.stack([near[0], far, near[1]])

    def halves(a, b):
        cut_at = a.shape[1] // 16 * 8
        return cut_at, [b[:, :cut_at], a[:, cut_at:]]

    def halved(own, even, core, cut_at):
        size = own.shape[0] // GROUP
        parts = []
        for j in range(GROUP):
            add = 5 if j & 1 else 0
            if j & 6 == 6:
                parts.append([(3 + add, 0, cut_at), (4 + add, cut_at, size - cut_at)])
            else:
                parts.append([({0: 0, 2: 1, 4: 2}[j & 6] + add, 0, size)])
        return Gathered(own, even + core, parts)

    attn_own = jnp.concatenate([key_weight.T, value_weight.T, query_projection_weight.T], axis=0)
    attn_own, attn_piece = order(attn_own, cut(attn_own))
    attn_parts = spread(attn_piece)
    relative_bias, query_bias, value_bias, up_projection_bias, segments, pooled_segments = order(
        relative_bias, query_bias, value_bias, up_projection_bias, segments, pooled_segments)
    own_bias = jnp.concatenate([query_bias, value_bias]).astype(F32).reshape(1, 1, 2 * local)
    seg = lax.dynamic_slice(segments, (t_index * rows, 0), (rows, seq)).reshape(rows, seq, 1)
    pseg = lax.dynamic_slice(pooled_segments, (t_index * rows, 0), (rows, pooled_len))
    pseg = pseg.reshape(rows, 1, pooled_len)
    seg, pseg, own_bias = order(seg, pseg, own_bias)
    own_out = call(
        partial(own_body, dims),
        (1,),
        [SMEM, whole((tokens, model)), whole(attn_own.shape), block((1, 2 * local)), block((heads, table_len)),
         whole(pseg.shape), whole(seg.shape)],
        [ptoken, ptoken] + saved_specs(0),
        [sds((ptokens, model), F32), sds((ptokens, model), B16)] + saved_shapes,
        [vmem((tokens, 128), F32), tile],
        (tick[0], hid, attn_own, own_bias, relative_bias[None], pseg, seg),
        20,
    )
    pooled, pool_low, saved = own_out[0], own_out[1], list(own_out[2:6])
    saved[3], up_projection_weight, output_projection_weight, down_projection_weight, *attn_parts = order(
        saved[3], up_projection_weight, output_projection_weight, down_projection_weight, *attn_parts)

    (attn_base,) = order(jnp.stack(attn_parts))
    attn_even = [attn_base] + plane(attn_base)
    attn_core = [across(attn_base, 1)]
    up_own = jnp.concatenate([up_projection_weight, output_projection_weight], axis=0)
    up_own, up_piece = order(up_own, cut(up_own))
    up_far = far_first(up_piece)
    down_own = down_projection_weight
    vector = jnp.concatenate(
        [
            relative_bias,
            jnp.pad(own_bias[0], ((0, 0), (0, table_len - 2 * local))),
            jnp.pad(row(up_projection_bias), ((0, 0), (0, table_len - ff))),
        ]
    )
    vector, down_piece, *attn_core = order(vector, cut(down_own), *attn_core)
    vector_far = far_first(vector)
    (up_far,) = order(up_far)
    (up_pair,) = order(pair(up_piece, up_far))
    up_near = along(up_pair, 1)
    (vector_far,) = order(vector_far)
    (vector_pair,) = order(pair(vector, vector_far))
    vector_near = along(vector_pair, 1)
    shared_rows = jnp.stack(
        [out_bias, first_gain, first_shift, down_bias, second_gain, second_shift]
    ).astype(F32)
    shared_rows, vector_near = order(shared_rows, vector_near)
    attn_base, *attn_even = order(*attn_even)
    attn_even = [attn_base] + attn_even
    attn_core += other(attn_even[1:])
    (down_piece,) = order(down_piece)
    down_far = far_first(down_piece)
    vectors = jnp.stack([vector, vector_near[0], vector_far, vector_near[1]])
    tables = vectors[:, :heads]
    attn_bias = vectors[:, heads : heads + 1, : 2 * local]
    up_bias = vectors[:, heads + 1 : heads + 2, :ff]
    tables, attn_bias, up_bias, up_near = order(tables, attn_bias, up_bias, up_near)
    attn_core = order(*attn_core)
    attn_w = weight(attn_own, attn_even, attn_core)
    (up_base,) = order(foreign(up_far, up_near))
    up_a, up_b, up_core = across(up_base, 2), across(up_base, 4), [across(up_base, 1)]

    def attend_blocks(saved, which):
        n_in = 7
        return list(call(
            partial(rest_body, dims, attn_w, which),
            (len(which),),
            [SMEM, whole((tokens, model)), ptoken, block((1, 2 * local), which[0]),
             block((heads, table_len), which[0]), whole(pseg.shape), whole(seg.shape)]
            + [ANY] * 4 + [ANY] * attn_w.count(),
            saved_specs(which[0]),
            saved_shapes,
            [vmem((len(which),) + attn_own.shape, B16), tile,
             pltpu.SemaphoreType.DMA((len(which), GROUP, 2))],
            (tick[0], hid, pool_low, attn_bias, tables, pseg, seg, *saved, attn_w.own, *attn_w.arrays),
            24,
            {n_in + i: i for i in range(4)},
        ))

    (down_far,) = order(down_far)
    (down_pair,) = order(pair(down_piece, down_far))
    down_near = along(down_pair, 1)
    saved = attend_blocks(saved, (1, 2))
    saved[3], up_a, up_b, down_near, *up_core = order(saved[3], up_a, up_b, down_near, *up_core)
    up_cut, up_halves = halves(up_a, up_b)
    down_base, *up_halves = order(foreign(down_far, down_near), *up_halves)
    up_dx, up_dy = across(up_halves[0], 2), across(up_halves[1], 4)
    up_core.append(across(up_a, 1))
    saved = attend_blocks(saved, (3,))
    saved[3], up_dx, up_dy, up_core[1], up_b, down_base = order(
        saved[3], up_dx, up_dy, up_core[1], up_b, down_base)
    up_core += other([up_b, up_dx, up_dy])
    down_even = plane(down_base)
    up_core = order(*up_core)
    (down_base,) = order(down_base)
    down_first = across(down_base, 1)
    up_w = halved(up_own, [up_base, up_a, up_b, up_dx, up_dy], up_core, up_cut)

    phase = lambda n, shape: pl.BlockSpec(
        (1,) + shape,
        lambda p, k: (jnp.where(p < n, 0, jnp.where(p == n, k, blocks - 1)),) + (0,) * len(shape),
    )

    def held_once(shape):
        zeros = (0,) * len(shape)
        return pl.BlockSpec(shape, lambda *_: zeros, pipeline_mode=pl.Buffered(1))

    once = held_once((ptokens, model))
    dims_ff = (blocks, ptokens, ff)
    ctx_spec = held_once((blocks, ptokens, local))
    normed, inverse, low, act, slope = call(
        partial(up_body, up_w),
        (2, blocks),
        [SMEM, ctx_spec, once, whole(shared_rows.shape), phase(1, (1, ff))] + [ANY] * up_w.count(),
        [once, held_once((ptokens, 1)), once, phase(1, (ptokens, ff)), phase(1, (ptokens, ff))],
        [sds((ptokens, model), F32), sds((ptokens, 1), F32), sds((ptokens, model), B16), sds(dims_ff, B16),
         sds(dims_ff, B16)],
        [vmem((blocks,) + up_own.shape, B16), vmem((ptokens, model), F32), sem],
        (tick[0], saved[2], pooled, shared_rows, up_bias, up_w.own, *up_w.arrays),
        60,
    )
    act, down_first, *down_even = order(act, down_first, *down_even)
    down_w = weight(down_own, [down_base] + down_even, [down_first] + order(*other(down_even)))

    def grad_shape(w):
        return sds((GROUP // 2, blocks, w.rows, model), B16)

    out_sem = pltpu.SemaphoreType.DMA((blocks, GROUP))
    (output, grad_first, gctx, up_bias_grad, sums, down_keep, down_send, up_keep, up_send) = call(
        partial(ffn_body, up_w, down_w),
        (3, blocks),
        [SMEM, pl.BlockSpec((1, ptokens, ff), lambda p, k: (jnp.where(p == 2, blocks - 1, k), 0, 0)),
         phase(1, (ptokens, ff)), ctx_spec, once, held_once((ptokens, 1)), once, once, whole(shared_rows.shape)]
        + [ANY] * (up_w.count() + down_w.count()),
        [once, once, phase(2, (ptokens, local)), phase(1, (1, ff)), whole((8, model)), ANY, ANY, ANY, ANY],
        [sds((ptokens, model), B16), sds((ptokens, model), F32), sds((blocks, ptokens, local), B16),
         sds((blocks, 1, ff), F32), sds((8, model), F32),
         grad_shape(down_w), grad_shape(down_w), grad_shape(up_w), grad_shape(up_w)],
        [vmem((blocks,) + up_own.shape, B16), vmem((blocks,) + down_own.shape, B16),
         vmem((ptokens, model), F32), vmem((ptokens, model), B16), vmem((blocks, ff, model), B16),
         vmem((blocks,) + up_own.shape, B16), sem, sem, out_sem, out_sem],
        (tick[0], act, slope, saved[2], normed, inverse, low, cot, shared_rows,
         up_w.own, *up_w.arrays, down_w.own, *down_w.arrays),
        60,
    )
    attn_rows = attn_own.shape[0]
    extra_rows = 8 * GROUP

    def attend_back(which, slots, into=None):
        by = which[1] - which[0] if len(which) > 1 else 0
        at = lambda shape: block(shape, which[0], by)
        first, n = slots
        piece = (attn_rows + extra_rows) // GROUP
        spec = pl.BlockSpec((GROUP // 2, 1, piece, model), lambda i: (0, first + i, 0, 0))
        grads = sds((GROUP // 2, n, piece, model), B16)
        n_in = 12
        return call(
            partial(attend_back_body, dims, 4 if into else 0),
            (len(which),),
            [SMEM, whole((tokens, model)), ptoken, at((heads, table_len)), whole(pseg.shape), whole(seg.shape)]
            + [at(s.shape[1:]) for s in saved_shapes]
            + [at((ptokens, local)), at((1, ff)), whole((8, model))] + ([ANY] * 4 if into else []),
            [block((ptokens, local), first), block((tokens, 2 * local), first), spec, spec],
            [sds((n, ptokens, local), B16), sds((n, tokens, 2 * local), B16), grads, grads],
            [tile, tile, vmem((attn_rows, model), F32), vmem((extra_rows, model), F32)],
            (tick[0], hid, pool_low, tables, pseg, seg, *saved, gctx, up_bias_grad, sums, *(into or ())),
            32,
            {13 + i: i for i in range(4)} if into else None,
        )

    f32 = lambda x: x.astype(F32)

    class Sum:
        def __init__(self, *arrays):
            self.arrays = arrays

        def __getitem__(self, at):
            return Sum(*[a[at] for a in self.arrays])

        def plus(self, *more):
            return Sum(*self.arrays, *more)

        def value(self):
            total = f32(self.arrays[0])
            for a in self.arrays[1:]:
                total = total + f32(a)
            return total

        def low(self):
            return self.value().astype(B16)

    def by_plane(keep, got):
        return Sum(*[a.reshape((2, 2) + a.shape[1:]) for a in (keep, got)])

    def wider(total):
        bit = GROUP
        while bit < n_dp:
            total = total.plus(across(total.low(), bit))
            bit *= 2
        return total

    def go_first(total):
        half = total.arrays[0].shape[2] // 2
        a, b = total[:, :, :half], total[:, :, half:]
        out = order(a[:, 1].low(), b[1].low())
        return (a[:, 0], b[0]), [across(out[0], 2), across(out[1], 4)]

    def go_second(kept, got):
        a, b = kept[0].plus(got[0]), kept[1].plus(got[1])
        out = order(a[1].low(), b[1].low())
        return (a[0], b[0]), [across(out[0], 4), across(out[1], 2)]

    def near_hop(blocks_of):
        (out,) = order(jnp.stack([blocks_of[1].low(), blocks_of[3].low()]))
        return (blocks_of[0], blocks_of[2]), along(out, 1)

    def far_hop(kept, got):
        (out,) = order(kept[1].plus(got[1]).low())
        return kept[0].plus(got[0]), along(out, 2)

    def hop_first(kept):
        a, b = wider(kept[0]), wider(kept[1])
        return near_hop([a[0], a[1], b[0], b[1]])

    gctx, down_send, up_send = order(gctx, down_send, up_send)
    down_got, up_got = across(down_send, 1), across(up_send, 1)
    (down_got,) = order(down_got)
    down_kept, down_got = go_first(by_plane(down_keep, down_got))
    back = attend_back((3, 1), (0, 4))
    back[0], up_got = order(back[0], up_got)
    up_kept, up_got = go_first(by_plane(up_keep, up_got))
    back = attend_back((2, 0), (2, 4), back)
    back[0], back[3], *got = order(back[0], back[3], *down_got, *up_got)
    down_got, up_got = got[:2], got[2:]
    attn_got = across(back[3], 1)
    down_kept, down_got = go_second(down_kept, down_got)
    up_kept, up_got = go_second(up_kept, up_got)
    (attn_got,) = order(attn_got)
    down_got = order(*down_got)
    attn_kept, attn_got = go_first(by_plane(back[2], attn_got))
    down_kept, down_got = hop_first([k.plus(g) for k, g in zip(down_kept, down_got)])

    hidden_grad = call(
        partial(hidden_back_body, attn_w, (3, 1, 2, 0)),
        (blocks,),
        [SMEM, ptoken] + [ANY] * attn_w.count() + [block((ptokens, local)), block((tokens, 2 * local))],
        whole((tokens, model)),
        sds((tokens, model), B16),
        [vmem((blocks,) + attn_own.shape, B16), vmem((tokens, model), F32), vmem((ptokens, model), F32),
         vmem((tokens, 128), F32), sem],
        (tick[0], grad_first, attn_w.own, *attn_w.arrays, back[0], back[1]),
        28,
    )
    hidden_grad, down_got, *up_got = order(hidden_grad, down_got, *up_got)
    down_kept, down_got = far_hop(down_kept, down_got)
    up_kept, up_got = hop_first([k.plus(g) for k, g in zip(up_kept, up_got)])
    attn_got = order(*attn_got)
    attn_kept, attn_got = go_second(attn_kept, attn_got)
    (down_got,) = order(down_got)
    (down_done,) = order(down_kept.plus(down_got).low())
    down_y = across(down_done, 4)
    (up_got,) = order(up_got)
    up_kept, up_got = far_hop(up_kept, up_got)
    attn_got = order(*attn_got)
    odd, even = wider(attn_kept[0].plus(attn_got[0])), wider(attn_kept[1].plus(attn_got[1]))
    attn_out = order(even[0].low(), odd[0].low(), odd[1].low())
    attn_got = [along(attn_out[0], 2), along(attn_out[1], 3), along(attn_out[2], 1)]
    attn_kept = even[1]
    (down_y,) = order(down_y)
    (down_pair,) = order(jnp.stack([down_done, down_y]))
    down_x = across(down_pair, 2)
    (up_got,) = order(up_got)
    (up_done,) = order(up_kept.plus(up_got).low())
    attn_got = order(*attn_got)
    (attn_done,) = order(attn_kept.plus(*attn_got).low())
    attn_even = [attn_done] + plane(attn_done)
    (down_x,) = order(down_x)
    (down_four,) = order(jnp.concatenate([down_pair, down_x]))
    down_core = across(down_four, 1)
    attn_even = order(*attn_even)
    up_even = [up_done] + plane(order(up_done)[0])
    (attn_stack,) = order(jnp.stack(attn_even))
    attn_core = across(attn_stack, 1)
    (down_core,) = order(down_core)
    down_place = [None] * GROUP
    for i, m in enumerate((0, 4, 2, 6)):
        down_place[m], down_place[m ^ 1] = (0, i), (1, i)
    place = [(0, None), (4, 0), (1, None), (4, 1), (2, None), (4, 2), (3, None), (4, 3)]

    def unpack(body, arrays, outs, scratch):
        return call(
            body, (1,), [SMEM] + [whole(a.shape) for a in arrays], [whole(o) for o in outs],
            [sds(o, F32) for o in outs], [vmem(x, F32) for x in scratch], (tick[0], *arrays), 12,
        )

    (down_weight_gradient,) = unpack(
        partial(unpack_rows_body, down_place), [down_four, down_core], [(ff, model)], [down_own.shape])
    down_weight_gradient, attn_core = order(down_weight_gradient, attn_core)
    key_grad, value_grad, query_grad, table_grad, q_bias_grad, v_bias_grad, up_bias_grad, norms = unpack(
        partial(unpack_attention_body, place, heads), attn_even + [attn_core],
        [(local, model)] * 3 + [(heads, table_len), (1, local), (1, local), (1, ff), (6, model)],
        [attn_own.shape, (extra_rows, model)])
    norms, *up_even = order(norms, *up_even)
    (up_stack,) = order(jnp.stack(up_even))
    up_core = across(up_stack, 1)
    up_weight_gradient, out_grad = unpack(
        partial(unpack_rows_body, place), up_even + [up_core], [(model, ff), (local, model)], [up_own.shape])

    return (
        output.reshape(rows, pooled_len, model),
        hidden_grad.reshape(rows, seq, model),
        query_grad.T,
        q_bias_grad.reshape(-1),
        key_grad.T,
        value_grad.T,
        v_bias_grad.reshape(-1),
        out_grad,
        norms[2],
        table_grad,
        norms[0],
        norms[1],
        up_weight_gradient,
        up_bias_grad.reshape(-1),
        down_weight_gradient,
        norms[5],
        norms[3],
        norms[4],
    )


def solution(mesh):
    placed = (
        P(("dp", "tensor"), None, None),
        P(("dp", "tensor"), None, None),
        P("dp", None),
        P("dp", None),
        P("dp", None),
        P(None, "tensor"),
        P("tensor"),
        P(None, "tensor"),
        P(None, "tensor"),
        P("tensor"),
        P("tensor", None),
        P(),
        P("tensor", None),
        P(),
        P(),
        P(None, "tensor"),
        P("tensor"),
        P("tensor", None),
        P(),
        P(),
        P(),
    )
    return jax.shard_map(
        partial(per_device, mesh.shape["dp"], mesh.shape["tensor"]),
        mesh=mesh,
        in_specs=placed,
        out_specs=(
            P(("dp", "tensor"), None, None),
            P(("dp", "tensor"), None, None),
            P(None, "tensor"),
            P("tensor"),
            P(None, "tensor"),
            P(None, "tensor"),
            P("tensor"),
            P("tensor", None),
            P(),
            P("tensor", None),
            P(),
            P(),
            P(None, "tensor"),
            P("tensor"),
            P("tensor", None),
            P(),
            P(),
            P(),
        ),
        check_vma=False,
    )
```
